32 devices in a mesh: dp: 4 (over y, x), seq: 4 (over z), mp: 2 (over core).
Axes of the slice: x: 2, y: 2, z: 4, core: 2. Of those that a mesh axis runs over, the one named last changes fastest.
Arguments:
- byte_ids: int32 [4608, 16], P('seq', 'dp'), may hold values from 0 to 258
- true_lengths: int32 [16], P('dp'), may hold values from 1152 to 4608, as said below
- byte_table: bfloat16 [259, 768], replicated, may hold values from -6 to 6
- conv_taps: bfloat16 [5, 768], replicated, may hold values from -2.5 to 2.5
- block_scorer: bfloat16 [768], replicated, may hold values from -0.4375 to 0.4375
- attn_gain: bfloat16 [768], replicated, may hold values from 0.5 to 1.5
- w_query: bfloat16 [768, 768], P(None, 'mp'), may hold values from -0.0546875 to 0.0546875
- w_key: bfloat16 [768, 768], P(None, 'mp'), may hold values from -0.21875 to 0.21875
- w_value: bfloat16 [768, 768], P(None, 'mp'), may hold values from -0.21875 to 0.21875
- w_output: bfloat16 [768, 768], P('mp'), may hold values from -0.4375 to 0.4375
- rel_table: bfloat16 [32, 12], P(None, 'mp'), may hold values from -4 to 4
- ffn_gain: bfloat16 [768], replicated, may hold values from 0.5 to 1.5
- w_gate: bfloat16 [768, 2048], P(None, 'mp'), may hold values from -0.21875 to 0.21875
- w_up: bfloat16 [768, 2048], P(None, 'mp'), may hold values from -0.21875 to 0.21875
- w_down: bfloat16 [2048, 768], P('mp'), may hold values from -0.125 to 0.125
- out_grad: bfloat16 [2304, 16, 768], P('seq', 'dp'), may hold values from -6 to 6
Outputs:
- layer_out: float32 [2304, 16, 768], P(('seq', 'mp'), 'dp')
- grad_table: float32 [259, 768], replicated
- grad_taps: float32 [5, 768], replicated
- grad_scorer: float32 [768], replicated
- grad_attn_gain: float32 [768], replicated
- grad_query: float32 [768, 768], P(None, 'mp')
- grad_key: float32 [768, 768], P(None, 'mp')
- grad_value: float32 [768, 768], P(None, 'mp')
- grad_output: float32 [768, 768], P('mp')
- grad_rel: float32 [32, 12], P(None, 'mp')
- grad_ffn_gain: float32 [768], replicated
- grad_gate: float32 [768, 2048], P(None, 'mp')
- grad_up: float32 [768, 2048], P(None, 'mp')
- grad_down: float32 [2048, 768], P('mp')
The draws below stay inside these ranges and needn't reach their ends.
Inputs may be any that keep to these rules, and one draw needn't show every extreme that they name: `true_lengths`: some item has exactly 4608 true bytes.
All inputs are finite; a program needn't handle non-finite values.
Results may differ from the reference program's by a relative error of at most 0.018.
Values may be sent and summed in bfloat16 or wider, within the bound.
No kernel may reach another device: no remote copies, remote signals or barrier semaphores. Data moves between devices by JAX's collectives and lax.ppermute only.
A program may use at most 768 MiB of HBM per device.

```python
import jax
import jax.numpy as jnp
from jax import lax

D = 768
HEADS = 12
DH = 64
FF = 2048
VOCAB = 259
BUCKETS = 32
L = 4608
ITEMS = 16
S = 2304
HD = 768


def draw_true_lengths(key, part):
    lengths = jax.random.randint(jax.random.fold_in(key, 3), (ITEMS,), L // 4, L + 1)
    chosen = jax.random.randint(jax.random.fold_in(key, 7), (), 0, ITEMS)
    return jnp.where(jnp.arange(ITEMS) == chosen, L, lengths).astype(jnp.int32)


def with_ends(entries, stream_key, low, largest):
    index_at = [jax.random.randint(jax.random.fold_in(stream_key, axis), (), 0, length) for axis, length in enumerate(entries.shape)]
    longest = entries.shape.index(max(entries.shape))
    neighbour = index_at[:longest] + [(index_at[longest] + 1) % entries.shape[longest]] + index_at[longest + 1:]
    return entries.at[tuple(index_at)].set(low).at[tuple(neighbour)].set(largest)


def level_of(own_key, shape, pieces, low, high):
    level, own = 1.0, jax.random.fold_in(own_key, 6)
    for position, blocks in pieces:
        heights = jnp.exp(jax.random.uniform(jax.random.fold_in(own, position), (blocks,), jnp.float32, low / len(pieces), high / len(pieces)))
        level = level * jnp.repeat(heights, shape[position] // blocks).reshape([-1 if axis == position else 1 for axis in range(len(shape))])
    return level


def noise(own_key, shape, scale, most, split=(), held_as=jnp.bfloat16):
    entries = scale * jax.random.normal(own_key, shape, jnp.float32)
    if split:
        entries = entries * level_of(own_key, shape, split, -0.22, 0.18)
    return jnp.clip(entries, -most, most).astype(held_as)


def setup_inputs(seed: int = 0) -> dict:
    streams_of = jax.random.split(jax.random.key(seed), 17)
    byte_ids = with_ends(jax.random.randint(streams_of[0], (L, ITEMS), 0, VOCAB), jax.random.fold_in(streams_of[0], 1), 0, VOCAB - 1).astype(jnp.int32)
    true_lengths = draw_true_lengths(jax.random.fold_in(streams_of[16], 71), 0)
    byte_table = noise(streams_of[2], (VOCAB, D), 1.0, 6.0)
    conv_taps = noise(streams_of[3], (5, D), 0.45, 2.5)
    block_scorer = noise(streams_of[4], (D,), (D // 4) ** -0.5, 0.4375)
    attn_gain = jnp.clip(1.0 + 0.1 * jax.random.normal(streams_of[5], (D,), jnp.float32), 0.5, 1.5).astype(jnp.bfloat16)
    w_query = noise(streams_of[6], (D, HD), (D * 16) ** -0.5, 0.0546875, ((1, 2),))
    w_key = noise(streams_of[7], (D, HD), D ** -0.5, 0.21875, ((1, 2),))
    w_value = noise(streams_of[8], (D, HD), D ** -0.5, 0.21875, ((1, 2),))
    w_output = noise(streams_of[9], (HD, D), (D // 4) ** -0.5, 0.4375, ((0, 2),))
    rel_table = noise(streams_of[10], (BUCKETS, HEADS), 1.0, 4.0, ((1, 2),))
    ffn_gain = jnp.clip(1.0 + 0.1 * jax.random.normal(streams_of[11], (D,), jnp.float32), 0.5, 1.5).astype(jnp.bfloat16)
    w_gate = noise(streams_of[12], (D, FF), D ** -0.5, 0.21875, ((1, 2),))
    w_up = noise(streams_of[13], (D, FF), D ** -0.5, 0.21875, ((1, 2),))
    w_down = noise(streams_of[14], (FF, D), FF ** -0.5, 0.125, ((0, 2),))
    out_grad = noise(streams_of[15], (S, ITEMS, D), 1.0, 6.0, ((0, 4), (1, 4)))
    return {"byte_ids": byte_ids, "true_lengths": true_lengths, "byte_table": byte_table, "conv_taps": conv_taps, "block_scorer": block_scorer, "attn_gain": attn_gain, "w_query": w_query, "w_key": w_key, "w_value": w_value, "w_output": w_output, "rel_table": rel_table, "ffn_gain": ffn_gain, "w_gate": w_gate, "w_up": w_up, "w_down": w_down, "out_grad": out_grad}


@jax.custom_vjp
def low(v):
    return lax.optimization_barrier(v.astype(jnp.bfloat16)).astype(jnp.float32)

@jax.custom_vjp
def low_back(v):
    return v

def low_keep(v):
    return (low(v), None)

def low_pass(kept, grad):
    return (grad,)

def back_keep(v):
    return (v, None)

def back_low(kept, grad):
    return (low(grad),)
low.defvjp(low_keep, low_pass)
low_back.defvjp(back_keep, back_low)
EPS = 1e-06
NEG = -1000000000.0
EDGES = (12, 16, 23, 32, 46, 64, 91)
HIGH = lax.Precision.HIGHEST

def bucket_of(offset):
    distance = jnp.abs(offset)
    far = jnp.full(offset.shape, 8, jnp.int32)
    for edge in EDGES:
        far = far + (distance >= edge).astype(jnp.int32)
    near = jnp.where(distance < 8, distance, far)
    return (near + 16 * (offset > 0).astype(jnp.int32)).astype(jnp.int32)

def rms_norm(hidden, gain):
    return hidden * lax.rsqrt(lax.optimization_barrier(jnp.mean(hidden * hidden, axis=-1, keepdims=True)) + EPS) * gain

def gbst_tail(conv_out, scorer):
    byte_count, item_count, model_width = conv_out.shape
    weighted = jnp.einsum('pid,d->pi', conv_out, scorer, precision=HIGH)
    pooled_all = []
    scores_all = []
    for block_size in (1, 2, 3, 4):
        block_means = conv_out.reshape(byte_count // block_size, block_size, item_count, model_width).mean(axis=1)
        pooled_all.append(jnp.repeat(block_means, block_size, axis=0))
        score_means = weighted.reshape(byte_count // block_size, block_size, item_count).mean(axis=1)
        scores_all.append(jnp.repeat(score_means, block_size, axis=0))
    mixing = jax.nn.softmax(jnp.stack(scores_all), axis=0)
    mixture = mixing[0][:, :, None] * pooled_all[0]
    for block_index in range(1, 4):
        mixture = mixture + mixing[block_index][:, :, None] * pooled_all[block_index]
    return mixture.reshape(byte_count // 2, 2, item_count, model_width).mean(axis=1)

def both(value):
    return low_back(low(value))

def item_forward(params, byte_row, length):
    byte_table, conv_taps, block_scorer, attn_gain, w_query, w_key, w_value, w_output, rel_table, ffn_gain, w_gate, w_up, w_down = params
    places = jnp.arange(L, dtype=jnp.int32)
    keep = (places < length).astype(jnp.float32)
    embedded = jnp.take(byte_table, byte_row, axis=0) * keep[:, None]
    padded = jnp.pad(embedded, ((2, 2), (0, 0)))
    conv_out = conv_taps[0] * padded[0:L]
    for tap_index in range(1, 5):
        conv_out = conv_out + conv_taps[tap_index] * padded[tap_index:tap_index + L]
    tokens = gbst_tail(conv_out[:, None, :], block_scorer)[:, 0, :]
    normed = low(rms_norm(tokens, attn_gain))
    query = both(jnp.dot(normed, w_query, precision=HIGH)).reshape(S, HEADS, DH)
    keys = both(jnp.dot(normed, w_key, precision=HIGH)).reshape(S, HEADS, DH)
    values = both(jnp.dot(normed, w_value, precision=HIGH)).reshape(S, HEADS, DH)
    token_places = jnp.arange(S, dtype=jnp.int32)
    key_ok = 2 * token_places < length
    rows = S // 4

    def attend(start):
        query_rows = lax.dynamic_slice_in_dim(query, start, rows, 0)
        raw = low_back(jnp.einsum('qhe,khe->hqk', query_rows, keys, precision=HIGH))
        offset = token_places[None, :] - (start + jnp.arange(rows, dtype=jnp.int32))[:, None]
        bias = jnp.transpose(jnp.take(rel_table, bucket_of(offset), axis=0), (2, 0, 1))
        scores = jnp.where(key_ok[None, None, :], raw + bias, NEG)
        probs = low(jax.nn.softmax(scores, axis=-1))
        return jnp.einsum('hqk,khe->qhe', probs, values, precision=HIGH).reshape(rows, HD)
    starts = jnp.arange(4, dtype=jnp.int32) * rows
    attended = both(lax.map(jax.checkpoint(attend), starts).reshape(S, HD))
    hidden_one = tokens + low_back(jnp.dot(attended, w_output, precision=HIGH))
    normed_two = low(rms_norm(hidden_one, ffn_gain))
    gate = low_back(jnp.dot(normed_two, w_gate, precision=HIGH))
    up = low_back(jnp.dot(normed_two, w_up, precision=HIGH))
    inner = low(jax.nn.gelu(gate, approximate=True) * up)
    return hidden_one + low_back(jnp.dot(inner, w_down, precision=HIGH))

def reference(byte_ids, true_lengths, byte_table, conv_taps, block_scorer, attn_gain, w_query, w_key, w_value, w_output, rel_table, ffn_gain, w_gate, w_up, w_down, out_grad):
    params = tuple((weight.astype(jnp.float32) for weight in (byte_table, conv_taps, block_scorer, attn_gain, w_query, w_key, w_value, w_output, rel_table, ffn_gain, w_gate, w_up, w_down)))
    zeros = jax.tree.map(jnp.zeros_like, params)

    def one_item(totals, inputs):
        byte_row, length, cotangent = inputs
        output, pullback = jax.vjp(lambda weights: item_forward(weights, byte_row, length), params)
        grads = pullback(cotangent)[0]
        return (jax.tree.map(jnp.add, totals, grads), output)
    cotangents = jnp.transpose(out_grad, (1, 0, 2)).astype(jnp.float32)
    totals, outputs = lax.scan(one_item, zeros, (jnp.transpose(byte_ids), true_lengths, cotangents))
    layer_out = jnp.transpose(outputs, (1, 0, 2))
    return (layer_out, totals[0], totals[1], totals[2], totals[3], totals[4], totals[5], totals[6], totals[7], totals[8], totals[9], totals[10], totals[11], totals[12])
```

```python
import functools

import jax
import jax.numpy as jnp
from jax import lax
from jax.experimental import pallas as pl
from jax.experimental.pallas import tpu as pltpu
from jax.sharding import PartitionSpec as P

DH = 64
BUCKETS = 32
MICRO = 4


EPS = 1e-06
NEG = -1000000000.0
EDGES = (12, 16, 23, 32, 46, 64, 91)
HIGH = lax.Precision.HIGHEST
F32 = jnp.float32
B16 = jnp.bfloat16


def extended(cells, sides, width):
    for axis, dim in sides:
        count = lax.axis_size(axis)
        ends = count - 1
        head = lax.slice_in_dim(cells, 0, width, axis=dim)
        tail = lax.slice_in_dim(cells, cells.shape[dim] - width, cells.shape[dim], axis=dim)
        cells = jnp.concatenate(
            [
                lax.ppermute(tail, axis, [(i, (i + 1) % count) for i in range(ends)]),
                cells,
                lax.ppermute(head, axis, [((i + 1) % count, i) for i in range(ends)]),
            ],
            axis=dim,
        )
    return cells


def for_sending(array):
    return jax.tree.map(lambda a: a.astype(jnp.bfloat16) if a.dtype == jnp.float32 else a, array)


def bucket_of(offset):
    distance = jnp.abs(offset)
    far = jnp.full(offset.shape, 8, jnp.int32)
    for edge in EDGES:
        far = far + (distance >= edge).astype(jnp.int32)
    near = jnp.where(distance < 8, distance, far)
    return near + 16 * (offset > 0).astype(jnp.int32)


def bias_onehot(query_places, key_places):
    offset = key_places[None, :] - query_places[:, None]
    return (bucket_of(offset)[:, :, None] == jnp.arange(BUCKETS, dtype=jnp.int32)).astype(F32)


def rms_norm(hidden, gain):
    return hidden * lax.rsqrt(jnp.mean(hidden * hidden, axis=-1, keepdims=True) + EPS) * gain


def activation(gate, up):
    return jax.nn.gelu(gate, approximate=True) * up


def gbst_tail(conv_out, scorer):
    byte_count, item_count, model_width = conv_out.shape
    weighted = jnp.einsum("pid,d->pi", conv_out, scorer, precision=HIGH)
    pooled_all = []
    scores_all = []
    for block_size in (1, 2, 3, 4):
        block_means = conv_out.reshape(
            byte_count // block_size, block_size, item_count, model_width
        ).mean(axis=1)
        pooled_all.append(jnp.repeat(block_means, block_size, axis=0))
        score_means = weighted.reshape(byte_count // block_size, block_size, item_count).mean(
            axis=1
        )
        scores_all.append(jnp.repeat(score_means, block_size, axis=0))
    mixing = jax.nn.softmax(jnp.stack(scores_all), axis=0)
    mixture = mixing[0][:, :, None] * pooled_all[0]
    for block_index in range(1, 4):
        mixture = mixture + mixing[block_index][:, :, None] * pooled_all[block_index]
    return mixture.reshape(byte_count // 2, 2, item_count, model_width).mean(axis=1)


def local_general(
    byte_ids,
    true_lengths,
    byte_table,
    conv_taps,
    block_scorer,
    attn_gain,
    w_query,
    w_key,
    w_value,
    w_output,
    rel_table,
    ffn_gain,
    w_gate,
    w_up,
    w_down,
    out_grad,
):
    seq_count = lax.axis_size("seq")
    seq_place = lax.axis_index("seq")
    core_place = lax.axis_index("mp")
    byte_rows = byte_ids.shape[0]
    tok_rows = byte_rows // 2
    half_rows = tok_rows // lax.axis_size("mp")
    total_tokens = tok_rows * seq_count
    item_count = byte_ids.shape[1] // MICRO
    proj_width = w_query.shape[1]
    head_count = proj_width // DH
    ffn_width = w_gate.shape[1]
    taps = conv_taps.astype(F32)
    scorer = block_scorer.astype(F32)
    gain_one = attn_gain.astype(F32)
    gain_two = ffn_gain.astype(F32)
    rel_local = rel_table.astype(F32)
    gate_up = jnp.concatenate([w_gate, w_up], axis=1)
    query_places = seq_place * tok_rows + jnp.arange(tok_rows, dtype=jnp.int32)
    key_places = jnp.arange(total_tokens, dtype=jnp.int32)
    onehot_bias = bias_onehot(query_places, key_places)
    bias = jnp.einsum("qkb,bh->hqk", onehot_bias, rel_local, precision=HIGH)
    byte_places = seq_place * byte_rows + jnp.arange(byte_rows, dtype=jnp.int32)
    vocab_range = jnp.arange(byte_table.shape[0], dtype=jnp.int32)
    sum_table = jnp.zeros(byte_table.shape, F32)
    sum_taps = jnp.zeros(conv_taps.shape, F32)
    sum_scorer = jnp.zeros(block_scorer.shape, F32)
    sum_gain_one = jnp.zeros(attn_gain.shape, F32)
    sum_query = jnp.zeros(w_query.shape, F32)
    sum_key = jnp.zeros(w_key.shape, F32)
    sum_value = jnp.zeros(w_value.shape, F32)
    sum_output = jnp.zeros(w_output.shape, F32)
    sum_rel = jnp.zeros(rel_table.shape, F32)
    sum_gain_two = jnp.zeros(ffn_gain.shape, F32)
    sum_gate = jnp.zeros(w_gate.shape, F32)
    sum_up = jnp.zeros(w_up.shape, F32)
    sum_down = jnp.zeros(w_down.shape, F32)
    outputs = []
    for micro in range(MICRO):
        first = micro * item_count
        ids_now = byte_ids[:, first : first + item_count]
        lengths = true_lengths[first : first + item_count]
        keep = (byte_places[:, None] < lengths[None, :]).astype(F32)
        onehot = (ids_now[:, :, None] == vocab_range).astype(F32) * keep[:, :, None]
        embedded = jnp.einsum(
            "piv,vd->pid", onehot.astype(B16), byte_table, preferred_element_type=F32
        ).astype(B16)
        framed = extended(embedded, (("seq", 0),), 2)
        conv_out = taps[0] * framed[0:byte_rows]
        for tap_index in range(1, 5):
            conv_out = conv_out + taps[tap_index] * framed[tap_index : tap_index + byte_rows]
        tokens, gbst_pull = jax.vjp(gbst_tail, conv_out, scorer)
        normed, norm_pull = jax.vjp(rms_norm, tokens, gain_one)
        normed_low = normed.astype(B16)
        query = jnp.einsum("qid,dh->qih", normed_low, w_query, preferred_element_type=F32).astype(
            B16
        )
        keys_here = jnp.einsum("qid,dh->qih", normed_low, w_key, preferred_element_type=F32).astype(
            B16
        )
        values_here = jnp.einsum(
            "qid,dh->qih", normed_low, w_value, preferred_element_type=F32
        ).astype(B16)
        keys_all, values_all = (
            lax.all_gather(keys_here, "seq", axis=0, tiled=True),
            lax.all_gather(values_here, "seq", axis=0, tiled=True),
        )
        query4 = query.reshape(tok_rows, item_count, head_count, DH)
        keys4 = keys_all.reshape(total_tokens, item_count, head_count, DH)
        values4 = values_all.reshape(total_tokens, item_count, head_count, DH)
        key_ok = 2 * key_places[None, :] < lengths[:, None]

        def scores_of():
            raw = jnp.einsum("qihe,kihe->ihqk", query4, keys4, preferred_element_type=F32)
            return jnp.where(key_ok[:, None, None, :], raw + bias[None], NEG)

        scores = scores_of()
        top = jnp.max(scores, axis=-1, keepdims=True)
        log_total = top + jnp.log(jnp.sum(jnp.exp(scores - top), axis=-1, keepdims=True))
        probs_low = jnp.exp(scores - log_total).astype(B16)
        attended = (
            jnp.einsum("ihqk,kihe->qihe", probs_low, values4, preferred_element_type=F32)
            .reshape(tok_rows, item_count, proj_width)
            .astype(B16)
        )
        attn_half = lax.psum_scatter(
            jnp.einsum("qih,hd->qid", attended, w_output, preferred_element_type=F32),
            "mp",
            scatter_dimension=0,
            tiled=True,
        )
        tokens_half = lax.dynamic_slice_in_dim(tokens, core_place * half_rows, half_rows, 0)
        hidden_half = tokens_half + attn_half
        normed_two, norm_two_pull = jax.vjp(rms_norm, hidden_half, gain_two)
        normed_full = lax.all_gather(normed_two.astype(B16), "mp", axis=0, tiled=True)
        projected = jnp.einsum("qid,df->qif", normed_full, gate_up, preferred_element_type=F32)
        inner, inner_pull = jax.vjp(
            activation, projected[..., :ffn_width], projected[..., ffn_width:]
        )
        inner_low = inner.astype(B16)
        ffn_half = lax.psum_scatter(
            jnp.einsum("qif,fd->qid", inner_low, w_down, preferred_element_type=F32).astype(
                jnp.bfloat16
            ),
            "mp",
            scatter_dimension=0,
            tiled=True,
        ).astype(jnp.float32)
        outputs.append(hidden_half + ffn_half)
        grad_low = out_grad[:, first : first + item_count]
        grad_half = lax.dynamic_slice_in_dim(grad_low, core_place * half_rows, half_rows, 0).astype(
            F32
        )
        sum_down = sum_down + jnp.einsum(
            "qif,qid->fd", inner_low, grad_low, preferred_element_type=F32
        )
        grad_inner = jnp.einsum("qid,fd->qif", grad_low, w_down, preferred_element_type=F32)
        gate_grad, up_grad = inner_pull(grad_inner)
        gate_low = gate_grad.astype(B16)
        up_low = up_grad.astype(B16)
        sum_gate = sum_gate + jnp.einsum(
            "qid,qif->df", normed_full, gate_low, preferred_element_type=F32
        )
        sum_up = sum_up + jnp.einsum("qid,qif->df", normed_full, up_low, preferred_element_type=F32)
        normed_two_grad = lax.psum_scatter(
            jnp.einsum("qif,df->qid", gate_low, w_gate, preferred_element_type=F32)
            + jnp.einsum("qif,df->qid", up_low, w_up, preferred_element_type=F32),
            "mp",
            scatter_dimension=0,
            tiled=True,
        )
        hidden_norm_grad, gain_two_grad = norm_two_pull(normed_two_grad)
        hidden_grad = grad_half + hidden_norm_grad
        hidden_full = lax.all_gather(for_sending(hidden_grad), "mp", axis=0, tiled=True).astype(
            hidden_grad.dtype
        )
        hidden_low = hidden_full.astype(B16)
        sum_output = sum_output + jnp.einsum(
            "qih,qid->hd", attended, hidden_low, preferred_element_type=F32
        )
        attended_grad = jnp.einsum(
            "qid,hd->qih", hidden_low, w_output, preferred_element_type=F32
        ).astype(B16)
        attended_grad4 = attended_grad.reshape(tok_rows, item_count, head_count, DH)
        scores = scores_of()
        probs = jnp.exp(scores - log_total)
        probs_low = probs.astype(B16)
        probs_grad = jnp.einsum(
            "qihe,kihe->ihqk", attended_grad4, values4, preferred_element_type=F32
        )
        inner_sum = jnp.sum(probs * probs_grad, axis=-1, keepdims=True)
        scores_grad = probs * (probs_grad - inner_sum)
        sum_rel = sum_rel + jnp.einsum(
            "qkb,hqk->bh", onehot_bias, jnp.sum(scores_grad, axis=0), precision=HIGH
        )
        scores_low = scores_grad.astype(B16)
        query_grad = (
            jnp.einsum("ihqk,kihe->qihe", scores_low, keys4, preferred_element_type=F32)
            .reshape(tok_rows, item_count, proj_width)
            .astype(B16)
        )
        key_part = jnp.einsum("ihqk,qihe->kihe", scores_low, query4, preferred_element_type=F32)
        value_part = jnp.einsum(
            "ihqk,qihe->kihe", probs_low, attended_grad4, preferred_element_type=F32
        )
        key_sums = lax.psum_scatter(
            jnp.concatenate(
                [
                    key_part.reshape(tok_rows * lax.axis_size("seq"), item_count, proj_width),
                    value_part.reshape(tok_rows * lax.axis_size("seq"), item_count, proj_width),
                ],
                axis=2,
            ).astype(jnp.bfloat16),
            "seq",
            scatter_dimension=0,
            tiled=True,
        ).astype(jnp.float32)
        keys_grad = key_sums[..., :proj_width].astype(B16)
        values_grad = key_sums[..., proj_width:].astype(B16)
        sum_query = sum_query + jnp.einsum(
            "qid,qih->dh", normed_low, query_grad, preferred_element_type=F32
        )
        sum_key = sum_key + jnp.einsum(
            "qid,qih->dh", normed_low, keys_grad, preferred_element_type=F32
        )
        sum_value = sum_value + jnp.einsum(
            "qid,qih->dh", normed_low, values_grad, preferred_element_type=F32
        )
        partial_grad = (
            jnp.einsum("qih,dh->qid", query_grad, w_query, preferred_element_type=F32)
            + jnp.einsum("qih,dh->qid", keys_grad, w_key, preferred_element_type=F32)
            + jnp.einsum("qih,dh->qid", values_grad, w_value, preferred_element_type=F32)
        )
        normed_grad, gain_two_total = (
            lax.psum(partial_grad.astype(jnp.bfloat16), "mp").astype(jnp.float32),
            lax.psum(gain_two_grad.astype(jnp.bfloat16), "mp").astype(jnp.float32),
        )
        sum_gain_two = sum_gain_two + gain_two_total
        tokens_norm_grad, gain_one_grad = norm_pull(normed_grad)
        sum_gain_one = sum_gain_one + gain_one_grad
        tokens_grad = hidden_full + tokens_norm_grad
        conv_grad, scorer_grad = gbst_pull(tokens_grad)
        sum_scorer = sum_scorer + scorer_grad
        framed_grad = extended(conv_grad.astype(jnp.bfloat16), (("seq", 0),), 2).astype(
            conv_grad.dtype
        )
        embedded_grad = taps[0] * framed_grad[4 : 4 + byte_rows]
        for tap_index in range(1, 5):
            embedded_grad = (
                embedded_grad
                + taps[tap_index] * framed_grad[4 - tap_index : 4 - tap_index + byte_rows]
            )
        tap_sums = [
            jnp.sum(conv_grad * framed[tap_index : tap_index + byte_rows], axis=(0, 1))
            for tap_index in range(5)
        ]
        sum_taps = sum_taps + jnp.stack(tap_sums)
        sum_table = sum_table + jnp.einsum("piv,pid->vd", onehot, embedded_grad, precision=HIGH)
    totals = lax.psum(
        (
            sum_table,
            sum_taps,
            sum_scorer,
            sum_gain_one,
            sum_query,
            sum_key,
            sum_value,
            sum_output,
            sum_rel,
            sum_gain_two,
            sum_gate,
            sum_up,
            sum_down,
        ),
        ("dp", "seq"),
    )
    layer_out = jnp.concatenate(outputs, axis=1)
    return (
        layer_out,
        totals[0],
        totals[1],
        totals[2],
        totals[3],
        totals[4],
        totals[5],
        totals[6],
        totals[7],
        totals[8],
        totals[9],
        totals[10],
        totals[11],
        totals[12],
    )


LOG2E = 1.4426950408889634
LN2 = 0.6931471805599453
NT = (((1,), (1,)), ((), ()))
NN = (((1,), (0,)), ((), ()))
CK = 256

def dot(a, b, dims):
    return lax.dot_general(a, b, dims, preferred_element_type=F32)

def split3(x):
    hi = x.astype(B16)
    rest = x - hi.astype(F32)
    mid = rest.astype(B16)
    lo = (rest - mid.astype(F32)).astype(B16)
    return hi, mid, lo

def split3_xla(x):
    cut = lambda a: lax.reduce_precision(a, exponent_bits=8, mantissa_bits=7)
    hi = cut(x)
    mid = cut(x - hi)
    return hi.astype(B16), mid.astype(B16), (x - hi - mid).astype(B16)


def attn_fwd_body(limit_ref, q_ref, k_ref, v_ref, curve_ref, e_ref, o_ref, linv_ref,
                  kext, vext, table, qext, acc, knorm):
    total = k_ref.shape[0]
    tq = q_ref.shape[0]
    chunks = total // CK
    step = pl.program_id(1)

    @pl.when(step == 0)
    def _():
        lane = lax.broadcasted_iota(jnp.int32, (total, 128), 1)
        place = lax.broadcasted_iota(jnp.int32, (total, 128), 0)
        masked = jnp.where(place < limit_ref[0], 0.0, -1e9).astype(F32)
        k = k_ref[...].astype(F32)
        vt = v_ref[...].T
        for h in range(2):
            own = (lane < 64) if h == 0 else (lane >= 64)
            base = 64 if h == 0 else 0
            extra = jnp.where(lane == base, masked, jnp.where((lane > base) & (lane < base + 4), 1.0, 0.0))
            kext[h] = jnp.where(own, k, extra).astype(B16)
            sq = jnp.where(own, k * k, 0.0)
            knorm[h] = jnp.max(jnp.sum(sq, axis=1, keepdims=True))
            vext[h, 0:64, :] = vt[64 * h : 64 * h + 64, :]
            vext[h, 64:80, :] = jnp.ones((16, total), B16)
            curve = curve_ref[h : h + 1, :]
            for g in range(5):
                lo = 1024 + 2 * CK - g * CK - 256
                window = jnp.broadcast_to(curve[:, lo : lo + 512], (CK, 512))
                rolled = pltpu.roll(window, 0, 1, stride=1, stride_axis=0)
                table[h, g * CK : (g + 1) * CK, :] = rolled[:, 256:512]

    lane_q = lax.broadcasted_iota(jnp.int32, (tq, 128), 1)
    q = q_ref[...].astype(F32)

    def scores(h, c):
        d = jnp.clip(c - step, -2, 2) + 2
        k_now = kext[h, pl.ds(pl.multiple_of(c * CK, CK), CK), :]
        return dot(k_now, qext[h], NT) * LOG2E + table[h, pl.ds(pl.multiple_of(d * CK, CK), CK), :]

    for h in range(2):
        own = (lane_q < 64) if h == 0 else (lane_q >= 64)
        base = 64 if h == 0 else 0
        qext[h] = jnp.where(own, q, jnp.where(lane_q == base, 1.0, 0.0)).astype(B16)
        sq = jnp.where(own, q * q, 0.0)
        qnorm = jnp.max(jnp.sum(sq, axis=1, keepdims=True))

        @pl.when(qnorm * knorm[h] > 50.0 * 50.0)
        def _(h=h, own=own, base=base):
            def grow(c, top):
                return jnp.maximum(top, jnp.max(scores(h, c), axis=0, keepdims=True))
            top = lax.fori_loop(0, chunks, grow, jnp.full((1, tq), -3e38, F32))
            hi, mid, lo = split3(-jnp.broadcast_to(top * LN2, (128, tq)).T)
            extra = jnp.where(lane_q == base, jnp.ones_like(hi), jnp.zeros_like(hi))
            for at, part in ((1, hi), (2, mid), (3, lo)):
                extra = jnp.where(lane_q == base + at, part, extra)
            qext[h] = jnp.where(own, q.astype(B16), extra)

    acc[...] = jnp.zeros_like(acc)

    def emit(c):
        for h in range(2):
            e_ref[h, pl.ds(pl.multiple_of(c * CK, CK), CK), :] = jnp.exp2(scores(h, c)).astype(B16)

    def gather(c):
        for h in range(2):
            at = pl.ds(pl.multiple_of(c * CK, CK), CK)
            acc[h] += dot(vext[h, :, at], e_ref[h, at, :], NN)

    emit(0)

    def body(c, carry):
        gather(c - 1)
        emit(c)
        return carry
    lax.fori_loop(1, chunks, body, 0)
    gather(chunks - 1)
    inv = [1.0 / acc[h, 64:65, :] for h in range(2)]
    o_ref[...] = jnp.concatenate([acc[h, 0:64, :] * inv[h] for h in range(2)], axis=0).T
    linv_ref[...] = jnp.concatenate([jnp.broadcast_to(inv[h], (64, tq)) for h in range(2)], axis=0).T

def attn_fwd(limit, qkv, curve):
    total = qkv.shape[0]
    pairs = qkv.shape[1] // 3 // 128
    tq = CK
    spec = pltpu.PrefetchScalarGridSpec(
        num_scalar_prefetch=1, grid=(pairs, total // tq),
        in_specs=[
            pl.BlockSpec((tq, 128), lambda p, i, s: (i, p)),
            pl.BlockSpec((total, 128), lambda p, i, s: (0, pairs + p)),
            pl.BlockSpec((total, 128), lambda p, i, s: (0, 2 * pairs + p)),
            pl.BlockSpec((None, 2, 2048), lambda p, i, s: (p, 0, 0)),
        ],
        out_specs=[
            pl.BlockSpec((2, total, tq), lambda p, i, s: (p, 0, i)),
            pl.BlockSpec((tq, 128), lambda p, i, s: (i, p)),
            pl.BlockSpec((tq, 128), lambda p, i, s: (i, p)),
        ],
        scratch_shapes=[
            pltpu.VMEM((2, total, 128), B16), pltpu.VMEM((2, 80, total), B16),
            pltpu.VMEM((2, 5 * CK, tq), F32), pltpu.VMEM((2, tq, 128), B16),
            pltpu.VMEM((2, 80, tq), F32), pltpu.SMEM((2,), F32),
        ])
    n = 2 * pairs * total * total
    return pl.pallas_call(
        attn_fwd_body, grid_spec=spec, name="attn_fwd",
        out_shape=[jax.ShapeDtypeStruct((2 * pairs, total, total), B16),
                   jax.ShapeDtypeStruct((total, 128 * pairs), F32),
                   jax.ShapeDtypeStruct((total, 128 * pairs), F32)],
        compiler_params=pltpu.CompilerParams(vmem_limit_bytes=56 << 20, dimension_semantics=("arbitrary", "arbitrary")),
        cost_estimate=pl.CostEstimate(flops=4 * 64 * n, transcendentals=n, bytes_accessed=2 * n),
    )(limit, qkv, qkv, qkv, curve)

def attn_bwd_body(e_ref, k_ref, v_ref, q_ref, do_ref, o_ref, linv_ref,
                  dk_ref, dv_ref, dq_ref, near_ref, far_ref,
                  dop, doe, qind, ds, dqt, band):
    total = q_ref.shape[0]
    ck = k_ref.shape[0]
    chunks = pl.num_programs(1)
    step = pl.program_id(1)

    @pl.when(step == 0)
    def _():
        lane = lax.broadcasted_iota(jnp.int32, (CK, 128), 1)
        def prep(i, carry):
            at = pl.ds(pl.multiple_of(i * CK, CK), CK)
            part = (do_ref[at, :].astype(F32) * linv_ref[at, :]).astype(B16)
            dop[at, :] = part
            prod = part.astype(F32) * o_ref[at, :]
            place = lax.broadcasted_iota(jnp.int32, (CK, 128), 0) + i * CK
            q = q_ref[at, :]
            for h in range(2):
                own = (lane < 64) if h == 0 else (lane >= 64)
                base = 64 if h == 0 else 0
                total_d = jnp.sum(jnp.where(own, prod, 0.0), axis=1, keepdims=True)
                hi, mid, lo = split3(-jnp.broadcast_to(total_d, (CK, 128)))
                extra = jnp.where(lane == base, hi, jnp.where(lane == base + 1, mid, jnp.where(lane == base + 2, lo, jnp.zeros_like(hi))))
                doe[h, at, :] = jnp.where(own, part, extra)
                ind = jnp.where(lane - base == place // 128, 1.0, 0.0).astype(B16)
                qind[h, at, :] = jnp.where(own, q, ind)
            return carry
        lax.fori_loop(0, total // CK, prep, 0)
        dqt[...] = jnp.zeros_like(dqt)
        band[...] = jnp.zeros_like(band)
        far_ref[...] = jnp.zeros_like(far_ref)

    lane = lax.broadcasted_iota(jnp.int32, (ck, 128), 1)
    v = v_ref[...]
    kt = k_ref[...].T
    outs_k, outs_v = [], []
    k0 = step * ck
    for h in range(2):
        own = (lane < 64) if h == 0 else (lane >= 64)
        base = 64 if h == 0 else 0
        ones = jnp.where((lane >= base) & (lane < base + 3), 1.0, 0.0).astype(B16)
        vx = jnp.where(own, v, ones)
        for c in range(total // CK):
            at = slice(c * CK, (c + 1) * CK)
            pg = dot(vx, doe[h, at, :], NT)
            ds[h, :, at] = e_ref[h, :, at] * pg.astype(B16)
        outs_v.append(dot(e_ref[h], dop[...], NN))
        dk = dot(ds[h], qind[h], NN)
        outs_k.append(dk)
        for c in range(total // CK):
            at = slice(c * CK, (c + 1) * CK)
            dqt[64 * h : 64 * h + 64, at] += dot(kt[64 * h : 64 * h + 64, :], ds[h, :, at], NN)
        sums = jnp.sum(dk, axis=0, keepdims=True)
        block = lax.broadcasted_iota(jnp.int32, (1, 128), 1) - base
        here = step * (ck // 128)
        inside = (block >= 0) & (block < total // 128)
        far_ref[h, 0:1, :] += jnp.where(inside & (block < here - 1), sums, 0.0)
        far_ref[h, 1:2, :] += jnp.where(inside & (block >= here + ck // 128 + 1), sums, 0.0)
        band[h, :, 128 : 128 + ck] += ds[h, :, pl.ds(pl.multiple_of(k0, 128), ck)].astype(F32)

        @pl.when(step > 0)
        def _(h=h):
            band[h, :, 0:128] += ds[h, :, pl.ds(pl.multiple_of(k0 - 128, 128), 128)].astype(F32)

        @pl.when(step < chunks - 1)
        def _(h=h):
            band[h, :, 128 + ck : 256 + ck] += ds[h, :, pl.ds(pl.multiple_of(k0 + ck, 128), 128)].astype(F32)
    dk_ref[...] = jnp.where(lane < 64, outs_k[0], outs_k[1]).astype(B16)
    dv_ref[...] = jnp.where(lane < 64, outs_v[0], outs_v[1]).astype(B16)

    @pl.when(step == chunks - 1)
    def _():
        for i in range(total // CK):
            at = slice(i * CK, (i + 1) * CK)
            dq_ref[at, :] = dqt[:, at].T.astype(B16)
        width = ck + 256
        row = lax.broadcasted_iota(jnp.int32, (ck, width), 0)
        col = lax.broadcasted_iota(jnp.int32, (ck, width), 1)
        offset = row - col + 128
        for h in range(2):
            all_now = band[h]
            near = jnp.where(jnp.abs(offset) < 128, all_now, 0.0)
            folded = near[0:8, :]
            for g in range(1, ck // 8):
                folded = folded + pltpu.roll(near[8 * g : 8 * g + 8, :], width - 8 * g, 1)
            line = folded[0:1, :]
            for g in range(1, 8):
                line = line + pltpu.roll(folded[g : g + 1, :], width - g, 1)
            near_ref[h, 0:1, :] = line
            near_ref[h, 1:2, :] = jnp.sum(jnp.where(offset >= 128, all_now, 0.0), axis=0, keepdims=True)
            near_ref[h, 2:3, :] = jnp.sum(jnp.where(offset <= -128, all_now, 0.0), axis=0, keepdims=True)
            near_ref[h, 3:8, :] = jnp.zeros((5, width), F32)

def attn_bwd(e, qkv, d_att, att, linv):
    total = qkv.shape[0]
    pairs = qkv.shape[1] // 3 // 128
    ck = CK
    full = lambda off: pl.BlockSpec((total, 128), lambda p, i: (0, off + p))
    part = lambda off: pl.BlockSpec((ck, 128), lambda p, i: (i, off + p))
    n = 2 * pairs * total * total
    return pl.pallas_call(
        attn_bwd_body, grid=(pairs, total // ck), name="attn_bwd",
        in_specs=[pl.BlockSpec((2, ck, total), lambda p, i: (p, i, 0)), part(pairs), part(2 * pairs),
                  full(0), full(0), full(0), full(0)],
        out_specs=[part(0), part(0), full(0),
                   pl.BlockSpec((2, 8, ck + 256), lambda p, i: (p, 0, 0)),
                   pl.BlockSpec((2, 8, 128), lambda p, i: (p, 0, 0))],
        out_shape=[jax.ShapeDtypeStruct((total, 128 * pairs), B16)] * 3
        + [jax.ShapeDtypeStruct((2 * pairs, 8, ck + 256), F32), jax.ShapeDtypeStruct((2 * pairs, 8, 128), F32)],
        scratch_shapes=[
            pltpu.VMEM((total, 128), B16), pltpu.VMEM((2, total, 128), B16), pltpu.VMEM((2, total, 128), B16),
            pltpu.VMEM((2, ck, total), B16), pltpu.VMEM((128, total), F32), pltpu.VMEM((2, ck, ck + 256), F32),
        ],
        compiler_params=pltpu.CompilerParams(vmem_limit_bytes=60 << 20, dimension_semantics=("arbitrary", "arbitrary")),
        cost_estimate=pl.CostEstimate(flops=8 * 64 * n, transcendentals=0, bytes_accessed=2 * n),
    )(e, qkv, qkv, qkv, d_att, att, linv)

def bias_curve(rel, heads):
    offset = 1024 - jnp.arange(2048, dtype=jnp.int32)
    onehot = (bucket_of(offset)[:, None] == jnp.arange(32, dtype=jnp.int32)).astype(F32)
    curve = jnp.einsum("xb,bh->hx", onehot, rel.astype(F32) * LOG2E, precision=lax.Precision.HIGHEST)
    return curve.reshape(heads // 2, 2, 2048)

def rel_grad(near, far, width):
    x = jnp.arange(width, dtype=jnp.int32)
    onehot = (bucket_of(128 - x)[:, None] == jnp.arange(32, dtype=jnp.int32)).astype(F32)
    onehot = onehot * (x[:, None] < 256)
    g = jnp.einsum("hx,xb->bh", near[:, 0, :], onehot, precision=lax.Precision.HIGHEST)
    up = jnp.sum(near[:, 1, :], axis=1) + jnp.sum(far[:, 0, :], axis=1)
    down = jnp.sum(near[:, 2, :], axis=1) + jnp.sum(far[:, 1, :], axis=1)
    slot = jnp.arange(32)[:, None]
    return g + jnp.where(slot == 31, up[None], 0.0) + jnp.where(slot == 15, down[None], 0.0)

CJ = 272
CC = 1408
TT = 384

def means_of(even, odd):
    t = lax.broadcasted_iota(jnp.int32, even.shape, 1)
    width = even.shape[1]
    prev = lambda x: pltpu.roll(x, 1, 1)
    succ = lambda x: pltpu.roll(x, width - 1, 1)
    two = even + odd
    four = two + jnp.where(t % 2 == 0, succ(two), prev(two))
    place = t - 3 * ((t * 21846) >> 16)
    first = two + succ(even)
    middle_e = prev(two) + even
    middle_o = odd + succ(two)
    last = prev(odd) + two
    three_e = jnp.where(place == 0, first, jnp.where(place == 1, middle_e, last))
    three_o = jnp.where(place == 0, first, jnp.where(place == 1, middle_o, last))
    third = 1.0 / 3.0
    return [(even, odd), (two * 0.5, two * 0.5), (three_e * third, three_o * third), (four * 0.25, four * 0.25)]

def masks():
    t = lax.broadcasted_iota(jnp.int32, (TT, 2 * TT), 0)
    p = lax.broadcasted_iota(jnp.int32, (TT, 2 * TT), 1)
    par = p >= TT
    tp = jnp.where(par, p - TT, p)
    byte = 2 * tp + jnp.where(par, 1, 0)
    third = lambda x: (x * 21846) >> 16
    blk = third(byte)
    return t == tp, par, (t >> 1) == (tp >> 1), third(2 * t) == blk, third(2 * t + 1) == blk

def fill_onehot(cid_ref, oht):
    row = lax.broadcasted_iota(jnp.int32, (CJ, 2 * TT), 0)
    for j in range(5):
        hit = row == (cid_ref[j : j + 1, :])
        oht[CJ * j : CJ * (j + 1), :] = jnp.where(hit, 1.0, 0.0).astype(B16)
    oht[5 * CJ :, :] = jnp.zeros((CC - 5 * CJ, 2 * TT), B16)

def gbst_fwd_body(cid_ref, tvec_ref, table_ref, rest_ref, gain_ref, tok_ref, norm_ref, w_ref, mix_ref, oht):
    fill_onehot(cid_ref, oht)
    parts = dot(tvec_ref[...], oht[...], NN)
    weighted = parts[0:1] + parts[1:2] + parts[2:3]
    scores = means_of(weighted[:, :TT], weighted[:, TT:])
    rows = []
    for side in range(2):
        mine = [s[side] for s in scores]
        top = jnp.maximum(jnp.maximum(mine[0], mine[1]), jnp.maximum(mine[2], mine[3]))
        e = [jnp.exp(s - top) for s in mine]
        inv = 1.0 / (e[0] + e[1] + e[2] + e[3])
        rows.append([x * inv for x in e])
    mix = jnp.concatenate([rows[side][b] for b in range(4) for side in range(2)], axis=0)
    mix_ref[...] = mix
    col = mix.T
    c = lambda i: col[:, i : i + 1]
    same, par, pair, tri_e, tri_o = masks()
    w = jnp.where(same, jnp.where(par, 0.5 * c(1), 0.5 * c(0)) + 0.25 * (c(2) + c(3)), 0.0)
    w = w + jnp.where(pair, 0.125 * (c(6) + c(7)), 0.0)
    w = w + jnp.where(tri_e, c(4) * (1.0 / 6.0), 0.0) + jnp.where(tri_o, c(5) * (1.0 / 6.0), 0.0)
    w_hi = w.astype(B16)
    w_lo = (w - w_hi.astype(F32)).astype(B16)
    w_ref[...] = w_hi
    a = dot(w_hi, oht[...], NT) + dot(w_lo, oht[...], NT)
    a_hi = a.astype(B16)
    a_lo = (a - a_hi.astype(F32)).astype(B16)
    tokens = dot(a_hi, table_ref[...], NN) + dot(a_lo, table_ref[...], NN) + dot(a_hi, rest_ref[...], NN)
    tok_ref[...] = tokens
    r = lax.rsqrt(jnp.mean(tokens * tokens, axis=1, keepdims=True) + EPS)
    norm_ref[...] = (tokens * r * gain_ref[...]).astype(B16)

def gbst_fwd(cid, tvec, table, rest, gain):
    tiles = cid.shape[0]
    d = table.shape[1]
    rows = tiles * TT
    const = lambda shape: pl.BlockSpec(shape, lambda i: (0,) * len(shape))
    return pl.pallas_call(
        gbst_fwd_body, grid=(tiles,), name="gbst_fwd",
        in_specs=[pl.BlockSpec((None, 8, 2 * TT), lambda i: (i, 0, 0)), const((8, CC)), const((CC, d)), const((CC, d)), const((1, d))],
        out_specs=[pl.BlockSpec((TT, d), lambda i: (i, 0)), pl.BlockSpec((TT, d), lambda i: (i, 0)),
                   pl.BlockSpec((TT, 2 * TT), lambda i: (i, 0)), pl.BlockSpec((None, 8, TT), lambda i: (i, 0, 0))],
        out_shape=[jax.ShapeDtypeStruct((rows, d), F32), jax.ShapeDtypeStruct((rows, d), B16),
                   jax.ShapeDtypeStruct((rows, 2 * TT), B16), jax.ShapeDtypeStruct((tiles, 8, TT), F32)],
        scratch_shapes=[pltpu.VMEM((CC, 2 * TT), B16)],
        compiler_params=pltpu.CompilerParams(vmem_limit_bytes=48 << 20),
        cost_estimate=pl.CostEstimate(flops=rows * CC * d * 5, transcendentals=0, bytes_accessed=rows * d * 8),
    )(cid, tvec, table, rest, gain)

def gbst_bwd_body(cid_ref, w_ref, mix_ref, tok_ref, hid_ref, nb_ref, gain_ref, table_ref, raw_ref, taps_ref, scorer_ref,
                  gt_ref, small_ref, oht, big, usum):
    i = pl.program_id(0)
    fill_onehot(cid_ref, oht)

    @pl.when(i == 0)
    def _():
        big[...] = jnp.zeros_like(big)
        usum[...] = jnp.zeros_like(usum)
        small_ref[...] = jnp.zeros_like(small_ref)
    x = tok_ref[...]
    n = nb_ref[...].astype(F32)
    r = lax.rsqrt(jnp.mean(x * x, axis=1, keepdims=True) + EPS)
    u = n * gain_ref[...]
    xr = x * r
    g = hid_ref[...].astype(F32) + r * (u - xr * jnp.mean(u * xr, axis=1, keepdims=True))
    small_ref[6:7, :] += jnp.sum(n * xr, axis=0, keepdims=True)
    gb = g.astype(B16)
    hh = dot(gb, table_ref[...], NT).astype(B16)
    gram = dot(hh, oht[...], NN)
    same, par, pair, tri_e, tri_o = masks()
    lanesum = lambda m: jnp.sum(jnp.where(m, gram, 0.0), axis=1, keepdims=True)
    me = 0.5 * lanesum(same & ~par)
    mo = 0.5 * lanesum(same & par)
    m2 = 0.5 * (me + mo)
    m4 = 0.125 * lanesum(pair)
    m3e = lanesum(tri_e) * (1.0 / 6.0)
    m3o = lanesum(tri_o) * (1.0 / 6.0)
    lane8 = lax.broadcasted_iota(jnp.int32, (TT, 128), 1)
    cols = jnp.zeros((TT, 128), F32)
    for k, v in enumerate((me, mo, m2, m2, m3e, m3o, m4, m4)):
        cols = jnp.where(lane8 == k, v, cols)
    dmix = cols.T[0:8, :]
    mix = mix_ref[...]
    row = lambda a, k: a[k : k + 1, :]
    sides = []
    for side in range(2):
        inner = sum(row(mix, 2 * b + side) * row(dmix, 2 * b + side) for b in range(4))
        sides.append([row(mix, 2 * b + side) * (row(dmix, 2 * b + side) - inner) for b in range(4)])
    dwe = jnp.zeros((1, TT), F32)
    dwo = jnp.zeros((1, TT), F32)
    for b in range(4):
        e, o = means_of(sides[0][b], sides[1][b])[b]
        dwe = dwe + e
        dwo = dwo + o
    dw = jnp.concatenate([dwe, dwo], axis=1)
    hi, mid, lo = split3(jnp.broadcast_to(dw, (16, 2 * TT)))
    which = lax.broadcasted_iota(jnp.int32, (16, 2 * TT), 0)
    dw3 = jnp.where(which == 0, hi, jnp.where(which == 1, mid, jnp.where(which == 2, lo, jnp.zeros_like(hi))))
    usum[...] += dot(dw3, oht[...], NT)
    at = dot(oht[...], w_ref[...], NT).astype(B16)
    big[...] += dot(at, gb, NN)

    @pl.when(i == pl.num_programs(0) - 1)
    def _():
        us = usum[...]
        urow = us[0:1] + us[1:2] + us[2:3]
        hi, mid, lo = split3(jnp.broadcast_to(urow, (16, CC)))
        which = lax.broadcasted_iota(jnp.int32, (16, CC), 0)
        u3 = jnp.where(which == 0, hi, jnp.where(which == 1, mid, jnp.where(which == 2, lo, jnp.zeros_like(hi))))
        gs = dot(u3, table_ref[...], NN)
        small_ref[5:6, :] = gs[0:1] + gs[1:2] + gs[2:3]
        ucol = jnp.broadcast_to(urow, (128, CC)).T[:, 0:1]
        total = jnp.zeros(gt_ref.shape, F32)
        for j in range(5):
            m = big[CJ * j : CJ * (j + 1), :] + ucol[CJ * j : CJ * (j + 1)] * scorer_ref[...]
            total = total + m * taps_ref[j : j + 1, :]
            small_ref[j : j + 1, :] = jnp.sum(m * raw_ref[...].astype(F32), axis=0, keepdims=True)
        gt_ref[...] = total

def gbst_bwd(cid, w, mix, tok, hid, nb, gain, table, raw, taps, scorer):
    tiles = cid.shape[0]
    d = table.shape[1]
    rows = tiles * TT
    const = lambda shape: pl.BlockSpec(shape, lambda i: (0,) * len(shape))
    tile = lambda width: pl.BlockSpec((TT, width), lambda i: (i, 0))
    return pl.pallas_call(
        gbst_bwd_body, grid=(tiles,), name="gbst_bwd",
        in_specs=[pl.BlockSpec((None, 8, 2 * TT), lambda i: (i, 0, 0)), tile(2 * TT), pl.BlockSpec((None, 8, TT), lambda i: (i, 0, 0)),
                  tile(d), tile(d), tile(d), const((1, d)), const((CC, d)), const((CJ, d)), const((8, d)), const((1, d))],
        out_specs=[const((CJ, d)), const((8, d))],
        out_shape=[jax.ShapeDtypeStruct((CJ, d), F32), jax.ShapeDtypeStruct((8, d), F32)],
        scratch_shapes=[pltpu.VMEM((CC, 2 * TT), B16), pltpu.VMEM((CC, d), F32), pltpu.VMEM((16, CC), F32)],
        compiler_params=pltpu.CompilerParams(vmem_limit_bytes=56 << 20),
        cost_estimate=pl.CostEstimate(flops=rows * CC * d * 8, transcendentals=0, bytes_accessed=rows * d * 12),
    )(cid, w, mix, tok, hid, nb, gain, table, raw, taps, scorer)

def gbst_tables(byte_table, conv_taps, block_scorer):
    table = byte_table.astype(F32)
    taps = conv_taps.astype(F32)
    scorer = block_scorer.astype(F32)
    vocab, d = table.shape
    raw = jnp.pad(table, ((0, CJ - vocab), (0, 0)))
    cat = (taps[:, None, :] * raw[None]).reshape(5 * CJ, d)
    cat = jnp.pad(cat, ((0, CC - 5 * CJ), (0, 0)))
    tv = jnp.einsum("jd,vd->jv", taps * scorer, raw, precision=lax.Precision.HIGHEST).reshape(1, 5 * CJ)
    tv = jnp.pad(tv, ((0, 0), (0, CC - 5 * CJ)))
    hi, mid, lo = split3_xla(tv)
    tvec = jnp.concatenate([hi, mid, lo, jnp.zeros((5, CC), B16)], axis=0)
    cat_hi, cat_lo, _ = split3_xla(cat)
    return cat_hi, cat_lo, tvec, raw.astype(B16), jnp.pad(taps, ((0, 3), (0, 0))), scorer[None]


def swapped(tree):
    return jax.tree.map(lambda a: lax.ppermute(a, "mp", [(0, 1), (1, 0)]), tree)


def matmul(a, b):
    return dot(a, b, NN)


def grad_of(a, b):
    return lax.dot_general(a, b, (((0,), (0,)), ((), ())), preferred_element_type=F32)


X_SWAP = ("dp", 0)
Y_SWAP = ("dp", 1)
Z_NEAR = ("seq", 0)
Z_FAR = ("seq", 1)


def hop(x, axis, bit):
    count = lax.axis_size(axis)
    return lax.ppermute(x, axis, [(i, i ^ (1 << bit)) for i in range(count)])


def side_of(axis, bit):
    return (lax.axis_index(axis) >> bit) & 1


def scatter_sum(x, order):
    for axis, bit in order:
        side = side_of(axis, bit)
        rows = x.shape[0] // 2
        keep = lax.dynamic_slice_in_dim(x, side * rows, rows, 0)
        send = lax.dynamic_slice_in_dim(x, (1 - side) * rows, rows, 0)
        x = keep + hop(send.astype(B16), axis, bit).astype(F32)
    return x


def gather_back(x, order):
    for axis, bit in reversed(order):
        side = side_of(axis, bit)
        other = hop(x, axis, bit)
        x = jnp.concatenate([jnp.where(side == 0, x, other), jnp.where(side == 0, other, x)], axis=0)
    return x


def reduced(parts, orders):
    parts = [scatter_sum(x, order).astype(B16) for x, order in zip(parts, orders)]
    return [gather_back(x, order) for x, order in zip(parts, orders)]


def queued_sum(x):
    x = lax.psum_scatter(x, "dp", scatter_dimension=0, tiled=True)
    x = lax.psum_scatter(x, "seq", scatter_dimension=0, tiled=True)
    x = lax.all_gather(x, "seq", axis=0, tiled=True)
    return lax.all_gather(x, "dp", axis=0, tiled=True).astype(F32)


def gelu_parts(gate):
    c = 0.7978845608028654
    inside = c * (gate + 0.044715 * gate * gate * gate)
    th = jnp.tanh(inside)
    value = 0.5 * gate * (1.0 + th)
    slope = 0.5 * (1.0 + th) + 0.5 * gate * (1.0 - th * th) * (c * (1.0 + 3.0 * 0.044715 * gate * gate))
    return value, slope


def local_item(
    byte_ids, true_lengths, byte_table, conv_taps, block_scorer, attn_gain, w_query, w_key, w_value,
    w_output, rel_table, ffn_gain, w_gate, w_up, w_down, out_grad,
):
    seq_count = lax.axis_size("seq")
    place = lax.axis_index("seq")
    core = lax.axis_index("mp")
    tok_rows = out_grad.shape[0]
    half = tok_rows // 2
    width = out_grad.shape[2]
    own_rows = seq_count * half
    total = 2 * own_rows
    proj = w_query.shape[1]
    first = core == 0

    def halves(full):
        parts = full.reshape(seq_count, 2, half, full.shape[1])
        own = jnp.where(first, parts[:, 0], parts[:, 1]).reshape(own_rows, -1)
        other = jnp.where(first, parts[:, 1], parts[:, 0]).reshape(own_rows, -1)
        return own, other

    def whole(own, other):
        shape = (seq_count, half, own.shape[1])
        low, high = jnp.where(first, own, other), jnp.where(first, other, own)
        return jnp.stack([low.reshape(shape), high.reshape(shape)], axis=1).reshape(total, -1)

    ids = lax.all_to_all(byte_ids, "seq", split_axis=1, concat_axis=0, tiled=True)[:, 0]
    length = lax.dynamic_index_in_dim(true_lengths, place, 0, keepdims=False)
    wo_other, wg_other, wu_other, wd_other = swapped((w_output, w_gate, w_up, w_down))
    grad_rows = lax.dynamic_slice_in_dim(out_grad, core * half, half, 0)
    grad_own = lax.all_to_all(grad_rows, "seq", split_axis=1, concat_axis=0, tiled=True)
    grad_own = grad_own.reshape(own_rows, width)

    byte_count = ids.shape[0]
    shown = jnp.where(jnp.arange(byte_count, dtype=jnp.int32) < length, ids, -1)
    framed = jnp.pad(shown, (2, 2), constant_values=-1)
    rows = jnp.stack([framed[j : j + byte_count] for j in range(5)])
    rows = rows.reshape(5, seq_count, 2, 2 * half)
    rows = jnp.where(first, rows[:, :, 0], rows[:, :, 1])
    tiles = own_rows // TT
    rows = rows.reshape(5, tiles, TT, 2).transpose(1, 0, 3, 2).reshape(tiles, 5, 2 * TT)
    cid = jnp.pad(rows, ((0, 0), (0, 3), (0, 0)), constant_values=-1)

    table_cat, table_rest, tvec, raw, taps8, scorer = gbst_tables(byte_table, conv_taps, block_scorer)
    gain_one = attn_gain.astype(F32)[None]
    gain_two = ffn_gain.astype(F32)[None]
    tokens, normed, pool_w, mix = gbst_fwd(cid, tvec, table_cat, table_rest, gain_one)
    normed_all = whole(normed, swapped(normed))
    w_qkv = jnp.concatenate([w_query, w_key, w_value], axis=1)
    qkv = matmul(normed_all, w_qkv).astype(B16)
    limit = ((length + 1) // 2).reshape(1)
    weights, att, linv = attn_fwd(limit, qkv, bias_curve(rel_table, proj // DH))
    att_own, att_send = halves(att.astype(B16))
    att_recv = swapped(att_send)
    hidden = tokens + matmul(att_own, w_output) + matmul(att_recv, wo_other)
    r_two = lax.rsqrt(jnp.mean(hidden * hidden, axis=1, keepdims=True) + EPS)
    normed_two = (hidden * r_two * gain_two).astype(B16)
    w_g = jnp.concatenate([w_gate, wg_other], axis=1)
    w_u = jnp.concatenate([w_up, wu_other], axis=1)
    w_d = jnp.concatenate([w_down, wd_other], axis=0)
    gate = matmul(normed_two, w_g)
    up = matmul(normed_two, w_u)
    act, slope = gelu_parts(gate)
    inner = (act * up).astype(B16)
    layer = (hidden + matmul(inner, w_d)).astype(B16)
    grad_inner = dot(grad_own, w_d, NT)
    gate_back = (grad_inner * up * slope).astype(B16)
    up_back = (grad_inner * act).astype(B16)
    g_down = grad_of(inner, grad_own)
    g_gate = grad_of(normed_two, gate_back)
    g_up = grad_of(normed_two, up_back)
    two_back = dot(gate_back, w_g, NT) + dot(up_back, w_u, NT)
    u_two = two_back * gain_two
    x_two = hidden * r_two
    g_gain_two = jnp.sum(two_back * x_two, axis=0)
    hidden_back = grad_own.astype(F32) + r_two * (u_two - x_two * jnp.mean(u_two * x_two, axis=1, keepdims=True))
    hidden_low = hidden_back.astype(B16)
    g_out_own = grad_of(att_own, hidden_low)
    g_out_other = grad_of(att_recv, hidden_low)
    d_own = dot(hidden_low, w_output, NT).astype(B16)
    d_send = dot(hidden_low, wo_other, NT).astype(B16)
    d_att = whole(d_own, swapped(d_send))

    ffn_width = w_gate.shape[1]
    low = lambda a: a.astype(B16)
    rows_two = jnp.concatenate([g_down[:ffn_width], g_out_own], axis=0)
    rows_two_send = low(jnp.concatenate([g_down[ffn_width:], g_out_other], axis=0))
    rows_one = jnp.concatenate([g_gate[:, :ffn_width], g_up[:, :ffn_width]], axis=1)
    rows_one_send = low(jnp.concatenate([g_gate[:, ffn_width:], g_up[:, ffn_width:]], axis=1))
    rows_two = queued_sum(low(rows_two + swapped(rows_two_send).astype(F32)))
    rows_one = queued_sum(low(rows_one + swapped(rows_one_send).astype(F32)))
    big = [rows_one[:, :ffn_width], rows_one[:, ffn_width:], rows_two[:ffn_width], rows_two[ffn_width:]]

    dk, dv, dq, near, far = attn_bwd(weights, qkv, d_att, att, linv)
    partial = dot(dq, w_query, NT) + dot(dk, w_key, NT) + dot(dv, w_value, NT)
    part_own, part_send = halves(partial.astype(B16))
    normed_back = (part_own.astype(F32) + swapped(part_send).astype(F32)).astype(B16)
    g_rel = rel_grad(near, far, near.shape[2])
    g_qkv = jnp.concatenate([grad_of(normed_all, d) for d in (dq, dk, dv)], axis=0)
    cut = g_qkv.shape[0] // 2
    first_order = (X_SWAP, Y_SWAP, Z_NEAR, Z_FAR)
    second_order = (Y_SWAP, X_SWAP, Z_NEAR, Z_FAR)
    g_qkv = jnp.concatenate(reduced([g_qkv[:cut], g_qkv[cut:]], [first_order, second_order]), axis=0).astype(F32)
    g_query, g_key, g_value = (g_qkv[i * width : (i + 1) * width] for i in range(3))
    g_table, small = gbst_bwd(
        cid, pool_w, mix, tokens, hidden_back, normed_back, gain_one, table_cat, raw, taps8, scorer
    )
    rel_row = jnp.pad(g_rel.reshape(1, -1), ((0, 0), (0, width - g_rel.size)))
    rel_rows = jnp.where(first, jnp.concatenate([rel_row, jnp.zeros_like(rel_row)]),
                         jnp.concatenate([jnp.zeros_like(rel_row), rel_row]))
    tail = jnp.concatenate([g_table, small[:7], g_gain_two[None], rel_rows, jnp.zeros((6, width), F32)], axis=0)
    half_tail = tail.shape[0] // 2
    lower = jnp.where(first, tail[:half_tail], tail[half_tail:])
    upper = jnp.where(first, tail[half_tail:], tail[:half_tail])
    mine = lower + swapped(upper.astype(B16)).astype(F32)
    short = (X_SWAP, Y_SWAP)
    mine = scatter_sum(mine, short)
    for axis, bit in (Z_NEAR, Z_FAR):
        mine = mine + hop(mine.astype(B16), axis, bit).astype(F32)
    mine = gather_back(mine.astype(B16), short)
    theirs = swapped(mine)
    tail = jnp.concatenate([jnp.where(first, mine, theirs), jnp.where(first, theirs, mine)], axis=0).astype(F32)
    g_table, small, g_gain_two = tail[:CJ], tail[CJ : CJ + 7], tail[CJ + 7]
    g_rel = jnp.where(first, tail[CJ + 8], tail[CJ + 9])[: g_rel.size].reshape(g_rel.shape)

    sent = layer.reshape(seq_count, half, width)
    layer_out = lax.all_to_all(sent[:, :, None], "seq", split_axis=0, concat_axis=2, tiled=True)
    layer_out = layer_out.reshape(half, seq_count, width).astype(F32)
    vocab = byte_table.shape[0]
    return (
        layer_out, g_table[:vocab], small[:5], small[5], small[6], g_query, g_key, g_value, big[3], g_rel,
        g_gain_two, big[0], big[1], big[2],
    )


def chosen(*args):
    ids, lengths, w_query, out_grad = args[0], args[1], args[6], args[15]
    seq_count = lax.axis_size("seq")
    total = out_grad.shape[0] * seq_count
    fits = (
        lengths.shape[0] == seq_count
        and lax.axis_size("mp") == 2
        and total % (2 * TT) == 0
        and total % CK == 0
        and w_query.shape[1] % 128 == 0
        and (ids.shape[0] // 2) % 12 == 0
    )
    return local_item(*args) if fits else local_general(*args)


def solution(mesh):
    return jax.shard_map(
        chosen,
        mesh=mesh,
        in_specs=(
            P("seq", "dp"),
            P("dp"),
            P(),
            P(),
            P(),
            P(),
            P(None, "mp"),
            P(None, "mp"),
            P(None, "mp"),
            P("mp", None),
            P(None, "mp"),
            P(),
            P(None, "mp"),
            P(None, "mp"),
            P("mp", None),
            P("seq", "dp", None),
        ),
        out_specs=(
            P(("seq", "mp"), "dp", None),
            P(),
            P(),
            P(),
            P(),
            P(None, "mp"),
            P(None, "mp"),
            P(None, "mp"),
            P("mp", None),
            P(None, "mp"),
            P(),
            P(None, "mp"),
            P(None, "mp"),
            P("mp", None),
        ),
        check_vma=False,
    )
```

```python
import functools

import jax
import jax.numpy as jnp
from jax import lax
from jax.experimental import pallas as pl
from jax.experimental.pallas import tpu as pltpu
from jax.sharding import PartitionSpec as P

DH = 64
BUCKETS = 32
MICRO = 4


EPS = 1e-06
NEG = -1000000000.0
EDGES = (12, 16, 23, 32, 46, 64, 91)
HIGH = lax.Precision.HIGHEST
F32 = jnp.float32
B16 = jnp.bfloat16


def extended(cells, sides, width):
    for axis, dim in sides:
        count = lax.axis_size(axis)
        ends = count - 1
        head = lax.slice_in_dim(cells, 0, width, axis=dim)
        tail = lax.slice_in_dim(cells, cells.shape[dim] - width, cells.shape[dim], axis=dim)
        cells = jnp.concatenate(
            [
                lax.ppermute(tail, axis, [(i, (i + 1) % count) for i in range(ends)]),
                cells,
                lax.ppermute(head, axis, [((i + 1) % count, i) for i in range(ends)]),
            ],
            axis=dim,
        )
    return cells


def for_sending(array):
    return jax.tree.map(lambda a: a.astype(jnp.bfloat16) if a.dtype == jnp.float32 else a, array)


def bucket_of(offset):
    distance = jnp.abs(offset)
    far = jnp.full(offset.shape, 8, jnp.int32)
    for edge in EDGES:
        far = far + (distance >= edge).astype(jnp.int32)
    near = jnp.where(distance < 8, distance, far)
    return near + 16 * (offset > 0).astype(jnp.int32)


def bias_onehot(query_places, key_places):
    offset = key_places[None, :] - query_places[:, None]
    return (bucket_of(offset)[:, :, None] == jnp.arange(BUCKETS, dtype=jnp.int32)).astype(F32)


def rms_norm(hidden, gain):
    return hidden * lax.rsqrt(jnp.mean(hidden * hidden, axis=-1, keepdims=True) + EPS) * gain


def activation(gate, up):
    return jax.nn.gelu(gate, approximate=True) * up


def gbst_tail(conv_out, scorer):
    byte_count, item_count, model_width = conv_out.shape
    weighted = jnp.einsum("pid,d->pi", conv_out, scorer, precision=HIGH)
    pooled_all = []
    scores_all = []
    for block_size in (1, 2, 3, 4):
        block_means = conv_out.reshape(
            byte_count // block_size, block_size, item_count, model_width
        ).mean(axis=1)
        pooled_all.append(jnp.repeat(block_means, block_size, axis=0))
        score_means = weighted.reshape(byte_count // block_size, block_size, item_count).mean(
            axis=1
        )
        scores_all.append(jnp.repeat(score_means, block_size, axis=0))
    mixing = jax.nn.softmax(jnp.stack(scores_all), axis=0)
    mixture = mixing[0][:, :, None] * pooled_all[0]
    for block_index in range(1, 4):
        mixture = mixture + mixing[block_index][:, :, None] * pooled_all[block_index]
    return mixture.reshape(byte_count // 2, 2, item_count, model_width).mean(axis=1)


def local_general(
    byte_ids,
    true_lengths,
    byte_table,
    conv_taps,
    block_scorer,
    attn_gain,
    w_query,
    w_key,
    w_value,
    w_output,
    rel_table,
    ffn_gain,
    w_gate,
    w_up,
    w_down,
    out_grad,
):
    seq_count = lax.axis_size("seq")
    seq_place = lax.axis_index("seq")
    core_place = lax.axis_index("mp")
    byte_rows = byte_ids.shape[0]
    tok_rows = byte_rows // 2
    half_rows = tok_rows // lax.axis_size("mp")
    total_tokens = tok_rows * seq_count
    item_count = byte_ids.shape[1] // MICRO
    proj_width = w_query.shape[1]
    head_count = proj_width // DH
    ffn_width = w_gate.shape[1]
    taps = conv_taps.astype(F32)
    scorer = block_scorer.astype(F32)
    gain_one = attn_gain.astype(F32)
    gain_two = ffn_gain.astype(F32)
    rel_local = rel_table.astype(F32)
    gate_up = jnp.concatenate([w_gate, w_up], axis=1)
    query_places = seq_place * tok_rows + jnp.arange(tok_rows, dtype=jnp.int32)
    key_places = jnp.arange(total_tokens, dtype=jnp.int32)
    onehot_bias = bias_onehot(query_places, key_places)
    bias = jnp.einsum("qkb,bh->hqk", onehot_bias, rel_local, precision=HIGH)
    byte_places = seq_place * byte_rows + jnp.arange(byte_rows, dtype=jnp.int32)
    vocab_range = jnp.arange(byte_table.shape[0], dtype=jnp.int32)
    sum_table = jnp.zeros(byte_table.shape, F32)
    sum_taps = jnp.zeros(conv_taps.shape, F32)
    sum_scorer = jnp.zeros(block_scorer.shape, F32)
    sum_gain_one = jnp.zeros(attn_gain.shape, F32)
    sum_query = jnp.zeros(w_query.shape, F32)
    sum_key = jnp.zeros(w_key.shape, F32)
    sum_value = jnp.zeros(w_value.shape, F32)
    sum_output = jnp.zeros(w_output.shape, F32)
    sum_rel = jnp.zeros(rel_table.shape, F32)
    sum_gain_two = jnp.zeros(ffn_gain.shape, F32)
    sum_gate = jnp.zeros(w_gate.shape, F32)
    sum_up = jnp.zeros(w_up.shape, F32)
    sum_down = jnp.zeros(w_down.shape, F32)
    outputs = []
    for micro in range(MICRO):
        first = micro * item_count
        ids_now = byte_ids[:, first : first + item_count]
        lengths = true_lengths[first : first + item_count]
        keep = (byte_places[:, None] < lengths[None, :]).astype(F32)
        onehot = (ids_now[:, :, None] == vocab_range).astype(F32) * keep[:, :, None]
        embedded = jnp.einsum(
            "piv,vd->pid", onehot.astype(B16), byte_table, preferred_element_type=F32
        ).astype(B16)
        framed = extended(embedded, (("seq", 0),), 2)
        conv_out = taps[0] * framed[0:byte_rows]
        for tap_index in range(1, 5):
            conv_out = conv_out + taps[tap_index] * framed[tap_index : tap_index + byte_rows]
        tokens, gbst_pull = jax.vjp(gbst_tail, conv_out, scorer)
        normed, norm_pull = jax.vjp(rms_norm, tokens, gain_one)
        normed_low = normed.astype(B16)
        query = jnp.einsum("qid,dh->qih", normed_low, w_query, preferred_element_type=F32).astype(
            B16
        )
        keys_here = jnp.einsum("qid,dh->qih", normed_low, w_key, preferred_element_type=F32).astype(
            B16
        )
        values_here = jnp.einsum(
            "qid,dh->qih", normed_low, w_value, preferred_element_type=F32
        ).astype(B16)
        keys_all, values_all = (
            lax.all_gather(keys_here, "seq", axis=0, tiled=True),
            lax.all_gather(values_here, "seq", axis=0, tiled=True),
        )
        query4 = query.reshape(tok_rows, item_count, head_count, DH)
        keys4 = keys_all.reshape(total_tokens, item_count, head_count, DH)
        values4 = values_all.reshape(total_tokens, item_count, head_count, DH)
        key_ok = 2 * key_places[None, :] < lengths[:, None]

        def scores_of():
            raw = jnp.einsum("qihe,kihe->ihqk", query4, keys4, preferred_element_type=F32)
            return jnp.where(key_ok[:, None, None, :], raw + bias[None], NEG)

        scores = scores_of()
        top = jnp.max(scores, axis=-1, keepdims=True)
        log_total = top + jnp.log(jnp.sum(jnp.exp(scores - top), axis=-1, keepdims=True))
        probs_low = jnp.exp(scores - log_total).astype(B16)
        attended = (
            jnp.einsum("ihqk,kihe->qihe", probs_low, values4, preferred_element_type=F32)
            .reshape(tok_rows, item_count, proj_width)
            .astype(B16)
        )
        attn_half = lax.psum_scatter(
            jnp.einsum("qih,hd->qid", attended, w_output, preferred_element_type=F32),
            "mp",
            scatter_dimension=0,
            tiled=True,
        )
        tokens_half = lax.dynamic_slice_in_dim(tokens, core_place * half_rows, half_rows, 0)
        hidden_half = tokens_half + attn_half
        normed_two, norm_two_pull = jax.vjp(rms_norm, hidden_half, gain_two)
        normed_full = lax.all_gather(normed_two.astype(B16), "mp", axis=0, tiled=True)
        projected = jnp.einsum("qid,df->qif", normed_full, gate_up, preferred_element_type=F32)
        inner, inner_pull = jax.vjp(
            activation, projected[..., :ffn_width], projected[..., ffn_width:]
        )
        inner_low = inner.astype(B16)
        ffn_half = lax.psum_scatter(
            jnp.einsum("qif,fd->qid", inner_low, w_down, preferred_element_type=F32).astype(
                jnp.bfloat16
            ),
            "mp",
            scatter_dimension=0,
            tiled=True,
        ).astype(jnp.float32)
        outputs.append(hidden_half + ffn_half)
        grad_low = out_grad[:, first : first + item_count]
        grad_half = lax.dynamic_slice_in_dim(grad_low, core_place * half_rows, half_rows, 0).astype(
            F32
        )
        sum_down = sum_down + jnp.einsum(
            "qif,qid->fd", inner_low, grad_low, preferred_element_type=F32
        )
        grad_inner = jnp.einsum("qid,fd->qif", grad_low, w_down, preferred_element_type=F32)
        gate_grad, up_grad = inner_pull(grad_inner)
        gate_low = gate_grad.astype(B16)
        up_low = up_grad.astype(B16)
        sum_gate = sum_gate + jnp.einsum(
            "qid,qif->df", normed_full, gate_low, preferred_element_type=F32
        )
        sum_up = sum_up + jnp.einsum("qid,qif->df", normed_full, up_low, preferred_element_type=F32)
        normed_two_grad = lax.psum_scatter(
            jnp.einsum("qif,df->qid", gate_low, w_gate, preferred_element_type=F32)
            + jnp.einsum("qif,df->qid", up_low, w_up, preferred_element_type=F32),
            "mp",
            scatter_dimension=0,
            tiled=True,
        )
        hidden_norm_grad, gain_two_grad = norm_two_pull(normed_two_grad)
        hidden_grad = grad_half + hidden_norm_grad
        hidden_full = lax.all_gather(for_sending(hidden_grad), "mp", axis=0, tiled=True).astype(
            hidden_grad.dtype
        )
        hidden_low = hidden_full.astype(B16)
        sum_output = sum_output + jnp.einsum(
            "qih,qid->hd", attended, hidden_low, preferred_element_type=F32
        )
        attended_grad = jnp.einsum(
            "qid,hd->qih", hidden_low, w_output, preferred_element_type=F32
        ).astype(B16)
        attended_grad4 = attended_grad.reshape(tok_rows, item_count, head_count, DH)
        scores = scores_of()
        probs = jnp.exp(scores - log_total)
        probs_low = probs.astype(B16)
        probs_grad = jnp.einsum(
            "qihe,kihe->ihqk", attended_grad4, values4, preferred_element_type=F32
        )
        inner_sum = jnp.sum(probs * probs_grad, axis=-1, keepdims=True)
        scores_grad = probs * (probs_grad - inner_sum)
        sum_rel = sum_rel + jnp.einsum(
            "qkb,hqk->bh", onehot_bias, jnp.sum(scores_grad, axis=0), precision=HIGH
        )
        scores_low = scores_grad.astype(B16)
        query_grad = (
            jnp.einsum("ihqk,kihe->qihe", scores_low, keys4, preferred_element_type=F32)
            .reshape(tok_rows, item_count, proj_width)
            .astype(B16)
        )
        key_part = jnp.einsum("ihqk,qihe->kihe", scores_low, query4, preferred_element_type=F32)
        value_part = jnp.einsum(
            "ihqk,qihe->kihe", probs_low, attended_grad4, preferred_element_type=F32
        )
        key_sums = lax.psum_scatter(
            jnp.concatenate(
                [
                    key_part.reshape(tok_rows * lax.axis_size("seq"), item_count, proj_width),
                    value_part.reshape(tok_rows * lax.axis_size("seq"), item_count, proj_width),
                ],
                axis=2,
            ).astype(jnp.bfloat16),
            "seq",
            scatter_dimension=0,
            tiled=True,
        ).astype(jnp.float32)
        keys_grad = key_sums[..., :proj_width].astype(B16)
        values_grad = key_sums[..., proj_width:].astype(B16)
        sum_query = sum_query + jnp.einsum(
            "qid,qih->dh", normed_low, query_grad, preferred_element_type=F32
        )
        sum_key = sum_key + jnp.einsum(
            "qid,qih->dh", normed_low, keys_grad, preferred_element_type=F32
        )
        sum_value = sum_value + jnp.einsum(
            "qid,qih->dh", normed_low, values_grad, preferred_element_type=F32
        )
        partial_grad = (
            jnp.einsum("qih,dh->qid", query_grad, w_query, preferred_element_type=F32)
            + jnp.einsum("qih,dh->qid", keys_grad, w_key, preferred_element_type=F32)
            + jnp.einsum("qih,dh->qid", values_grad, w_value, preferred_element_type=F32)
        )
        normed_grad, gain_two_total = (
            lax.psum(partial_grad.astype(jnp.bfloat16), "mp").astype(jnp.float32),
            lax.psum(gain_two_grad.astype(jnp.bfloat16), "mp").astype(jnp.float32),
        )
        sum_gain_two = sum_gain_two + gain_two_total
        tokens_norm_grad, gain_one_grad = norm_pull(normed_grad)
        sum_gain_one = sum_gain_one + gain_one_grad
        tokens_grad = hidden_full + tokens_norm_grad
        conv_grad, scorer_grad = gbst_pull(tokens_grad)
        sum_scorer = sum_scorer + scorer_grad
        framed_grad = extended(conv_grad.astype(jnp.bfloat16), (("seq", 0),), 2).astype(
            conv_grad.dtype
        )
        embedded_grad = taps[0] * framed_grad[4 : 4 + byte_rows]
        for tap_index in range(1, 5):
            embedded_grad = (
                embedded_grad
                + taps[tap_index] * framed_grad[4 - tap_index : 4 - tap_index + byte_rows]
            )
        tap_sums = [
            jnp.sum(conv_grad * framed[tap_index : tap_index + byte_rows], axis=(0, 1))
            for tap_index in range(5)
        ]
        sum_taps = sum_taps + jnp.stack(tap_sums)
        sum_table = sum_table + jnp.einsum("piv,pid->vd", onehot, embedded_grad, precision=HIGH)
    totals = lax.psum(
        (
            sum_table,
            sum_taps,
            sum_scorer,
            sum_gain_one,
            sum_query,
            sum_key,
            sum_value,
            sum_output,
            sum_rel,
            sum_gain_two,
            sum_gate,
            sum_up,
            sum_down,
        ),
        ("dp", "seq"),
    )
    layer_out = jnp.concatenate(outputs, axis=1)
    return (
        layer_out,
        totals[0],
        totals[1],
        totals[2],
        totals[3],
        totals[4],
        totals[5],
        totals[6],
        totals[7],
        totals[8],
        totals[9],
        totals[10],
        totals[11],
        totals[12],
    )


LOG2E = 1.4426950408889634
LN2 = 0.6931471805599453
NT = (((1,), (1,)), ((), ()))
NN = (((1,), (0,)), ((), ()))
CK = 256
SUB = 3

def dot(a, b, dims):
    return lax.dot_general(a, b, dims, preferred_element_type=F32)

def split3(x):
    hi = x.astype(B16)
    rest = x - hi.astype(F32)
    mid = rest.astype(B16)
    lo = (rest - mid.astype(F32)).astype(B16)
    return hi, mid, lo

def split3_xla(x):
    cut = lambda a: lax.reduce_precision(a, exponent_bits=8, mantissa_bits=7)
    hi = cut(x)
    mid = cut(x - hi)
    return hi.astype(B16), mid.astype(B16), (x - hi - mid).astype(B16)


def attn_fwd_body(limit_ref, q_ref, k_ref, v_ref, curve_ref, e_ref, o_ref, ot_ref, inv_ref,
                  kext, vext, table, qext, norms):
    total = k_ref.shape[0]
    tq = CK
    chunks = total // CK
    step = pl.program_id(1)

    @pl.when(step == 0)
    def _():
        lane = lax.broadcasted_iota(jnp.int32, (total, 128), 1)
        place = lax.broadcasted_iota(jnp.int32, (total, 128), 0)
        masked = jnp.where(place < limit_ref[0], 0.0, -1e9).astype(F32)
        k = k_ref[...].astype(F32)
        q = q_ref[...].astype(F32)
        pick = lax.broadcasted_iota(jnp.int32, (128, 128), 0) // 64 == lax.broadcasted_iota(jnp.int32, (128, 128), 1)
        pick = jnp.where(pick, 1.0, 0.0).astype(B16)
        size_q = jnp.max(dot((q * q).astype(B16), pick, NN), axis=0, keepdims=True)
        size_k = jnp.max(dot((k * k).astype(B16), pick, NN), axis=0, keepdims=True)
        both = size_q * size_k
        vt = v_ref[...].T
        for h in range(2):
            norms[h] = jnp.max(both[:, h : h + 1])
            own = (lane < 64) if h == 0 else (lane >= 64)
            base = 64 if h == 0 else 0
            extra = jnp.where(lane == base, masked, jnp.where((lane > base) & (lane < base + 4), 1.0, 0.0))
            kext[h] = jnp.where(own, k, extra).astype(B16)
            vext[h, 0:64, :] = vt[64 * h : 64 * h + 64, :]
            vext[h, 64:80, :] = jnp.ones((16, total), B16)
            curve = curve_ref[h : h + 1, :]
            for g in range(5):
                lo = 1024 + 2 * CK - g * CK - 256
                if g in (0, 4):
                    table[h, g * CK : (g + 1) * CK, :] = jnp.broadcast_to(curve[:, lo : lo + 1], (CK, CK))
                else:
                    window = jnp.broadcast_to(curve[:, lo : lo + 512], (CK, 512))
                    rolled = pltpu.roll(window, 0, 1, stride=1, stride_axis=0)
                    table[h, g * CK : (g + 1) * CK, :] = rolled[:, 256:512]

    lane_q = lax.broadcasted_iota(jnp.int32, (tq, 128), 1)

    def scores(h, u, c):
        d = jnp.clip(c - (step * SUB + u), -2, 2) + 2
        k_now = kext[h, pl.ds(c * CK if isinstance(c, int) else pl.multiple_of(c * CK, CK), CK), :]
        return dot(k_now, qext[u, h], NT) * LOG2E + table[h, pl.ds(pl.multiple_of(d * CK, CK), CK), :]

    for u in range(SUB):
        q = q_ref[pl.ds(pl.multiple_of((step * SUB + u) * tq, tq), tq), :]
        for h in range(2):
            own = (lane_q < 64) if h == 0 else (lane_q >= 64)
            base = 64 if h == 0 else 0
            qext[u, h] = jnp.where(own, q, jnp.where(lane_q == base, 1.0, 0.0).astype(B16))

    for h in range(2):
        @pl.when(norms[h] > 48.0 * 48.0)
        def _(h=h):
            own = (lane_q < 64) if h == 0 else (lane_q >= 64)
            base = 64 if h == 0 else 0

            def settle(u, carry):
                def grow(c, top):
                    return jnp.maximum(top, jnp.max(scores(h, u, c), axis=0, keepdims=True))
                top = lax.fori_loop(0, chunks, grow, jnp.full((1, tq), -3e38, F32))
                hi, mid, lo = split3(-jnp.broadcast_to(top * LN2, (128, tq)).T)
                extra = jnp.where(lane_q == base, jnp.ones_like(hi), jnp.zeros_like(hi))
                for at, part in ((1, hi), (2, mid), (3, lo)):
                    extra = jnp.where(lane_q == base + at, part, extra)
                qext[u, h] = jnp.where(own, qext[u, h], extra)
                return carry
            lax.fori_loop(0, SUB, settle, 0)

    for u in range(SUB):
        cols = slice(u * tq, (u + 1) * tq)
        for h in range(2):
            for c in range(chunks):
                e_ref[h, c * CK : (c + 1) * CK, cols] = jnp.exp2(scores(h, u, c)).astype(B16)
        outs = []
        for h in range(2):
            sums = dot(vext[h], e_ref[h, :, cols], NN)
            inv = 1.0 / sums[64:65, :]
            inv_ref[h : h + 1, cols] = inv
            outs.append(sums[0:64, :] * inv)
        out = jnp.concatenate(outs, axis=0)
        ot_ref[:, cols] = out
        o_ref[cols, :] = out.astype(B16).T

def attn_fwd(limit, qkv, curve):
    total = qkv.shape[0]
    pairs = qkv.shape[1] // 3 // 128
    tq = CK
    full = lambda off: pl.BlockSpec((total, 128), lambda p, i, s: (0, off + p))
    spec = pltpu.PrefetchScalarGridSpec(
        num_scalar_prefetch=1, grid=(pairs, total // (tq * SUB)),
        in_specs=[full(0), full(pairs), full(2 * pairs), pl.BlockSpec((None, 2, 2048), lambda p, i, s: (p, 0, 0))],
        out_specs=[
            pl.BlockSpec((2, total, SUB * tq), lambda p, i, s: (p, 0, i)),
            pl.BlockSpec((SUB * tq, 128), lambda p, i, s: (i, p)),
            pl.BlockSpec((128, SUB * tq), lambda p, i, s: (p, i)),
            pl.BlockSpec((None, 2, SUB * tq), lambda p, i, s: (p, 0, i)),
        ],
        scratch_shapes=[
            pltpu.VMEM((2, total, 128), B16), pltpu.VMEM((2, 80, total), B16),
            pltpu.VMEM((2, 5 * CK, tq), F32), pltpu.VMEM((SUB, 2, tq, 128), B16),
            pltpu.SMEM((2,), F32),
        ])
    n = 2 * pairs * total * total
    return pl.pallas_call(
        attn_fwd_body, grid_spec=spec, name="attn_fwd",
        out_shape=[jax.ShapeDtypeStruct((2 * pairs, total, total), B16),
                   jax.ShapeDtypeStruct((total, 128 * pairs), B16),
                   jax.ShapeDtypeStruct((128 * pairs, total), F32),
                   jax.ShapeDtypeStruct((pairs, 2, total), F32)],
        compiler_params=pltpu.CompilerParams(vmem_limit_bytes=56 << 20, dimension_semantics=("arbitrary", "arbitrary")),
        cost_estimate=pl.CostEstimate(flops=4 * 64 * n, transcendentals=n, bytes_accessed=2 * n),
    )(limit, qkv, qkv, qkv, curve)

def attn_bwd_body(e_ref, k_ref, v_ref, q_ref, do_ref, ot_ref, inv_ref,
                  dk_ref, dv_ref, dqo_ref, near_ref, far_ref,
                  doe, dot_, qind, ds, band, dq_ref):
    total = q_ref.shape[0]
    ck = k_ref.shape[0]
    blocks = total // CK
    chunks = pl.num_programs(1)
    step = pl.program_id(1)

    @pl.when(step == 0)
    def _():
        qt = q_ref[...].T
        dt = do_ref[...].T
        row = lax.broadcasted_iota(jnp.int32, (64, total), 0)
        col = lax.broadcasted_iota(jnp.int32, (64, total), 1)
        for h in range(2):
            at = slice(64 * h, 64 * h + 64)
            part = (dt[at].astype(F32) * inv_ref[h : h + 1, :]).astype(B16)
            dot_[h] = part
            inner = -jnp.sum(part.astype(F32) * ot_ref[at, :], axis=0, keepdims=True)
            hi, mid, lo = split3(jnp.broadcast_to(inner, (64, total)))
            extra = jnp.where(row == 0, hi, jnp.where(row == 1, mid, jnp.where(row == 2, lo, jnp.zeros_like(hi))))
            doe[h, 64 * h : 64 * h + 64, :] = part
            doe[h, 64 - 64 * h : 128 - 64 * h, :] = extra
            qind[h, 0:64, :] = qt[at]
            qind[h, 64:96, :] = jnp.where(row == (col >> 7), 1.0, 0.0)[0:32].astype(B16)
        dq_ref[...] = jnp.zeros_like(dq_ref)
        band[...] = jnp.zeros_like(band)
        far_ref[...] = jnp.zeros_like(far_ref)

    lane = lax.broadcasted_iota(jnp.int32, (ck, 128), 1)
    v = v_ref[...]
    kt = k_ref[...].T
    for h in range(2):
        own = (lane < 64) if h == 0 else (lane >= 64)
        base = 64 if h == 0 else 0
        ones = jnp.where((lane >= base) & (lane < base + 3), 1.0, 0.0).astype(B16)
        vx = jnp.where(own, v, ones)
        for c in range(blocks):
            cols = slice(c * CK, (c + 1) * CK)
            pg = dot(vx, doe[h, :, cols], NN)
            ds[h, :, cols] = e_ref[h, :, cols] * pg.astype(B16)
    block = lax.broadcasted_iota(jnp.int32, (32, CK), 0)
    for h in range(2):
        at = slice(64 * h, 64 * h + 64)
        dv_ref[at, :] = dot(dot_[h], e_ref[h], NT).astype(B16)
        dk = dot(qind[h], ds[h], NT)
        dk_ref[at, :] = dk[0:64].astype(B16)
        dq_ref[at, :] += dot(kt[at], ds[h], NN)
        for u in range(SUB):
            kb = step * SUB + u
            rows = slice(u * CK, (u + 1) * CK)
            sums_u = dk[64:96, rows]
            far_ref[h, 0] += jnp.where(block < 2 * kb - 1, sums_u, 0.0)
            far_ref[h, 1] += jnp.where(block >= 2 * kb + 3, sums_u, 0.0)
            band[h, :, 128 : 128 + CK] += ds[h, rows, pl.ds(pl.multiple_of(kb * CK, CK), CK)].astype(F32)

            @pl.when(kb > 0)
            def _(h=h, kb=kb, rows=rows):
                band[h, :, 0:128] += ds[h, rows, pl.ds(pl.multiple_of(kb * CK - 128, 128), 128)].astype(F32)

            @pl.when(kb < blocks - 1)
            def _(h=h, kb=kb, rows=rows):
                band[h, :, 128 + CK : 256 + CK] += ds[h, rows, pl.ds(pl.multiple_of(kb * CK + CK, 128), 128)].astype(F32)

    @pl.when(step == chunks - 1)
    def _():
        dqo_ref[...] = dq_ref[...].astype(B16)
        width = CK + 256
        row = lax.broadcasted_iota(jnp.int32, (CK, width), 0)
        col = lax.broadcasted_iota(jnp.int32, (CK, width), 1)
        offset = row - col + 128
        for h in range(2):
            all_now = band[h]
            near = jnp.where(jnp.abs(offset) < 128, all_now, 0.0)
            folded = near[0:8, :]
            for g in range(1, CK // 8):
                folded = folded + pltpu.roll(near[8 * g : 8 * g + 8, :], width - 8 * g, 1)
            line = folded[0:1, :]
            for g in range(1, 8):
                line = line + pltpu.roll(folded[g : g + 1, :], width - g, 1)
            near_ref[h, 0:1, :] = line
            near_ref[h, 1:2, :] = jnp.sum(jnp.where(offset >= 128, all_now, 0.0), axis=0, keepdims=True)
            near_ref[h, 2:3, :] = jnp.sum(jnp.where(offset <= -128, all_now, 0.0), axis=0, keepdims=True)
            near_ref[h, 3:8, :] = jnp.zeros((5, width), F32)

def attn_bwd(e, qkv, d_att, att_t, inv):
    total = qkv.shape[0]
    pairs = qkv.shape[1] // 3 // 128
    ck = CK * SUB
    full = lambda off: pl.BlockSpec((total, 128), lambda p, i: (0, off + p))
    part = lambda off: pl.BlockSpec((ck, 128), lambda p, i: (i, off + p))
    flat = pl.BlockSpec((128, ck), lambda p, i: (p, i))
    tall = pl.BlockSpec((128, total), lambda p, i: (p, 0))
    n = 2 * pairs * total * total
    return pl.pallas_call(
        attn_bwd_body, grid=(pairs, total // ck), name="attn_bwd",
        in_specs=[pl.BlockSpec((2, ck, total), lambda p, i: (p, i, 0)), part(pairs), part(2 * pairs),
                  full(0), full(0), tall, pl.BlockSpec((None, 2, total), lambda p, i: (p, 0, 0))],
        out_specs=[flat, flat, tall,
                   pl.BlockSpec((2, 8, CK + 256), lambda p, i: (p, 0, 0)),
                   pl.BlockSpec((2, 2, 32, CK), lambda p, i: (p, 0, 0, 0))],
        out_shape=[jax.ShapeDtypeStruct((128 * pairs, total), B16)] * 3
        + [jax.ShapeDtypeStruct((2 * pairs, 8, CK + 256), F32), jax.ShapeDtypeStruct((2 * pairs, 2, 32, CK), F32)],
        scratch_shapes=[
            pltpu.VMEM((2, 128, total), B16), pltpu.VMEM((2, 64, total), B16), pltpu.VMEM((2, 96, total), B16),
            pltpu.VMEM((2, ck, total), B16), pltpu.VMEM((2, CK, CK + 256), F32), pltpu.VMEM((128, total), F32),
        ],
        compiler_params=pltpu.CompilerParams(vmem_limit_bytes=60 << 20, dimension_semantics=("arbitrary", "arbitrary")),
        cost_estimate=pl.CostEstimate(flops=8 * 64 * n, transcendentals=0, bytes_accessed=2 * n),
    )(e, qkv, qkv, qkv, d_att, att_t, inv)

def bias_curve(rel, heads):
    offset = 1024 - jnp.arange(2048, dtype=jnp.int32)
    onehot = (bucket_of(offset)[:, None] == jnp.arange(32, dtype=jnp.int32)).astype(F32)
    curve = jnp.einsum("xb,bh->hx", onehot, rel.astype(F32) * LOG2E, precision=lax.Precision.HIGHEST)
    return curve.reshape(heads // 2, 2, 2048)

def rel_grad(near, far, width):
    x = jnp.arange(width, dtype=jnp.int32)
    onehot = (bucket_of(128 - x)[:, None] == jnp.arange(32, dtype=jnp.int32)).astype(F32)
    onehot = onehot * (x[:, None] < 256)
    g = jnp.einsum("hx,xb->bh", near[:, 0, :], onehot, precision=lax.Precision.HIGHEST)
    up = jnp.sum(near[:, 1, :], axis=1) + jnp.sum(far[:, 0], axis=(1, 2))
    down = jnp.sum(near[:, 2, :], axis=1) + jnp.sum(far[:, 1], axis=(1, 2))
    slot = jnp.arange(32)[:, None]
    return g + jnp.where(slot == 31, up[None], 0.0) + jnp.where(slot == 15, down[None], 0.0)

CJ = 272
CC = 1408
TT = 384

def means_of(even, odd):
    t = lax.broadcasted_iota(jnp.int32, even.shape, 1)
    width = even.shape[1]
    prev = lambda x: pltpu.roll(x, 1, 1)
    succ = lambda x: pltpu.roll(x, width - 1, 1)
    two = even + odd
    four = two + jnp.where(t % 2 == 0, succ(two), prev(two))
    place = t - 3 * ((t * 21846) >> 16)
    first = two + succ(even)
    middle_e = prev(two) + even
    middle_o = odd + succ(two)
    last = prev(odd) + two
    three_e = jnp.where(place == 0, first, jnp.where(place == 1, middle_e, last))
    three_o = jnp.where(place == 0, first, jnp.where(place == 1, middle_o, last))
    third = 1.0 / 3.0
    return [(even, odd), (two * 0.5, two * 0.5), (three_e * third, three_o * third), (four * 0.25, four * 0.25)]

def masks():
    t = lax.broadcasted_iota(jnp.int32, (TT, 2 * TT), 0)
    p = lax.broadcasted_iota(jnp.int32, (TT, 2 * TT), 1)
    par = p >= TT
    tp = jnp.where(par, p - TT, p)
    byte = 2 * tp + jnp.where(par, 1, 0)
    third = lambda x: (x * 21846) >> 16
    blk = third(byte)
    return t == tp, par, (t >> 1) == (tp >> 1), third(2 * t) == blk, third(2 * t + 1) == blk

def fill_onehot(ids_ref, oht):
    row = lax.broadcasted_iota(jnp.int32, (CJ, TT), 0)
    for j in range(5):
        for side in range(2):
            hit = row == ids_ref[j + side : j + side + 1, :]
            oht[CJ * j : CJ * (j + 1), TT * side : TT * (side + 1)] = jnp.where(hit, 1.0, 0.0).astype(B16)
    oht[5 * CJ :, :] = jnp.zeros((CC - 5 * CJ, 2 * TT), B16)

def gbst_fwd_body(cid_ref, raw_ref, taps_ref, scorer_ref, gain_ref, tok_ref, norm_ref, w_ref, mix_ref, table_ref,
                  oht, rest, tvec, both, wide):
    @pl.when(pl.program_id(0) == 0)
    def _():
        raw = raw_ref[...].astype(F32)
        for j in range(5):
            at = slice(CJ * j, CJ * (j + 1))
            tap = taps_ref[j : j + 1, :].astype(F32)
            cat = raw * tap
            hi = cat.astype(B16)
            table_ref[at, :] = hi
            rest[at, :] = (cat - hi.astype(F32)).astype(B16)
            parts = split3(jnp.broadcast_to(tap * scorer_ref[...].astype(F32), (16, cat.shape[1])))
            which = lax.broadcasted_iota(jnp.int32, (16, cat.shape[1]), 0)
            zero = jnp.zeros_like(parts[0])
            rows = jnp.where(which == 0, parts[0], jnp.where(which == 1, parts[1], jnp.where(which == 2, parts[2], zero)))
            scores = dot(rows, raw_ref[...], NT)
            line = split3(jnp.broadcast_to(scores[0:1] + scores[1:2] + scores[2:3], (16, CJ)))
            which = lax.broadcasted_iota(jnp.int32, (16, CJ), 0)
            zero = jnp.zeros_like(line[0])
            tvec[j] = jnp.where(which == 0, line[0], jnp.where(which == 1, line[1], jnp.where(which == 2, line[2], zero)))
        table_ref[5 * CJ :, :] = jnp.zeros((CC - 5 * CJ, table_ref.shape[1]), B16)
        rest[5 * CJ :, :] = jnp.zeros((CC - 5 * CJ, table_ref.shape[1]), B16)
    fill_onehot(cid_ref, oht)
    parts = dot(tvec[0], oht[0:CJ, :], NN)
    for j in range(1, 5):
        parts = parts + dot(tvec[j], oht[CJ * j : CJ * (j + 1), :], NN)
    weighted = parts[0:1] + parts[1:2] + parts[2:3]
    scores = means_of(weighted[:, :TT], weighted[:, TT:])
    rows = []
    for side in range(2):
        mine = [s[side] for s in scores]
        top = jnp.maximum(jnp.maximum(mine[0], mine[1]), jnp.maximum(mine[2], mine[3]))
        e = [jnp.exp(s - top) for s in mine]
        inv = 1.0 / (e[0] + e[1] + e[2] + e[3])
        rows.append([x * inv for x in e])
    mix = jnp.concatenate([rows[side][b] for b in range(4) for side in range(2)], axis=0)
    mix_ref[...] = mix
    col = mix.T
    c = lambda i: col[:, i : i + 1]
    same, par, pair, tri_e, tri_o = masks()
    w = jnp.where(same, jnp.where(par, 0.5 * c(1), 0.5 * c(0)) + 0.25 * (c(2) + c(3)), 0.0)
    w = w + jnp.where(pair, 0.125 * (c(6) + c(7)), 0.0)
    w = w + jnp.where(tri_e, c(4) * (1.0 / 6.0), 0.0) + jnp.where(tri_o, c(5) * (1.0 / 6.0), 0.0)
    w_hi = w.astype(B16)
    w_lo = (w - w_hi.astype(F32)).astype(B16)
    w_ref[...] = w_hi
    both[0:TT, :] = w_hi
    both[TT:, :] = w_lo
    a = dot(both[...], oht[...], NT)
    a = a[0:TT] + a[TT:]
    a_hi = a.astype(B16)
    wide[0:TT, :] = a_hi
    wide[TT:, :] = (a - a_hi.astype(F32)).astype(B16)
    tokens = dot(wide[...], table_ref[...], NN)
    tokens = tokens[0:TT] + tokens[TT:] + dot(a_hi, rest[...], NN)
    tok_ref[...] = tokens
    r = lax.rsqrt(jnp.mean(tokens * tokens, axis=1, keepdims=True) + EPS)
    norm_ref[...] = (tokens * r * gain_ref[...].astype(F32)).astype(B16)

def gbst_fwd(cid, raw, taps, scorer, gain):
    tiles = cid.shape[0]
    d = raw.shape[1]
    rows = tiles * TT
    const = lambda shape: pl.BlockSpec(shape, lambda i: (0,) * len(shape))
    return pl.pallas_call(
        gbst_fwd_body, grid=(tiles,), name="gbst_fwd",
        in_specs=[pl.BlockSpec((None, 8, TT), lambda i: (i, 0, 0)), const((CJ, d)), const((5, d)), const((1, d)), const((1, d))],
        out_specs=[pl.BlockSpec((TT, d), lambda i: (i, 0)), pl.BlockSpec((TT, d), lambda i: (i, 0)),
                   pl.BlockSpec((TT, 2 * TT), lambda i: (i, 0)), pl.BlockSpec((None, 8, TT), lambda i: (i, 0, 0)),
                   const((CC, d))],
        out_shape=[jax.ShapeDtypeStruct((rows, d), F32), jax.ShapeDtypeStruct((rows, d), B16),
                   jax.ShapeDtypeStruct((rows, 2 * TT), B16), jax.ShapeDtypeStruct((tiles, 8, TT), F32),
                   jax.ShapeDtypeStruct((CC, d), B16)],
        scratch_shapes=[pltpu.VMEM((CC, 2 * TT), B16), pltpu.VMEM((CC, d), B16), pltpu.VMEM((5, 16, CJ), B16),
                        pltpu.VMEM((2 * TT, 2 * TT), B16), pltpu.VMEM((2 * TT, CC), B16)],
        compiler_params=pltpu.CompilerParams(vmem_limit_bytes=56 << 20),
        cost_estimate=pl.CostEstimate(flops=rows * CC * d * 8, transcendentals=0, bytes_accessed=rows * d * 8),
    )(cid, raw, taps, scorer, gain)

def gbst_bwd_body(cid_ref, w_ref, mix_ref, tok_ref, hid_ref, nb_ref, gain_ref, table_ref, raw_ref, taps_ref, scorer_ref,
                  gt_ref, small_ref, oht, big, usum):
    i = pl.program_id(0)
    fill_onehot(cid_ref, oht)

    @pl.when(i == 0)
    def _():
        big[...] = jnp.zeros_like(big)
        usum[...] = jnp.zeros_like(usum)
        small_ref[...] = jnp.zeros_like(small_ref)
    x = tok_ref[...]
    n = nb_ref[...].astype(F32)
    r = lax.rsqrt(jnp.mean(x * x, axis=1, keepdims=True) + EPS)
    u = n * gain_ref[...].astype(F32)
    xr = x * r
    g = hid_ref[...].astype(F32) + r * (u - xr * jnp.mean(u * xr, axis=1, keepdims=True))
    small_ref[6:7, :] += jnp.sum(n * xr, axis=0, keepdims=True)
    gb = g.astype(B16)
    hh = dot(gb, table_ref[...], NT).astype(B16)
    gram = dot(hh, oht[...], NN)
    same, par, pair, tri_e, tri_o = masks()
    lanesum = lambda m: jnp.sum(jnp.where(m, gram, 0.0), axis=1, keepdims=True)
    me = 0.5 * lanesum(same & ~par)
    mo = 0.5 * lanesum(same & par)
    m2 = 0.5 * (me + mo)
    m4 = 0.125 * lanesum(pair)
    m3e = lanesum(tri_e) * (1.0 / 6.0)
    m3o = lanesum(tri_o) * (1.0 / 6.0)
    lane8 = lax.broadcasted_iota(jnp.int32, (TT, 128), 1)
    cols = jnp.zeros((TT, 128), F32)
    for k, v in enumerate((me, mo, m2, m2, m3e, m3o, m4, m4)):
        cols = jnp.where(lane8 == k, v, cols)
    dmix = cols.T[0:8, :]
    mix = mix_ref[...]
    row = lambda a, k: a[k : k + 1, :]
    sides = []
    for side in range(2):
        inner = sum(row(mix, 2 * b + side) * row(dmix, 2 * b + side) for b in range(4))
        sides.append([row(mix, 2 * b + side) * (row(dmix, 2 * b + side) - inner) for b in range(4)])
    dwe = jnp.zeros((1, TT), F32)
    dwo = jnp.zeros((1, TT), F32)
    for b in range(4):
        e, o = means_of(sides[0][b], sides[1][b])[b]
        dwe = dwe + e
        dwo = dwo + o
    dw = jnp.concatenate([dwe, dwo], axis=1)
    hi, mid, lo = split3(jnp.broadcast_to(dw, (16, 2 * TT)))
    which = lax.broadcasted_iota(jnp.int32, (16, 2 * TT), 0)
    dw3 = jnp.where(which == 0, hi, jnp.where(which == 1, mid, jnp.where(which == 2, lo, jnp.zeros_like(hi))))
    usum[...] += dot(dw3, oht[...], NT)
    at = dot(oht[...], w_ref[...], NT).astype(B16)
    big[...] += dot(at, gb, NN)

    @pl.when(i == pl.num_programs(0) - 1)
    def _():
        us = usum[...]
        urow = us[0:1] + us[1:2] + us[2:3]
        hi, mid, lo = split3(jnp.broadcast_to(urow, (16, CC)))
        which = lax.broadcasted_iota(jnp.int32, (16, CC), 0)
        u3 = jnp.where(which == 0, hi, jnp.where(which == 1, mid, jnp.where(which == 2, lo, jnp.zeros_like(hi))))
        gs = dot(u3, table_ref[...], NN)
        small_ref[5:6, :] = gs[0:1] + gs[1:2] + gs[2:3]
        ucol = jnp.broadcast_to(urow, (128, CC)).T[:, 0:1]
        total = jnp.zeros(gt_ref.shape, F32)
        for j in range(5):
            m = big[CJ * j : CJ * (j + 1), :] + ucol[CJ * j : CJ * (j + 1)] * scorer_ref[...].astype(F32)
            total = total + m * taps_ref[j : j + 1, :].astype(F32)
            small_ref[j : j + 1, :] = jnp.sum(m * raw_ref[...].astype(F32), axis=0, keepdims=True)
        gt_ref[...] = total

def gbst_bwd(cid, w, mix, tok, hid, nb, gain, table, raw, taps, scorer):
    tiles = cid.shape[0]
    d = table.shape[1]
    rows = tiles * TT
    const = lambda shape: pl.BlockSpec(shape, lambda i: (0,) * len(shape))
    tile = lambda width: pl.BlockSpec((TT, width), lambda i: (i, 0))
    return pl.pallas_call(
        gbst_bwd_body, grid=(tiles,), name="gbst_bwd",
        in_specs=[pl.BlockSpec((None, 8, TT), lambda i: (i, 0, 0)), tile(2 * TT), pl.BlockSpec((None, 8, TT), lambda i: (i, 0, 0)),
                  tile(d), tile(d), tile(d), const((1, d)), const((CC, d)), const((CJ, d)), const((5, d)), const((1, d))],
        out_specs=[const((CJ, d)), const((8, d))],
        out_shape=[jax.ShapeDtypeStruct((CJ, d), F32), jax.ShapeDtypeStruct((8, d), F32)],
        scratch_shapes=[pltpu.VMEM((CC, 2 * TT), B16), pltpu.VMEM((CC, d), F32), pltpu.VMEM((16, CC), F32)],
        compiler_params=pltpu.CompilerParams(vmem_limit_bytes=56 << 20),
        cost_estimate=pl.CostEstimate(flops=rows * CC * d * 8, transcendentals=0, bytes_accessed=rows * d * 12),
    )(cid, w, mix, tok, hid, nb, gain, table, raw, taps, scorer)


FC = 512
RT = 288


def middle_body(tok_ref, ao_ref, ar_ref, woo_ref, wor_ref, wgo_ref, wgr_ref, wuo_ref, wur_ref, wdo_ref, wdr_ref,
                og_ref, gain_ref,
                layer_ref, back_ref, down_ref, dsend_ref, goo_ref, gor_ref, ggo_ref, guo_ref, gdo_ref, ggr_ref, gur_ref, gdr_ref,
                gain_out,
                hid, n2, n2t, ogt, outs, n2b, wg, wu, wd, inner_s, gb_s, ub_s):
    i = pl.program_id(0)
    steps = pl.num_programs(0)
    rows = tok_ref.shape[0]
    tiles = [slice(r, r + RT) for r in range(0, rows, RT)]
    gain = gain_ref[...].astype(F32)

    @pl.when(i == 0)
    def _():
        for at in tiles:
            h = tok_ref[at, :] + dot(ao_ref[at, :], woo_ref[...], NN) + dot(ar_ref[at, :], wor_ref[...], NN)
            hid[at, :] = h
            r = lax.rsqrt(jnp.mean(h * h, axis=1, keepdims=True) + EPS)
            n2[at, :] = (h * r * gain).astype(B16)
            outs[at, :] = h
            n2b[at, :] = jnp.zeros((RT, h.shape[1]), F32)
        n2t[...] = n2[...].T
        ogt[...] = og_ref[...].T

    @pl.when(i < steps // 2)
    def _():
        wg[...] = wgo_ref[...]
        wu[...] = wuo_ref[...]
        wd[...] = wdo_ref[...]

    @pl.when(i >= steps // 2)
    def _():
        wg[...] = wgr_ref[...]
        wu[...] = wur_ref[...]
        wd[...] = wdr_ref[...]

    for at in tiles:
        x = n2[at, :]
        gate = dot(x, wg[...], NN)
        up = dot(x, wu[...], NN)
        gi = dot(og_ref[at, :], wd[...], NT)
        act, slope = gelu_parts(gate)
        inner = (act * up).astype(B16)
        gb = (gi * up * slope).astype(B16)
        ub = (gi * act).astype(B16)
        inner_s[at, :] = inner
        gb_s[at, :] = gb
        ub_s[at, :] = ub
        outs[at, :] += dot(inner, wd[...], NN)
        n2b[at, :] += dot(gb, wg[...], NT) + dot(ub, wu[...], NT)
    pieces = [dot(n2t[...], gb_s[...], NN), dot(n2t[...], ub_s[...], NN), dot(ogt[...], inner_s[...], NN)]
    pieces = [x.astype(B16) for x in pieces]

    @pl.when(i < steps // 2)
    def _():
        for ref, x in zip((ggo_ref, guo_ref, gdo_ref), pieces):
            ref[...] = x

    @pl.when(i >= steps // 2)
    def _():
        for ref, x in zip((ggr_ref, gur_ref, gdr_ref), pieces):
            ref[...] = x

    @pl.when(i == steps - 1)
    def _():
        total = jnp.zeros(gain.shape, F32)
        for at in tiles:
            h = hid[at, :]
            layer_ref[at, :] = outs[at, :].astype(B16)
            r = lax.rsqrt(jnp.mean(h * h, axis=1, keepdims=True) + EPS)
            back = n2b[at, :]
            u = back * gain
            hr = h * r
            total = total + jnp.sum(back * hr, axis=0, keepdims=True)
            hb = og_ref[at, :].astype(F32) + r * (u - hr * jnp.mean(u * hr, axis=1, keepdims=True))
            back_ref[at, :] = hb
            low = hb.astype(B16)
            n2[at, :] = low
            down_ref[at, :] = dot(low, woo_ref[...], NT).astype(B16)
            dsend_ref[at, :] = dot(low, wor_ref[...], NT).astype(B16)
        gain_out[...] = total
        n2t[...] = n2[...].T
        goo_ref[...] = dot(n2t[...], ao_ref[...], NN).astype(B16)
        gor_ref[...] = dot(n2t[...], ar_ref[...], NN).astype(B16)


def middle(tok, att_own, att_recv, wo, wo_other, wg, wg_other, wu, wu_other, wd, wd_other, og, gain):
    rows, d = tok.shape
    proj = att_own.shape[1]
    ffn = wg.shape[1]
    half = ffn // FC
    const = lambda *shape: pl.BlockSpec(shape, lambda i: (0,) * len(shape))
    once = lambda *shape: pl.BlockSpec(shape, lambda i: (0,) * len(shape), pipeline_mode=pl.Buffered(1))
    low = lambda i: jnp.minimum(i, half - 1)
    high = lambda i: jnp.maximum(i - half, 0)
    wide = lambda f: pl.BlockSpec((d, FC), lambda i: (0, f(i)))
    tall = lambda f: pl.BlockSpec((FC, d), lambda i: (f(i), 0))
    sds = jax.ShapeDtypeStruct
    flops = 2 * rows * d * (8 * 2 * ffn + 6 * proj) * 9 // 8
    return pl.pallas_call(
        middle_body, grid=(2 * half,), name="middle",
        in_specs=[once(rows, d), once(rows, proj), once(rows, proj), once(proj, d), once(proj, d),
                  wide(low), wide(high), wide(low), wide(high), tall(low), tall(high), once(rows, d), const(1, d)],
        out_specs=[once(rows, d), once(rows, d), once(rows, proj), once(rows, proj), once(d, proj), once(d, proj),
                   wide(low), wide(low), wide(low), wide(high), wide(high), wide(high), const(1, d)],
        out_shape=[sds((rows, d), B16), sds((rows, d), F32), sds((rows, proj), B16), sds((rows, proj), B16),
                   sds((d, proj), B16), sds((d, proj), B16)] + [sds((d, ffn), B16)] * 6 + [sds((1, d), F32)],
        scratch_shapes=[
            pltpu.VMEM((rows, d), F32), pltpu.VMEM((rows, d), B16), pltpu.VMEM((d, rows), B16), pltpu.VMEM((d, rows), B16),
            pltpu.VMEM((rows, d), F32), pltpu.VMEM((rows, d), F32),
            pltpu.VMEM((d, FC), B16), pltpu.VMEM((d, FC), B16), pltpu.VMEM((FC, d), B16),
            pltpu.VMEM((rows, FC), B16), pltpu.VMEM((rows, FC), B16), pltpu.VMEM((rows, FC), B16),
        ],
        compiler_params=pltpu.CompilerParams(vmem_limit_bytes=61 << 20, dimension_semantics=("arbitrary",)),
        cost_estimate=pl.CostEstimate(flops=flops, transcendentals=rows * 2 * ffn, bytes_accessed=rows * d * 20 + 24 * d * ffn),
    )(tok, att_own, att_recv, wo, wo_other, wg, wg_other, wu, wu_other, wd, wd_other, og, gain)


def swapped(tree):
    return jax.tree.map(lambda a: lax.ppermute(a, "mp", [(0, 1), (1, 0)]), tree)


def matmul(a, b):
    return dot(a, b, NN)


def grad_of(a, b):
    return lax.dot_general(a, b, (((0,), (0,)), ((), ())), preferred_element_type=F32)


X_SWAP = ("dp", 0)
Y_SWAP = ("dp", 1)
Z_NEAR = ("seq", 0)
Z_FAR = ("seq", 1)


def hop(x, axis, bit):
    count = lax.axis_size(axis)
    return lax.ppermute(x, axis, [(i, i ^ (1 << bit)) for i in range(count)])


def side_of(axis, bit):
    return (lax.axis_index(axis) >> bit) & 1


def give(x, axis, bit):
    side = side_of(axis, bit)
    rows = x.shape[0] // 2
    keep = lax.dynamic_slice_in_dim(x, side * rows, rows, 0)
    send = lax.dynamic_slice_in_dim(x, (1 - side) * rows, rows, 0)
    return keep.astype(F32) + hop(send.astype(B16), axis, bit).astype(F32)


def take(x, axis, bit):
    first = side_of(axis, bit) == 0
    other = hop(x, axis, bit)
    return jnp.concatenate([jnp.where(first, x, other), jnp.where(first, other, x)], axis=0)


def two_ways(x, step, ways):
    cut = x.shape[1] // 2
    return [step(x[:, :cut], *ways[0]), step(x[:, cut:], *ways[1])]


def after(value, *others):
    return lax.optimization_barrier((value,) + others)[0]


def gelu_parts(gate):
    c = 0.7978845608028654
    inside = c * (gate + 0.044715 * gate * gate * gate)
    th = jnp.tanh(inside)
    value = 0.5 * gate * (1.0 + th)
    slope = 0.5 * (1.0 + th) + 0.5 * gate * (1.0 - th * th) * (c * (1.0 + 3.0 * 0.044715 * gate * gate))
    return value, slope


def local_item(
    byte_ids, true_lengths, byte_table, conv_taps, block_scorer, attn_gain, w_query, w_key, w_value,
    w_output, rel_table, ffn_gain, w_gate, w_up, w_down, out_grad,
):
    seq_count = lax.axis_size("seq")
    place = lax.axis_index("seq")
    core = lax.axis_index("mp")
    tok_rows = out_grad.shape[0]
    half = tok_rows // 2
    width = out_grad.shape[2]
    own_rows = seq_count * half
    total = 2 * own_rows
    proj = w_query.shape[1]
    first = core == 0

    def halves(full):
        parts = full.reshape(seq_count, 2, half, full.shape[1])
        own = jnp.where(first, parts[:, 0], parts[:, 1]).reshape(own_rows, -1)
        other = jnp.where(first, parts[:, 1], parts[:, 0]).reshape(own_rows, -1)
        return own, other

    def whole(own, other):
        shape = (seq_count, half, own.shape[1])
        low, high = jnp.where(first, own, other), jnp.where(first, other, own)
        return jnp.stack([low.reshape(shape), high.reshape(shape)], axis=1).reshape(total, -1)

    byte_rows = byte_ids.shape[0]
    here = place * byte_rows + jnp.arange(byte_rows, dtype=jnp.int32)
    shown = jnp.where(here[:, None] < true_lengths[None, :], byte_ids, -1)
    shown = shown.reshape(tok_rows, 2, seq_count).transpose(2, 1, 0)
    shown = lax.all_to_all(shown, "seq", split_axis=0, concat_axis=0, tiled=True)
    length = lax.dynamic_index_in_dim(true_lengths, place, 0, keepdims=False)
    wo_other, wg_other, wu_other, wd_other = swapped((w_output, w_gate, w_up, w_down))
    grad_rows = lax.dynamic_slice_in_dim(out_grad, core * half, half, 0)
    grad_own = lax.all_to_all(grad_rows, "seq", split_axis=1, concat_axis=0, tiled=True)
    grad_own = grad_own.reshape(own_rows, width)

    tiles = own_rows // TT
    pairs = jnp.pad(shown.transpose(1, 0, 2).reshape(2, total), ((0, 0), (1, 1)), constant_values=-1)
    rows = jnp.concatenate([pairs[:, j : j + total] for j in range(3)], axis=0).reshape(6, seq_count, 2, half)
    rows = jnp.where(first, rows[:, :, 0], rows[:, :, 1]).reshape(6, tiles, TT).transpose(1, 0, 2)
    cid = jnp.pad(rows, ((0, 0), (0, 2), (0, 0)), constant_values=-1)

    vocab = byte_table.shape[0]
    raw = jnp.pad(byte_table, ((0, CJ - vocab), (0, 0)))
    scorer, gain_one, gain_two = block_scorer[None], attn_gain[None], ffn_gain[None]
    tokens, normed, pool_w, mix, table_cat = gbst_fwd(cid, raw, conv_taps, scorer, gain_one)
    normed_all = whole(normed, swapped(normed))
    w_qkv = jnp.concatenate([w_query, w_key, w_value], axis=1)
    qkv = matmul(normed_all, w_qkv).astype(B16)
    limit = ((length + 1) // 2).reshape(1)
    weights, att, att_t, inv = attn_fwd(limit, qkv, bias_curve(rel_table, proj // DH))
    att_own, att_send = halves(att)
    att_recv = swapped(att_send)
    (layer, hidden_back, d_own, d_send, out_own, out_other, gate_own, up_own, down_own,
     gate_other, up_other, down_other, g_gain_two) = middle(
        tokens, att_own, att_recv, w_output, wo_other, w_gate, wg_other, w_up, wu_other, w_down, wd_other,
        grad_own, gain_two
    )
    d_att = whole(d_own, swapped(d_send))

    ffn_width = w_gate.shape[1]
    add = lambda a, b: (a.astype(F32) + b.astype(F32)).astype(B16)
    own_cols = (gate_own, up_own, down_own, out_own)
    other_cols = swapped((gate_other, up_other, down_other, out_other))
    large = jnp.concatenate([add(a, b) for a, b in zip(own_cols, other_cols)], axis=1)
    large = lax.psum_scatter(large, "dp", scatter_dimension=0, tiled=True)

    dk, dv, dq, near, far = attn_bwd(weights, qkv, d_att, att_t, inv)
    d_all = jnp.concatenate([dq, dk, dv], axis=0)
    partial = lax.dot_general(d_all, w_qkv, (((0,), (1,)), ((), ())), preferred_element_type=F32)
    part_own, part_send = halves(partial.astype(B16))
    part_recv = swapped(part_send)
    g_qkv = lax.dot_general(normed_all, d_all, (((0,), (1,)), ((), ())), preferred_element_type=F32)
    normed_back = (part_own.astype(F32) + part_recv.astype(F32)).astype(B16)
    large = lax.psum_scatter(after(large, d_all), "seq", scatter_dimension=0, tiled=True)
    normed_back = after(normed_back, g_qkv, large)
    large = lax.all_gather(large, "seq", axis=0, tiled=True)
    left, right = two_ways(g_qkv, give, (X_SWAP, Y_SWAP))
    g_rel = rel_grad(near, far, near.shape[2])
    g_table, small = gbst_bwd(
        cid, pool_w, mix, tokens, hidden_back, normed_back, gain_one, table_cat, raw, conv_taps, scorer
    )
    large = lax.all_gather(after(large, g_table), "dp", axis=0, tiled=True)
    rel_row = jnp.pad(g_rel.reshape(1, -1), ((0, 0), (0, width - g_rel.size)))
    blank = jnp.zeros_like(rel_row)
    rel_rows = [jnp.where(first, rel_row, blank), jnp.where(first, blank, rel_row)]
    tail = jnp.concatenate([g_table, small[:7], g_gain_two] + rel_rows + [jnp.zeros((6, width), F32)], axis=0)
    left, right, tail = lax.optimization_barrier((left, right, tail))
    tail = give(tail, "mp", 0)
    left = give(left, *Y_SWAP)
    right = give(right, *X_SWAP)
    tail = give(tail, *X_SWAP)
    both = give(jnp.concatenate([left, right], axis=1), *Z_NEAR)
    tail = give(tail, *Y_SWAP)
    both = give(both, *Z_FAR).astype(B16)
    tail = tail + hop(tail.astype(B16), *Z_NEAR).astype(F32)
    both = take(both, *Z_FAR)
    tail = (tail + hop(tail.astype(B16), *Z_FAR).astype(F32)).astype(B16)
    both = take(both, *Z_NEAR)
    cut = both.shape[1] // 2
    left, right = take(both[:, :cut], *Y_SWAP), take(both[:, cut:], *X_SWAP)
    tail = take(tail, *Y_SWAP)
    left, right = take(left, *X_SWAP), take(right, *Y_SWAP)
    tail = take(tail, *X_SWAP)
    tail = take(tail, "mp", 0).astype(F32)
    large = large.astype(F32)
    big = [large[:, :ffn_width], large[:, ffn_width : 2 * ffn_width], large[:, 2 * ffn_width : 3 * ffn_width].T]
    g_out = large[:, 3 * ffn_width :].T
    g_qkv = jnp.concatenate([left, right], axis=1).astype(F32)
    g_query, g_key, g_value = (g_qkv[:, i * proj : (i + 1) * proj] for i in range(3))
    g_table, small, g_gain_two = tail[:CJ], tail[CJ : CJ + 7], tail[CJ + 7]
    g_rel = jnp.where(first, tail[CJ + 8], tail[CJ + 9])[: g_rel.size].reshape(g_rel.shape)

    sent = layer.reshape(seq_count, half, width)
    layer_out = lax.all_to_all(sent[:, :, None], "seq", split_axis=0, concat_axis=2, tiled=True)
    layer_out = layer_out.reshape(half, seq_count, width).astype(F32)
    return (
        layer_out, g_table[:vocab], small[:5], small[5], small[6], g_query, g_key, g_value, g_out, g_rel,
        g_gain_two, big[0], big[1], big[2],
    )


def chosen(*args):
    ids, lengths, w_query, out_grad = args[0], args[1], args[6], args[15]
    seq_count = lax.axis_size("seq")
    total = out_grad.shape[0] * seq_count
    fits = (
        lengths.shape[0] == seq_count
        and lax.axis_size("mp") == 2
        and lax.axis_size("dp") == 4
        and seq_count == 4
        and total % (2 * TT) == 0
        and total % CK == 0
        and total % (CK * SUB) == 0
        and w_query.shape[1] % 128 == 0
        and args[12].shape[1] % FC == 0
        and (total // 2) % RT == 0
        and (ids.shape[0] // 2) % 12 == 0
    )
    return local_item(*args) if fits else local_general(*args)


def solution(mesh):
    return jax.shard_map(
        chosen,
        mesh=mesh,
        in_specs=(
            P("seq", "dp"),
            P("dp"),
            P(),
            P(),
            P(),
            P(),
            P(None, "mp"),
            P(None, "mp"),
            P(None, "mp"),
            P("mp", None),
            P(None, "mp"),
            P(),
            P(None, "mp"),
            P(None, "mp"),
            P("mp", None),
            P("seq", "dp", None),
        ),
        out_specs=(
            P(("seq", "mp"), "dp", None),
            P(),
            P(),
            P(),
            P(),
            P(None, "mp"),
            P(None, "mp"),
            P(None, "mp"),
            P("mp", None),
            P(None, "mp"),
            P(),
            P(None, "mp"),
            P(None, "mp"),
            P("mp", None),
        ),
        check_vma=False,
    )
```

```python
import functools

import jax
import jax.numpy as jnp
from jax import lax
from jax.experimental import pallas as pl
from jax.experimental.pallas import tpu as pltpu
from jax.sharding import PartitionSpec as P

DH = 64
BUCKETS = 32
MICRO = 4


EPS = 1e-06
NEG = -1000000000.0
EDGES = (12, 16, 23, 32, 46, 64, 91)
HIGH = lax.Precision.HIGHEST
F32 = jnp.float32
B16 = jnp.bfloat16


def extended(cells, sides, width):
    for axis, dim in sides:
        count = lax.axis_size(axis)
        ends = count - 1
        head = lax.slice_in_dim(cells, 0, width, axis=dim)
        tail = lax.slice_in_dim(cells, cells.shape[dim] - width, cells.shape[dim], axis=dim)
        cells = jnp.concatenate(
            [
                lax.ppermute(tail, axis, [(i, (i + 1) % count) for i in range(ends)]),
                cells,
                lax.ppermute(head, axis, [((i + 1) % count, i) for i in range(ends)]),
            ],
            axis=dim,
        )
    return cells


def for_sending(array):
    return jax.tree.map(lambda a: a.astype(jnp.bfloat16) if a.dtype == jnp.float32 else a, array)


def bucket_of(offset):
    distance = jnp.abs(offset)
    far = jnp.full(offset.shape, 8, jnp.int32)
    for edge in EDGES:
        far = far + (distance >= edge).astype(jnp.int32)
    near = jnp.where(distance < 8, distance, far)
    return near + 16 * (offset > 0).astype(jnp.int32)


def bias_onehot(query_places, key_places):
    offset = key_places[None, :] - query_places[:, None]
    return (bucket_of(offset)[:, :, None] == jnp.arange(BUCKETS, dtype=jnp.int32)).astype(F32)


def rms_norm(hidden, gain):
    return hidden * lax.rsqrt(jnp.mean(hidden * hidden, axis=-1, keepdims=True) + EPS) * gain


def activation(gate, up):
    return jax.nn.gelu(gate, approximate=True) * up


def gbst_tail(conv_out, scorer):
    byte_count, item_count, model_width = conv_out.shape
    weighted = jnp.einsum("pid,d->pi", conv_out, scorer, precision=HIGH)
    pooled_all = []
    scores_all = []
    for block_size in (1, 2, 3, 4):
        block_means = conv_out.reshape(
            byte_count // block_size, block_size, item_count, model_width
        ).mean(axis=1)
        pooled_all.append(jnp.repeat(block_means, block_size, axis=0))
        score_means = weighted.reshape(byte_count // block_size, block_size, item_count).mean(
            axis=1
        )
        scores_all.append(jnp.repeat(score_means, block_size, axis=0))
    mixing = jax.nn.softmax(jnp.stack(scores_all), axis=0)
    mixture = mixing[0][:, :, None] * pooled_all[0]
    for block_index in range(1, 4):
        mixture = mixture + mixing[block_index][:, :, None] * pooled_all[block_index]
    return mixture.reshape(byte_count // 2, 2, item_count, model_width).mean(axis=1)


def local_general(
    byte_ids,
    true_lengths,
    byte_table,
    conv_taps,
    block_scorer,
    attn_gain,
    w_query,
    w_key,
    w_value,
    w_output,
    rel_table,
    ffn_gain,
    w_gate,
    w_up,
    w_down,
    out_grad,
):
    seq_count = lax.axis_size("seq")
    seq_place = lax.axis_index("seq")
    core_place = lax.axis_index("mp")
    byte_rows = byte_ids.shape[0]
    tok_rows = byte_rows // 2
    half_rows = tok_rows // lax.axis_size("mp")
    total_tokens = tok_rows * seq_count
    item_count = byte_ids.shape[1] // MICRO
    proj_width = w_query.shape[1]
    head_count = proj_width // DH
    ffn_width = w_gate.shape[1]
    taps = conv_taps.astype(F32)
    scorer = block_scorer.astype(F32)
    gain_one = attn_gain.astype(F32)
    gain_two = ffn_gain.astype(F32)
    rel_local = rel_table.astype(F32)
    gate_up = jnp.concatenate([w_gate, w_up], axis=1)
    query_places = seq_place * tok_rows + jnp.arange(tok_rows, dtype=jnp.int32)
    key_places = jnp.arange(total_tokens, dtype=jnp.int32)
    onehot_bias = bias_onehot(query_places, key_places)
    bias = jnp.einsum("qkb,bh->hqk", onehot_bias, rel_local, precision=HIGH)
    byte_places = seq_place * byte_rows + jnp.arange(byte_rows, dtype=jnp.int32)
    vocab_range = jnp.arange(byte_table.shape[0], dtype=jnp.int32)
    sum_table = jnp.zeros(byte_table.shape, F32)
    sum_taps = jnp.zeros(conv_taps.shape, F32)
    sum_scorer = jnp.zeros(block_scorer.shape, F32)
    sum_gain_one = jnp.zeros(attn_gain.shape, F32)
    sum_query = jnp.zeros(w_query.shape, F32)
    sum_key = jnp.zeros(w_key.shape, F32)
    sum_value = jnp.zeros(w_value.shape, F32)
    sum_output = jnp.zeros(w_output.shape, F32)
    sum_rel = jnp.zeros(rel_table.shape, F32)
    sum_gain_two = jnp.zeros(ffn_gain.shape, F32)
    sum_gate = jnp.zeros(w_gate.shape, F32)
    sum_up = jnp.zeros(w_up.shape, F32)
    sum_down = jnp.zeros(w_down.shape, F32)
    outputs = []
    for micro in range(MICRO):
        first = micro * item_count
        ids_now = byte_ids[:, first : first + item_count]
        lengths = true_lengths[first : first + item_count]
        keep = (byte_places[:, None] < lengths[None, :]).astype(F32)
        onehot = (ids_now[:, :, None] == vocab_range).astype(F32) * keep[:, :, None]
        embedded = jnp.einsum(
            "piv,vd->pid", onehot.astype(B16), byte_table, preferred_element_type=F32
        ).astype(B16)
        framed = extended(embedded, (("seq", 0),), 2)
        conv_out = taps[0] * framed[0:byte_rows]
        for tap_index in range(1, 5):
            conv_out = conv_out + taps[tap_index] * framed[tap_index : tap_index + byte_rows]
        tokens, gbst_pull = jax.vjp(gbst_tail, conv_out, scorer)
        normed, norm_pull = jax.vjp(rms_norm, tokens, gain_one)
        normed_low = normed.astype(B16)
        query = jnp.einsum("qid,dh->qih", normed_low, w_query, preferred_element_type=F32).astype(
            B16
        )
        keys_here = jnp.einsum("qid,dh->qih", normed_low, w_key, preferred_element_type=F32).astype(
            B16
        )
        values_here = jnp.einsum(
            "qid,dh->qih", normed_low, w_value, preferred_element_type=F32
        ).astype(B16)
        keys_all, values_all = (
            lax.all_gather(keys_here, "seq", axis=0, tiled=True),
            lax.all_gather(values_here, "seq", axis=0, tiled=True),
        )
        query4 = query.reshape(tok_rows, item_count, head_count, DH)
        keys4 = keys_all.reshape(total_tokens, item_count, head_count, DH)
        values4 = values_all.reshape(total_tokens, item_count, head_count, DH)
        key_ok = 2 * key_places[None, :] < lengths[:, None]

        def scores_of():
            raw = jnp.einsum("qihe,kihe->ihqk", query4, keys4, preferred_element_type=F32)
            return jnp.where(key_ok[:, None, None, :], raw + bias[None], NEG)

        scores = scores_of()
        top = jnp.max(scores, axis=-1, keepdims=True)
        log_total = top + jnp.log(jnp.sum(jnp.exp(scores - top), axis=-1, keepdims=True))
        probs_low = jnp.exp(scores - log_total).astype(B16)
        attended = (
            jnp.einsum("ihqk,kihe->qihe", probs_low, values4, preferred_element_type=F32)
            .reshape(tok_rows, item_count, proj_width)
            .astype(B16)
        )
        attn_half = lax.psum_scatter(
            jnp.einsum("qih,hd->qid", attended, w_output, preferred_element_type=F32),
            "mp",
            scatter_dimension=0,
            tiled=True,
        )
        tokens_half = lax.dynamic_slice_in_dim(tokens, core_place * half_rows, half_rows, 0)
        hidden_half = tokens_half + attn_half
        normed_two, norm_two_pull = jax.vjp(rms_norm, hidden_half, gain_two)
        normed_full = lax.all_gather(normed_two.astype(B16), "mp", axis=0, tiled=True)
        projected = jnp.einsum("qid,df->qif", normed_full, gate_up, preferred_element_type=F32)
        inner, inner_pull = jax.vjp(
            activation, projected[..., :ffn_width], projected[..., ffn_width:]
        )
        inner_low = inner.astype(B16)
        ffn_half = lax.psum_scatter(
            jnp.einsum("qif,fd->qid", inner_low, w_down, preferred_element_type=F32).astype(
                jnp.bfloat16
            ),
            "mp",
            scatter_dimension=0,
            tiled=True,
        ).astype(jnp.float32)
        outputs.append(hidden_half + ffn_half)
        grad_low = out_grad[:, first : first + item_count]
        grad_half = lax.dynamic_slice_in_dim(grad_low, core_place * half_rows, half_rows, 0).astype(
            F32
        )
        sum_down = sum_down + jnp.einsum(
            "qif,qid->fd", inner_low, grad_low, preferred_element_type=F32
        )
        grad_inner = jnp.einsum("qid,fd->qif", grad_low, w_down, preferred_element_type=F32)
        gate_grad, up_grad = inner_pull(grad_inner)
        gate_low = gate_grad.astype(B16)
        up_low = up_grad.astype(B16)
        sum_gate = sum_gate + jnp.einsum(
            "qid,qif->df", normed_full, gate_low, preferred_element_type=F32
        )
        sum_up = sum_up + jnp.einsum("qid,qif->df", normed_full, up_low, preferred_element_type=F32)
        normed_two_grad = lax.psum_scatter(
            jnp.einsum("qif,df->qid", gate_low, w_gate, preferred_element_type=F32)
            + jnp.einsum("qif,df->qid", up_low, w_up, preferred_element_type=F32),
            "mp",
            scatter_dimension=0,
            tiled=True,
        )
        hidden_norm_grad, gain_two_grad = norm_two_pull(normed_two_grad)
        hidden_grad = grad_half + hidden_norm_grad
        hidden_full = lax.all_gather(for_sending(hidden_grad), "mp", axis=0, tiled=True).astype(
            hidden_grad.dtype
        )
        hidden_low = hidden_full.astype(B16)
        sum_output = sum_output + jnp.einsum(
            "qih,qid->hd", attended, hidden_low, preferred_element_type=F32
        )
        attended_grad = jnp.einsum(
            "qid,hd->qih", hidden_low, w_output, preferred_element_type=F32
        ).astype(B16)
        attended_grad4 = attended_grad.reshape(tok_rows, item_count, head_count, DH)
        scores = scores_of()
        probs = jnp.exp(scores - log_total)
        probs_low = probs.astype(B16)
        probs_grad = jnp.einsum(
            "qihe,kihe->ihqk", attended_grad4, values4, preferred_element_type=F32
        )
        inner_sum = jnp.sum(probs * probs_grad, axis=-1, keepdims=True)
        scores_grad = probs * (probs_grad - inner_sum)
        sum_rel = sum_rel + jnp.einsum(
            "qkb,hqk->bh", onehot_bias, jnp.sum(scores_grad, axis=0), precision=HIGH
        )
        scores_low = scores_grad.astype(B16)
        query_grad = (
            jnp.einsum("ihqk,kihe->qihe", scores_low, keys4, preferred_element_type=F32)
            .reshape(tok_rows, item_count, proj_width)
            .astype(B16)
        )
        key_part = jnp.einsum("ihqk,qihe->kihe", scores_low, query4, preferred_element_type=F32)
        value_part = jnp.einsum(
            "ihqk,qihe->kihe", probs_low, attended_grad4, preferred_element_type=F32
        )
        key_sums = lax.psum_scatter(
            jnp.concatenate(
                [
                    key_part.reshape(tok_rows * lax.axis_size("seq"), item_count, proj_width),
                    value_part.reshape(tok_rows * lax.axis_size("seq"), item_count, proj_width),
                ],
                axis=2,
            ).astype(jnp.bfloat16),
            "seq",
            scatter_dimension=0,
            tiled=True,
        ).astype(jnp.float32)
        keys_grad = key_sums[..., :proj_width].astype(B16)
        values_grad = key_sums[..., proj_width:].astype(B16)
        sum_query = sum_query + jnp.einsum(
            "qid,qih->dh", normed_low, query_grad, preferred_element_type=F32
        )
        sum_key = sum_key + jnp.einsum(
            "qid,qih->dh", normed_low, keys_grad, preferred_element_type=F32
        )
        sum_value = sum_value + jnp.einsum(
            "qid,qih->dh", normed_low, values_grad, preferred_element_type=F32
        )
        partial_grad = (
            jnp.einsum("qih,dh->qid", query_grad, w_query, preferred_element_type=F32)
            + jnp.einsum("qih,dh->qid", keys_grad, w_key, preferred_element_type=F32)
            + jnp.einsum("qih,dh->qid", values_grad, w_value, preferred_element_type=F32)
        )
        normed_grad, gain_two_total = (
            lax.psum(partial_grad.astype(jnp.bfloat16), "mp").astype(jnp.float32),
            lax.psum(gain_two_grad.astype(jnp.bfloat16), "mp").astype(jnp.float32),
        )
        sum_gain_two = sum_gain_two + gain_two_total
        tokens_norm_grad, gain_one_grad = norm_pull(normed_grad)
        sum_gain_one = sum_gain_one + gain_one_grad
        tokens_grad = hidden_full + tokens_norm_grad
        conv_grad, scorer_grad = gbst_pull(tokens_grad)
        sum_scorer = sum_scorer + scorer_grad
        framed_grad = extended(conv_grad.astype(jnp.bfloat16), (("seq", 0),), 2).astype(
            conv_grad.dtype
        )
        embedded_grad = taps[0] * framed_grad[4 : 4 + byte_rows]
        for tap_index in range(1, 5):
            embedded_grad = (
                embedded_grad
                + taps[tap_index] * framed_grad[4 - tap_index : 4 - tap_index + byte_rows]
            )
        tap_sums = [
            jnp.sum(conv_grad * framed[tap_index : tap_index + byte_rows], axis=(0, 1))
            for tap_index in range(5)
        ]
        sum_taps = sum_taps + jnp.stack(tap_sums)
        sum_table = sum_table + jnp.einsum("piv,pid->vd", onehot, embedded_grad, precision=HIGH)
    totals = lax.psum(
        (
            sum_table,
            sum_taps,
            sum_scorer,
            sum_gain_one,
            sum_query,
            sum_key,
            sum_value,
            sum_output,
            sum_rel,
            sum_gain_two,
            sum_gate,
            sum_up,
            sum_down,
        ),
        ("dp", "seq"),
    )
    layer_out = jnp.concatenate(outputs, axis=1)
    return (
        layer_out,
        totals[0],
        totals[1],
        totals[2],
        totals[3],
        totals[4],
        totals[5],
        totals[6],
        totals[7],
        totals[8],
        totals[9],
        totals[10],
        totals[11],
        totals[12],
    )


LOG2E = 1.4426950408889634
LN2 = 0.6931471805599453
NT = (((1,), (1,)), ((), ()))
NN = (((1,), (0,)), ((), ()))
CK = 256
SUB = 3

def dot(a, b, dims):
    return lax.dot_general(a, b, dims, preferred_element_type=F32)

def split3(x):
    hi = x.astype(B16)
    rest = x - hi.astype(F32)
    mid = rest.astype(B16)
    lo = (rest - mid.astype(F32)).astype(B16)
    return hi, mid, lo

def split3_xla(x):
    cut = lambda a: lax.reduce_precision(a, exponent_bits=8, mantissa_bits=7)
    hi = cut(x)
    mid = cut(x - hi)
    return hi.astype(B16), mid.astype(B16), (x - hi - mid).astype(B16)


def attn_fwd_body(limit_ref, q_ref, k_ref, v_ref, curve_ref, e_ref, o_ref, ot_ref, inv_ref,
                  kext, vext, table, qext, norms):
    total = k_ref.shape[0]
    tq = CK
    chunks = total // CK
    step = pl.program_id(1)

    @pl.when(step == 0)
    def _():
        lane = lax.broadcasted_iota(jnp.int32, (total, 128), 1)
        place = lax.broadcasted_iota(jnp.int32, (total, 128), 0)
        masked = jnp.where(place < limit_ref[0], 0.0, -1e9).astype(F32)
        k = k_ref[...].astype(F32)
        q = q_ref[...].astype(F32)
        pick = lax.broadcasted_iota(jnp.int32, (128, 128), 0) // 64 == lax.broadcasted_iota(jnp.int32, (128, 128), 1)
        pick = jnp.where(pick, 1.0, 0.0).astype(B16)
        size_q = jnp.max(dot((q * q).astype(B16), pick, NN), axis=0, keepdims=True)
        size_k = jnp.max(dot((k * k).astype(B16), pick, NN), axis=0, keepdims=True)
        both = size_q * size_k
        vt = v_ref[...].T
        for h in range(2):
            norms[h] = jnp.max(both[:, h : h + 1])
            own = (lane < 64) if h == 0 else (lane >= 64)
            base = 64 if h == 0 else 0
            extra = jnp.where(lane == base, masked, jnp.where((lane > base) & (lane < base + 4), 1.0, 0.0))
            kext[h] = jnp.where(own, k, extra).astype(B16)
            vext[h, 0:64, :] = vt[64 * h : 64 * h + 64, :]
            vext[h, 64:80, :] = jnp.ones((16, total), B16)
            curve = curve_ref[h : h + 1, :]
            for g in range(5):
                lo = 1024 + 2 * CK - g * CK - 256
                if g in (0, 4):
                    table[h, g * CK : (g + 1) * CK, :] = jnp.broadcast_to(curve[:, lo : lo + 1], (CK, CK))
                else:
                    window = jnp.broadcast_to(curve[:, lo : lo + 512], (CK, 512))
                    rolled = pltpu.roll(window, 0, 1, stride=1, stride_axis=0)
                    table[h, g * CK : (g + 1) * CK, :] = rolled[:, 256:512]

    lane_q = lax.broadcasted_iota(jnp.int32, (tq, 128), 1)

    def scores(h, u, c):
        d = jnp.clip(c - (step * SUB + u), -2, 2) + 2
        k_now = kext[h, pl.ds(c * CK if isinstance(c, int) else pl.multiple_of(c * CK, CK), CK), :]
        return dot(k_now, qext[u, h], NT) * LOG2E + table[h, pl.ds(pl.multiple_of(d * CK, CK), CK), :]

    for u in range(SUB):
        q = q_ref[pl.ds(pl.multiple_of((step * SUB + u) * tq, tq), tq), :]
        for h in range(2):
            own = (lane_q < 64) if h == 0 else (lane_q >= 64)
            base = 64 if h == 0 else 0
            qext[u, h] = jnp.where(own, q, jnp.where(lane_q == base, 1.0, 0.0).astype(B16))

    for h in range(2):
        @pl.when(norms[h] > 48.0 * 48.0)
        def _(h=h):
            own = (lane_q < 64) if h == 0 else (lane_q >= 64)
            base = 64 if h == 0 else 0

            def settle(u, carry):
                def grow(c, top):
                    return jnp.maximum(top, jnp.max(scores(h, u, c), axis=0, keepdims=True))
                top = lax.fori_loop(0, chunks, grow, jnp.full((1, tq), -3e38, F32))
                hi, mid, lo = split3(-jnp.broadcast_to(top * LN2, (128, tq)).T)
                extra = jnp.where(lane_q == base, jnp.ones_like(hi), jnp.zeros_like(hi))
                for at, part in ((1, hi), (2, mid), (3, lo)):
                    extra = jnp.where(lane_q == base + at, part, extra)
                qext[u, h] = jnp.where(own, qext[u, h], extra)
                return carry
            lax.fori_loop(0, SUB, settle, 0)

    for u in range(SUB):
        cols = slice(u * tq, (u + 1) * tq)
        for h in range(2):
            for c in range(chunks):
                e_ref[h, c * CK : (c + 1) * CK, cols] = jnp.exp2(scores(h, u, c)).astype(B16)
        outs = []
        for h in range(2):
            sums = dot(vext[h], e_ref[h, :, cols], NN)
            inv = 1.0 / sums[64:65, :]
            inv_ref[h : h + 1, cols] = inv
            outs.append(sums[0:64, :] * inv)
        out = jnp.concatenate(outs, axis=0)
        ot_ref[:, cols] = out
        o_ref[cols, :] = out.astype(B16).T

def attn_fwd(limit, qkv, curve):
    total = qkv.shape[0]
    pairs = qkv.shape[1] // 3 // 128
    tq = CK
    full = lambda off: pl.BlockSpec((total, 128), lambda p, i, s: (0, off + p))
    spec = pltpu.PrefetchScalarGridSpec(
        num_scalar_prefetch=1, grid=(pairs, total // (tq * SUB)),
        in_specs=[full(0), full(pairs), full(2 * pairs), pl.BlockSpec((None, 2, 2048), lambda p, i, s: (p, 0, 0))],
        out_specs=[
            pl.BlockSpec((2, total, SUB * tq), lambda p, i, s: (p, 0, i)),
            pl.BlockSpec((SUB * tq, 128), lambda p, i, s: (i, p)),
            pl.BlockSpec((128, SUB * tq), lambda p, i, s: (p, i)),
            pl.BlockSpec((None, 2, SUB * tq), lambda p, i, s: (p, 0, i)),
        ],
        scratch_shapes=[
            pltpu.VMEM((2, total, 128), B16), pltpu.VMEM((2, 80, total), B16),
            pltpu.VMEM((2, 5 * CK, tq), F32), pltpu.VMEM((SUB, 2, tq, 128), B16),
            pltpu.SMEM((2,), F32),
        ])
    n = 2 * pairs * total * total
    return pl.pallas_call(
        attn_fwd_body, grid_spec=spec, name="attn_fwd",
        out_shape=[jax.ShapeDtypeStruct((2 * pairs, total, total), B16),
                   jax.ShapeDtypeStruct((total, 128 * pairs), B16),
                   jax.ShapeDtypeStruct((128 * pairs, total), F32),
                   jax.ShapeDtypeStruct((pairs, 2, total), F32)],
        compiler_params=pltpu.CompilerParams(vmem_limit_bytes=56 << 20, dimension_semantics=("arbitrary", "arbitrary")),
        cost_estimate=pl.CostEstimate(flops=4 * 64 * n, transcendentals=n, bytes_accessed=2 * n),
    )(limit, qkv, qkv, qkv, curve)

def attn_bwd_body(e_ref, k_ref, v_ref, q_ref, do_ref, ot_ref, inv_ref,
                  dk_ref, dv_ref, dqo_ref, near_ref, far_ref,
                  doe, dop, qind, ds, band, dq_ref):
    total = q_ref.shape[0]
    ck = k_ref.shape[0]
    blocks = total // CK
    chunks = pl.num_programs(1)
    step = pl.program_id(1)

    @pl.when(step == 0)
    def _():
        parts = []
        dt = do_ref[...].T
        row = lax.broadcasted_iota(jnp.int32, (64, total), 0)
        for h in range(2):
            at = slice(64 * h, 64 * h + 64)
            part = (dt[at].astype(F32) * inv_ref[h : h + 1, :]).astype(B16)
            parts.append(part)
            inner = -jnp.sum(part.astype(F32) * ot_ref[at, :], axis=0, keepdims=True)
            hi, mid, lo = split3(jnp.broadcast_to(inner, (64, total)))
            extra = jnp.where(row == 0, hi, jnp.where(row == 1, mid, jnp.where(row == 2, lo, jnp.zeros_like(hi))))
            doe[h, 64 * h : 64 * h + 64, :] = part
            doe[h, 64 - 64 * h : 128 - 64 * h, :] = extra
            lane = lax.broadcasted_iota(jnp.int32, (total, 128), 1)
            own = (lane < 64) if h == 0 else (lane >= 64)
            base = 64 if h == 0 else 0
            at128 = lax.broadcasted_iota(jnp.int32, (total, 128), 0) >> 7
            qind[h] = jnp.where(own, q_ref[...], jnp.where(lane - base == at128, 1.0, 0.0).astype(B16))
        dop[...] = jnp.concatenate(parts, axis=0).T
        dq_ref[...] = jnp.zeros_like(dq_ref)
        band[...] = jnp.zeros_like(band)
        far_ref[...] = jnp.zeros_like(far_ref)

    lane = lax.broadcasted_iota(jnp.int32, (ck, 128), 1)
    v = v_ref[...]
    kt = k_ref[...].T
    for h in range(2):
        own = (lane < 64) if h == 0 else (lane >= 64)
        base = 64 if h == 0 else 0
        ones = jnp.where((lane >= base) & (lane < base + 3), 1.0, 0.0).astype(B16)
        vx = jnp.where(own, v, ones)
        for c in range(blocks):
            cols = slice(c * CK, (c + 1) * CK)
            pg = dot(vx, doe[h, :, cols], NN)
            ds[h, :, cols] = e_ref[h, :, cols] * pg.astype(B16)
    block = lax.broadcasted_iota(jnp.int32, (1, 128), 1)
    dvs, dks = [], []
    for h in range(2):
        at = slice(64 * h, 64 * h + 64)
        base = 64 if h == 0 else 0
        dvs.append(dot(e_ref[h], dop[...], NN))
        dk = dot(ds[h], qind[h], NN)
        dks.append(dk)
        dq_ref[at, :] += dot(kt[at], ds[h], NN)
        for u in range(SUB):
            kb = step * SUB + u
            rows = slice(u * CK, (u + 1) * CK)
            sums_u = jnp.sum(dk[rows], axis=0, keepdims=True)
            spot = block - base
            inside = (spot >= 0) & (spot < total // 128)
            far_ref[h, 0:1, :] += jnp.where(inside & (spot < 2 * kb - 1), sums_u, 0.0)
            far_ref[h, 1:2, :] += jnp.where(inside & (spot >= 2 * kb + 3), sums_u, 0.0)
            band[h, :, 128 : 128 + CK] += ds[h, rows, pl.ds(pl.multiple_of(kb * CK, CK), CK)].astype(F32)

            @pl.when(kb > 0)
            def _(h=h, kb=kb, rows=rows):
                band[h, :, 0:128] += ds[h, rows, pl.ds(pl.multiple_of(kb * CK - 128, 128), 128)].astype(F32)

            @pl.when(kb < blocks - 1)
            def _(h=h, kb=kb, rows=rows):
                band[h, :, 128 + CK : 256 + CK] += ds[h, rows, pl.ds(pl.multiple_of(kb * CK + CK, 128), 128)].astype(F32)

    dk_ref[...] = jnp.where(lane < 64, dks[0], dks[1]).astype(B16).T
    dv_ref[...] = jnp.where(lane < 64, dvs[0], dvs[1]).astype(B16).T

    @pl.when(step == chunks - 1)
    def _():
        dqo_ref[...] = dq_ref[...].astype(B16)
        width = CK + 256
        row = lax.broadcasted_iota(jnp.int32, (CK, width), 0)
        col = lax.broadcasted_iota(jnp.int32, (CK, width), 1)
        offset = row - col + 128
        for h in range(2):
            all_now = band[h]
            near = jnp.where(jnp.abs(offset) < 128, all_now, 0.0)
            folded = near[0:8, :]
            for g in range(1, CK // 8):
                folded = folded + pltpu.roll(near[8 * g : 8 * g + 8, :], width - 8 * g, 1)
            line = folded[0:1, :]
            for g in range(1, 8):
                line = line + pltpu.roll(folded[g : g + 1, :], width - g, 1)
            near_ref[h, 0:1, :] = line
            near_ref[h, 1:2, :] = jnp.sum(jnp.where(offset >= 128, all_now, 0.0), axis=0, keepdims=True)
            near_ref[h, 2:3, :] = jnp.sum(jnp.where(offset <= -128, all_now, 0.0), axis=0, keepdims=True)
            near_ref[h, 3:8, :] = jnp.zeros((5, width), F32)

def attn_bwd(e, qkv, d_att, att_t, inv, start, count):
    total = qkv.shape[0]
    pairs = qkv.shape[1] // 3 // 128
    ck = CK * SUB
    full = pl.BlockSpec((total, 128), lambda p, i: (0, start + p))
    part = lambda off: pl.BlockSpec((ck, 128), lambda p, i: (i, off + start + p))
    flat = pl.BlockSpec((128, ck), lambda p, i: (p, i))
    tall = pl.BlockSpec((128, total), lambda p, i: (p, 0))
    n = 2 * count * total * total
    return pl.pallas_call(
        attn_bwd_body, grid=(count, total // ck), name="attn_bwd",
        in_specs=[pl.BlockSpec((2, ck, total), lambda p, i: (start + p, i, 0)), part(pairs), part(2 * pairs),
                  full, full, pl.BlockSpec((128, total), lambda p, i: (start + p, 0)),
                  pl.BlockSpec((None, 2, total), lambda p, i: (start + p, 0, 0))],
        out_specs=[flat, flat, tall,
                   pl.BlockSpec((2, 8, CK + 256), lambda p, i: (p, 0, 0)),
                   pl.BlockSpec((2, 8, 128), lambda p, i: (p, 0, 0))],
        out_shape=[jax.ShapeDtypeStruct((128 * count, total), B16)] * 3
        + [jax.ShapeDtypeStruct((2 * count, 8, CK + 256), F32), jax.ShapeDtypeStruct((2 * count, 8, 128), F32)],
        scratch_shapes=[
            pltpu.VMEM((2, 128, total), B16), pltpu.VMEM((total, 128), B16), pltpu.VMEM((2, total, 128), B16),
            pltpu.VMEM((2, ck, total), B16), pltpu.VMEM((2, CK, CK + 256), F32), pltpu.VMEM((128, total), F32),
        ],
        compiler_params=pltpu.CompilerParams(vmem_limit_bytes=60 << 20, dimension_semantics=("arbitrary", "arbitrary")),
        cost_estimate=pl.CostEstimate(flops=8 * 64 * n, transcendentals=0, bytes_accessed=2 * n),
    )(e, qkv, qkv, qkv, d_att, att_t, inv)

def bias_curve(rel, heads):
    offset = 1024 - jnp.arange(2048, dtype=jnp.int32)
    onehot = (bucket_of(offset)[:, None] == jnp.arange(32, dtype=jnp.int32)).astype(F32)
    curve = jnp.einsum("xb,bh->hx", onehot, rel.astype(F32) * LOG2E, precision=lax.Precision.HIGHEST)
    return curve.reshape(heads // 2, 2, 2048)

def rel_grad(near, far, width):
    x = jnp.arange(width, dtype=jnp.int32)
    onehot = (bucket_of(128 - x)[:, None] == jnp.arange(32, dtype=jnp.int32)).astype(F32)
    onehot = onehot * (x[:, None] < 256)
    g = jnp.einsum("hx,xb->bh", near[:, 0, :], onehot, precision=lax.Precision.HIGHEST)
    up = jnp.sum(near[:, 1, :], axis=1) + jnp.sum(far[:, 0], axis=1)
    down = jnp.sum(near[:, 2, :], axis=1) + jnp.sum(far[:, 1], axis=1)
    slot = jnp.arange(32)[:, None]
    return g + jnp.where(slot == 31, up[None], 0.0) + jnp.where(slot == 15, down[None], 0.0)

CJ = 272
CC = 1408
TT = 384

def means_of(even, odd):
    t = lax.broadcasted_iota(jnp.int32, even.shape, 1)
    width = even.shape[1]
    prev = lambda x: pltpu.roll(x, 1, 1)
    succ = lambda x: pltpu.roll(x, width - 1, 1)
    two = even + odd
    four = two + jnp.where(t % 2 == 0, succ(two), prev(two))
    place = t - 3 * ((t * 21846) >> 16)
    first = two + succ(even)
    middle_e = prev(two) + even
    middle_o = odd + succ(two)
    last = prev(odd) + two
    three_e = jnp.where(place == 0, first, jnp.where(place == 1, middle_e, last))
    three_o = jnp.where(place == 0, first, jnp.where(place == 1, middle_o, last))
    third = 1.0 / 3.0
    return [(even, odd), (two * 0.5, two * 0.5), (three_e * third, three_o * third), (four * 0.25, four * 0.25)]

def masks():
    t = lax.broadcasted_iota(jnp.int32, (TT, 1), 0)
    p = lax.broadcasted_iota(jnp.int32, (1, 2 * TT), 1)
    par = p >= TT
    tp = jnp.where(par, p - TT, p)
    third = lambda x: (x * 21846) >> 16
    blk = third(2 * tp + jnp.where(par, 1, 0))
    even = t == jnp.where(par, -1, tp)
    odd = t == jnp.where(par, tp, -1)
    return even, odd, (t >> 1) == (tp >> 1), third(2 * t) == blk, third(2 * t + 1) == blk


def fill_onehot(ids_ref, oht):
    row = lax.broadcasted_iota(jnp.int32, (CJ, TT), 0)
    for j in range(5):
        for side in range(2):
            hit = row == ids_ref[j + side : j + side + 1, :]
            oht[CJ * j : CJ * (j + 1), TT * side : TT * (side + 1)] = jnp.where(hit, 1.0, 0.0).astype(B16)
    oht[5 * CJ :, :] = jnp.zeros((CC - 5 * CJ, 2 * TT), B16)

def gbst_fwd_body(cid_ref, raw_ref, taps_ref, scorer_ref, gain_ref, tok_ref, norm_ref, w_ref, mix_ref, table_ref,
                  oht, rest, tvec, both, wide):
    @pl.when(pl.program_id(0) == 0)
    def _():
        raw = raw_ref[...].astype(F32)
        for j in range(5):
            at = slice(CJ * j, CJ * (j + 1))
            tap = taps_ref[j : j + 1, :].astype(F32)
            cat = raw * tap
            hi = cat.astype(B16)
            table_ref[at, :] = hi
            rest[at, :] = (cat - hi.astype(F32)).astype(B16)
            parts = split3(jnp.broadcast_to(tap * scorer_ref[...].astype(F32), (16, cat.shape[1])))
            which = lax.broadcasted_iota(jnp.int32, (16, cat.shape[1]), 0)
            zero = jnp.zeros_like(parts[0])
            rows = jnp.where(which == 0, parts[0], jnp.where(which == 1, parts[1], jnp.where(which == 2, parts[2], zero)))
            scores = dot(rows, raw_ref[...], NT)
            line = split3(jnp.broadcast_to(scores[0:1] + scores[1:2] + scores[2:3], (16, CJ)))
            which = lax.broadcasted_iota(jnp.int32, (16, CJ), 0)
            zero = jnp.zeros_like(line[0])
            tvec[j] = jnp.where(which == 0, line[0], jnp.where(which == 1, line[1], jnp.where(which == 2, line[2], zero)))
        table_ref[5 * CJ :, :] = jnp.zeros((CC - 5 * CJ, table_ref.shape[1]), B16)
        rest[5 * CJ :, :] = jnp.zeros((CC - 5 * CJ, table_ref.shape[1]), B16)
    fill_onehot(cid_ref, oht)
    parts = dot(tvec[0], oht[0:CJ, :], NN)
    for j in range(1, 5):
        parts = parts + dot(tvec[j], oht[CJ * j : CJ * (j + 1), :], NN)
    weighted = parts[0:1] + parts[1:2] + parts[2:3]
    scores = means_of(weighted[:, :TT], weighted[:, TT:])
    rows = []
    for side in range(2):
        mine = [s[side] for s in scores]
        top = jnp.maximum(jnp.maximum(mine[0], mine[1]), jnp.maximum(mine[2], mine[3]))
        e = [jnp.exp(s - top) for s in mine]
        inv = 1.0 / (e[0] + e[1] + e[2] + e[3])
        rows.append([x * inv for x in e])
    mix = jnp.concatenate([rows[side][b] for b in range(4) for side in range(2)], axis=0)
    mix_ref[...] = mix
    col = mix.T
    c = lambda i: col[:, i : i + 1]
    even, odd, pair, tri_e, tri_o = masks()
    two = 0.25 * (c(2) + c(3))
    w = jnp.where(even, 0.5 * c(0) + two, jnp.where(odd, 0.5 * c(1) + two, 0.0))
    w = w + jnp.where(pair, 0.125 * (c(6) + c(7)), 0.0)
    w = w + jnp.where(tri_e, c(4) * (1.0 / 6.0), 0.0) + jnp.where(tri_o, c(5) * (1.0 / 6.0), 0.0)
    w_hi = w.astype(B16)
    w_lo = (w - w_hi.astype(F32)).astype(B16)
    w_ref[...] = w_hi
    both[0:TT, :] = w_hi
    both[TT:, :] = w_lo
    a = dot(both[...], oht[...], NT)
    a = a[0:TT] + a[TT:]
    a_hi = a.astype(B16)
    wide[0:TT, :] = a_hi
    wide[TT:, :] = (a - a_hi.astype(F32)).astype(B16)
    tokens = dot(wide[...], table_ref[...], NN)
    tokens = tokens[0:TT] + tokens[TT:] + dot(a_hi, rest[...], NN)
    tok_ref[...] = tokens
    r = lax.rsqrt(jnp.mean(tokens * tokens, axis=1, keepdims=True) + EPS)
    norm_ref[...] = (tokens * r * gain_ref[...].astype(F32)).astype(B16)

def gbst_fwd(cid, raw, taps, scorer, gain):
    tiles = cid.shape[0]
    d = raw.shape[1]
    rows = tiles * TT
    const = lambda shape: pl.BlockSpec(shape, lambda i: (0,) * len(shape))
    return pl.pallas_call(
        gbst_fwd_body, grid=(tiles,), name="gbst_fwd",
        in_specs=[pl.BlockSpec((None, 8, TT), lambda i: (i, 0, 0)), const((CJ, d)), const((5, d)), const((1, d)), const((1, d))],
        out_specs=[pl.BlockSpec((TT, d), lambda i: (i, 0)), pl.BlockSpec((TT, d), lambda i: (i, 0)),
                   pl.BlockSpec((TT, 2 * TT), lambda i: (i, 0)), pl.BlockSpec((None, 8, TT), lambda i: (i, 0, 0)),
                   const((CC, d))],
        out_shape=[jax.ShapeDtypeStruct((rows, d), F32), jax.ShapeDtypeStruct((rows, d), B16),
                   jax.ShapeDtypeStruct((rows, 2 * TT), B16), jax.ShapeDtypeStruct((tiles, 8, TT), F32),
                   jax.ShapeDtypeStruct((CC, d), B16)],
        scratch_shapes=[pltpu.VMEM((CC, 2 * TT), B16), pltpu.VMEM((CC, d), B16), pltpu.VMEM((5, 16, CJ), B16),
                        pltpu.VMEM((2 * TT, 2 * TT), B16), pltpu.VMEM((2 * TT, CC), B16)],
        compiler_params=pltpu.CompilerParams(vmem_limit_bytes=56 << 20),
        cost_estimate=pl.CostEstimate(flops=rows * CC * d * 8, transcendentals=0, bytes_accessed=rows * d * 8),
    )(cid, raw, taps, scorer, gain)

def gbst_bwd_body(cid_ref, w_ref, mix_ref, tok_ref, hid_ref, nb_ref, nr_ref, gain_ref, table_ref, raw_ref, taps_ref, scorer_ref,
                  extra_ref, gt_ref, small_ref, oht, big, usum):
    i = pl.program_id(0)
    fill_onehot(cid_ref, oht)

    @pl.when(i == 0)
    def _():
        big[...] = jnp.zeros_like(big)
        usum[...] = jnp.zeros_like(usum)
        small_ref[...] = jnp.zeros_like(small_ref)
    x = tok_ref[...]
    n = nb_ref[...].astype(F32) + nr_ref[...].astype(F32)
    r = lax.rsqrt(jnp.mean(x * x, axis=1, keepdims=True) + EPS)
    u = n * gain_ref[...].astype(F32)
    xr = x * r
    g = hid_ref[...].astype(F32) + r * (u - xr * jnp.mean(u * xr, axis=1, keepdims=True))
    small_ref[6:7, :] += jnp.sum(n * xr, axis=0, keepdims=True)
    gb = g.astype(B16)
    hh = dot(gb, table_ref[...], NT).astype(B16)
    gram = dot(hh, oht[...], NN)
    even, odd, pair, tri_e, tri_o = masks()
    lanesum = lambda m: jnp.sum(jnp.where(m, gram, 0.0), axis=1, keepdims=True)
    me = 0.5 * lanesum(even)
    mo = 0.5 * lanesum(odd)
    m2 = 0.5 * (me + mo)
    m4 = 0.125 * lanesum(pair)
    m3e = lanesum(tri_e) * (1.0 / 6.0)
    m3o = lanesum(tri_o) * (1.0 / 6.0)
    lane8 = lax.broadcasted_iota(jnp.int32, (TT, 128), 1)
    cols = jnp.zeros((TT, 128), F32)
    for k, v in enumerate((me, mo, m2, m2, m3e, m3o, m4, m4)):
        cols = jnp.where(lane8 == k, v, cols)
    dmix = cols.T[0:8, :]
    mix = mix_ref[...]
    row = lambda a, k: a[k : k + 1, :]
    sides = []
    for side in range(2):
        inner = sum(row(mix, 2 * b + side) * row(dmix, 2 * b + side) for b in range(4))
        sides.append([row(mix, 2 * b + side) * (row(dmix, 2 * b + side) - inner) for b in range(4)])
    dwe = jnp.zeros((1, TT), F32)
    dwo = jnp.zeros((1, TT), F32)
    for b in range(4):
        e, o = means_of(sides[0][b], sides[1][b])[b]
        dwe = dwe + e
        dwo = dwo + o
    dw = jnp.concatenate([dwe, dwo], axis=1)
    hi, mid, lo = split3(jnp.broadcast_to(dw, (16, 2 * TT)))
    which = lax.broadcasted_iota(jnp.int32, (16, 2 * TT), 0)
    dw3 = jnp.where(which == 0, hi, jnp.where(which == 1, mid, jnp.where(which == 2, lo, jnp.zeros_like(hi))))
    usum[...] += dot(dw3, oht[...], NT)
    at = dot(oht[...], w_ref[...], NT).astype(B16)
    big[...] += dot(at, gb, NN)

    @pl.when(i == pl.num_programs(0) - 1)
    def _():
        us = usum[...]
        urow = us[0:1] + us[1:2] + us[2:3]
        hi, mid, lo = split3(jnp.broadcast_to(urow, (16, CC)))
        which = lax.broadcasted_iota(jnp.int32, (16, CC), 0)
        u3 = jnp.where(which == 0, hi, jnp.where(which == 1, mid, jnp.where(which == 2, lo, jnp.zeros_like(hi))))
        gs = dot(u3, table_ref[...], NN)
        small_ref[5:6, :] = gs[0:1] + gs[1:2] + gs[2:3]
        ucol = jnp.broadcast_to(urow, (128, CC)).T[:, 0:1]
        total = jnp.zeros((CJ, gt_ref.shape[1]), F32)
        for j in range(5):
            m = big[CJ * j : CJ * (j + 1), :] + ucol[CJ * j : CJ * (j + 1)] * scorer_ref[...].astype(F32)
            total = total + m * taps_ref[j : j + 1, :].astype(F32)
            small_ref[j : j + 1, :] = jnp.sum(m * raw_ref[...].astype(F32), axis=0, keepdims=True)
        gt_ref[0:CJ, :] = total
        gt_ref[CJ : CJ + 8, :] = small_ref[...]
        gt_ref[CJ + 8 :, :] = extra_ref[...]

def gbst_bwd(cid, w, mix, tok, hid, nb, nr, gain, table, raw, taps, scorer, extra):
    tiles = cid.shape[0]
    d = table.shape[1]
    rows = tiles * TT
    const = lambda shape: pl.BlockSpec(shape, lambda i: (0,) * len(shape))
    tile = lambda width: pl.BlockSpec((TT, width), lambda i: (i, 0))
    return pl.pallas_call(
        gbst_bwd_body, grid=(tiles,), name="gbst_bwd",
        in_specs=[pl.BlockSpec((None, 8, TT), lambda i: (i, 0, 0)), tile(2 * TT), pl.BlockSpec((None, 8, TT), lambda i: (i, 0, 0)),
                  tile(d), tile(d), tile(d), tile(d), const((1, d)), const((CC, d)), const((CJ, d)), const((5, d)), const((1, d)), const((8, d))],
        out_specs=const((CJ + 16, d)),
        out_shape=jax.ShapeDtypeStruct((CJ + 16, d), F32),
        scratch_shapes=[pltpu.VMEM((8, d), F32), pltpu.VMEM((CC, 2 * TT), B16), pltpu.VMEM((CC, d), F32), pltpu.VMEM((16, CC), F32)],
        compiler_params=pltpu.CompilerParams(vmem_limit_bytes=56 << 20),
        cost_estimate=pl.CostEstimate(flops=rows * CC * d * 8, transcendentals=0, bytes_accessed=rows * d * 12),
    )(cid, w, mix, tok, hid, nb, nr, gain, table, raw, taps, scorer, extra)


FC = 512
RT = 288


def middle_body(tok_ref, ao_ref, ar_ref, woo_ref, wor_ref, wgo_ref, wgr_ref, wuo_ref, wur_ref, wdo_ref, wdr_ref,
                og_ref, gain_ref,
                layer_ref, back_ref, down_ref, dsend_ref, goo_ref, gor_ref, ggo_ref, guo_ref, gdo_ref, ggr_ref, gur_ref, gdr_ref,
                gain_out,
                hid, n2, n2t, ogt, outs, n2b, wg, wu, wd, inner_s, gb_s, ub_s):
    i = pl.program_id(0)
    steps = pl.num_programs(0)
    rows = tok_ref.shape[0]
    tiles = [slice(r, r + RT) for r in range(0, rows, RT)]
    gain = gain_ref[...].astype(F32)

    @pl.when(i == 0)
    def _():
        for at in tiles:
            h = tok_ref[at, :] + dot(ao_ref[at, :], woo_ref[...], NN) + dot(ar_ref[at, :], wor_ref[...], NN)
            hid[at, :] = h
            r = lax.rsqrt(jnp.mean(h * h, axis=1, keepdims=True) + EPS)
            n2[at, :] = (h * r * gain).astype(B16)
            outs[at, :] = h
            n2b[at, :] = jnp.zeros((RT, h.shape[1]), F32)
        n2t[...] = n2[...].T
        ogt[...] = og_ref[...].T

    @pl.when(i < steps // 2)
    def _():
        wg[...] = wgo_ref[...]
        wu[...] = wuo_ref[...]
        wd[...] = wdo_ref[...]

    @pl.when(i >= steps // 2)
    def _():
        wg[...] = wgr_ref[...]
        wu[...] = wur_ref[...]
        wd[...] = wdr_ref[...]

    for at in tiles:
        x = n2[at, :]
        gate = dot(x, wg[...], NN)
        up = dot(x, wu[...], NN)
        gi = dot(og_ref[at, :], wd[...], NT)
        act, slope = gelu_parts(gate)
        inner = (act * up).astype(B16)
        gb = (gi * up * slope).astype(B16)
        ub = (gi * act).astype(B16)
        inner_s[at, :] = inner
        gb_s[at, :] = gb
        ub_s[at, :] = ub
        outs[at, :] += dot(inner, wd[...], NN)
        n2b[at, :] += dot(gb, wg[...], NT) + dot(ub, wu[...], NT)
    pieces = [dot(n2t[...], gb_s[...], NN), dot(n2t[...], ub_s[...], NN), dot(ogt[...], inner_s[...], NN)]
    pieces = [x.astype(B16) for x in pieces]

    @pl.when(i < steps // 2)
    def _():
        for ref, x in zip((ggo_ref, guo_ref, gdo_ref), pieces):
            ref[...] = x

    @pl.when(i >= steps // 2)
    def _():
        for ref, x in zip((ggr_ref, gur_ref, gdr_ref), pieces):
            ref[...] = x

    @pl.when(i == steps - 1)
    def _():
        total = jnp.zeros(gain.shape, F32)
        for at in tiles:
            h = hid[at, :]
            layer_ref[at, :] = outs[at, :].astype(B16)
            r = lax.rsqrt(jnp.mean(h * h, axis=1, keepdims=True) + EPS)
            back = n2b[at, :]
            u = back * gain
            hr = h * r
            total = total + jnp.sum(back * hr, axis=0, keepdims=True)
            hb = og_ref[at, :].astype(F32) + r * (u - hr * jnp.mean(u * hr, axis=1, keepdims=True))
            back_ref[at, :] = hb
            low = hb.astype(B16)
            n2[at, :] = low
            down_ref[at, :] = dot(low, woo_ref[...], NT).astype(B16)
            dsend_ref[at, :] = dot(low, wor_ref[...], NT).astype(B16)
        gain_out[...] = total
        n2t[...] = n2[...].T
        goo_ref[...] = dot(n2t[...], ao_ref[...], NN).astype(B16)
        gor_ref[...] = dot(n2t[...], ar_ref[...], NN).astype(B16)


def middle(tok, att_own, att_recv, wo, wo_other, wg, wg_other, wu, wu_other, wd, wd_other, og, gain):
    rows, d = tok.shape
    proj = att_own.shape[1]
    ffn = wg.shape[1]
    half = ffn // FC
    const = lambda *shape: pl.BlockSpec(shape, lambda i: (0,) * len(shape))
    once = lambda *shape: pl.BlockSpec(shape, lambda i: (0,) * len(shape), pipeline_mode=pl.Buffered(1))
    low = lambda i: jnp.minimum(i, half - 1)
    high = lambda i: jnp.maximum(i - half, 0)
    wide = lambda f: pl.BlockSpec((d, FC), lambda i: (0, f(i)))
    tall = lambda f: pl.BlockSpec((FC, d), lambda i: (f(i), 0))
    sds = jax.ShapeDtypeStruct
    flops = 2 * rows * d * (8 * 2 * ffn + 6 * proj) * 9 // 8
    return pl.pallas_call(
        middle_body, grid=(2 * half,), name="middle",
        in_specs=[once(rows, d), once(rows, proj), once(rows, proj), once(proj, d), once(proj, d),
                  wide(low), wide(high), wide(low), wide(high), tall(low), tall(high), once(rows, d), const(1, d)],
        out_specs=[once(rows, d), once(rows, d), once(rows, proj), once(rows, proj), once(d, proj), once(d, proj),
                   wide(low), wide(low), wide(low), wide(high), wide(high), wide(high), const(1, d)],
        out_shape=[sds((rows, d), B16), sds((rows, d), F32), sds((rows, proj), B16), sds((rows, proj), B16),
                   sds((d, proj), B16), sds((d, proj), B16)] + [sds((d, ffn), B16)] * 6 + [sds((1, d), F32)],
        scratch_shapes=[
            pltpu.VMEM((rows, d), F32), pltpu.VMEM((rows, d), B16), pltpu.VMEM((d, rows), B16), pltpu.VMEM((d, rows), B16),
            pltpu.VMEM((rows, d), F32), pltpu.VMEM((rows, d), F32),
            pltpu.VMEM((d, FC), B16), pltpu.VMEM((d, FC), B16), pltpu.VMEM((FC, d), B16),
            pltpu.VMEM((rows, FC), B16), pltpu.VMEM((rows, FC), B16), pltpu.VMEM((rows, FC), B16),
        ],
        compiler_params=pltpu.CompilerParams(vmem_limit_bytes=61 << 20, dimension_semantics=("arbitrary",)),
        cost_estimate=pl.CostEstimate(flops=flops, transcendentals=rows * 2 * ffn, bytes_accessed=rows * d * 20 + 24 * d * ffn),
    )(tok, att_own, att_recv, wo, wo_other, wg, wg_other, wu, wu_other, wd, wd_other, og, gain)


def post_body(core_ref, qa, qb, ka, kb, va, vb, w_ref, n_ref, own_ref, send_ref, g_ref, rows):
    i = pl.program_id(0)
    span = n_ref.shape[0]
    d = jnp.concatenate([qa[...], qb[...], ka[...], kb[...], va[...], vb[...]], axis=0)
    back = dot(w_ref[...], d, NN).astype(B16).T
    rows[pl.ds(pl.multiple_of(i * span, span), span), :] = back
    part = dot(n_ref[...].T, d, NT)

    @pl.when(i == 0)
    def _():
        g_ref[...] = part

    @pl.when(i > 0)
    def _():
        g_ref[...] += part

    @pl.when(i == pl.num_programs(0) - 1)
    def _():
        core = core_ref[0]
        half = own_ref.shape[1]
        for s in range(own_ref.shape[0]):
            own_ref[s] = rows[pl.ds(pl.multiple_of((2 * s + core) * half, 32), half), :]
            send_ref[s] = rows[pl.ds(pl.multiple_of((2 * s + 1 - core) * half, 32), half), :]


def post(core, pieces, w, normed, blocks):
    total, d = normed.shape
    span = CK * SUB
    half = total // blocks // 2
    lanes = lambda x: pl.BlockSpec((x.shape[0], span), lambda i, s: (0, i))
    const = lambda *shape: pl.BlockSpec(shape, lambda i, s: (0,) * len(shape))
    spec = pltpu.PrefetchScalarGridSpec(
        num_scalar_prefetch=1, grid=(total // span,),
        in_specs=[lanes(x) for x in pieces] + [const(*w.shape), pl.BlockSpec((span, d), lambda i, s: (i, 0))],
        out_specs=[const(blocks, half, d), const(blocks, half, d), const(*w.shape)],
        scratch_shapes=[pltpu.VMEM((total, d), B16)])
    return pl.pallas_call(
        post_body, grid_spec=spec, name="post",
        out_shape=[jax.ShapeDtypeStruct((blocks, half, d), B16), jax.ShapeDtypeStruct((blocks, half, d), B16),
                   jax.ShapeDtypeStruct(w.shape, F32)],
        compiler_params=pltpu.CompilerParams(vmem_limit_bytes=56 << 20, dimension_semantics=("arbitrary",)),
        cost_estimate=pl.CostEstimate(flops=4 * total * d * w.shape[1], transcendentals=0, bytes_accessed=30 * total * d // 4),
    )(core, *pieces, w, normed)


def unpack_body(x_ref, gate_ref, up_ref, down_ref, out_ref):
    f = gate_ref.shape[1]
    gate_ref[...] = x_ref[:, 0:f].astype(F32)
    up_ref[...] = x_ref[:, f : 2 * f].astype(F32)
    down_ref[...] = x_ref[:, 2 * f : 3 * f].astype(F32).T
    out_ref[...] = x_ref[:, 3 * f :].astype(F32).T


def unpack(x, f):
    d, columns = x.shape
    p = columns - 3 * f
    row = lambda width: pl.BlockSpec((128, width), lambda i: (i, 0))
    col = lambda width: pl.BlockSpec((width, 128), lambda i: (0, i))
    return pl.pallas_call(
        unpack_body, grid=(d // 128,), name="unpack",
        in_specs=[row(columns)], out_specs=[row(f), row(f), col(f), col(p)],
        out_shape=[jax.ShapeDtypeStruct((d, f), F32), jax.ShapeDtypeStruct((d, f), F32),
                   jax.ShapeDtypeStruct((f, d), F32), jax.ShapeDtypeStruct((p, d), F32)],
        compiler_params=pltpu.CompilerParams(vmem_limit_bytes=40 << 20, dimension_semantics=("arbitrary",)),
        cost_estimate=pl.CostEstimate(flops=0, transcendentals=0, bytes_accessed=6 * d * columns),
    )(x)


def swapped(tree):
    return jax.tree.map(lambda a: lax.ppermute(a, "mp", [(0, 1), (1, 0)]), tree)


def matmul(a, b):
    return dot(a, b, NN)


def grad_of(a, b):
    return lax.dot_general(a, b, (((0,), (0,)), ((), ())), preferred_element_type=F32)


X_SWAP = ("dp", 0)
Y_SWAP = ("dp", 1)
Z_NEAR = ("seq", 0)
Z_FAR = ("seq", 1)


def hop(x, axis, bit):
    count = lax.axis_size(axis)
    return lax.ppermute(x, axis, [(i, i ^ (1 << bit)) for i in range(count)])


def side_of(axis, bit):
    return (lax.axis_index(axis) >> bit) & 1


def give(x, axis, bit, behind=None):
    side = side_of(axis, bit)
    rows = x.shape[0] // 2
    keep = lax.dynamic_slice_in_dim(x, side * rows, rows, 0)
    send = lax.dynamic_slice_in_dim(x, (1 - side) * rows, rows, 0)
    recv = hop(send.astype(B16), axis, bit)
    if behind is not None:
        recv, keep = after(recv, behind), after(keep, behind)
    return keep.astype(F32) + recv.astype(F32)


def take(x, axis, bit):
    first = side_of(axis, bit) == 0
    other = hop(x, axis, bit)
    return jnp.concatenate([jnp.where(first, x, other), jnp.where(first, other, x)], axis=0)


def two_ways(x, step, ways):
    cut = x.shape[1] // 2
    return [step(x[:, :cut], *ways[0]), step(x[:, cut:], *ways[1])]


def after(value, *others):
    return lax.optimization_barrier((value,) + others)[0]


def gelu_parts(gate):
    c = 0.7978845608028654
    inside = c * (gate + 0.044715 * gate * gate * gate)
    th = jnp.tanh(inside)
    value = 0.5 * gate * (1.0 + th)
    slope = 0.5 * (1.0 + th) + 0.5 * gate * (1.0 - th * th) * (c * (1.0 + 3.0 * 0.044715 * gate * gate))
    return value, slope


def local_item(
    byte_ids, true_lengths, byte_table, conv_taps, block_scorer, attn_gain, w_query, w_key, w_value,
    w_output, rel_table, ffn_gain, w_gate, w_up, w_down, out_grad,
):
    seq_count = lax.axis_size("seq")
    place = lax.axis_index("seq")
    core = lax.axis_index("mp")
    tok_rows = out_grad.shape[0]
    half = tok_rows // 2
    width = out_grad.shape[2]
    own_rows = seq_count * half
    total = 2 * own_rows
    proj = w_query.shape[1]
    first = core == 0

    def halves(full):
        parts = full.reshape(seq_count, 2, half, full.shape[1])
        own = jnp.where(first, parts[:, 0], parts[:, 1]).reshape(own_rows, -1)
        other = jnp.where(first, parts[:, 1], parts[:, 0]).reshape(own_rows, -1)
        return own, other

    def whole(own, other):
        shape = (seq_count, half, own.shape[1])
        low, high = jnp.where(first, own, other), jnp.where(first, other, own)
        return jnp.stack([low.reshape(shape), high.reshape(shape)], axis=1).reshape(total, -1)

    byte_rows = byte_ids.shape[0]
    here = place * byte_rows + jnp.arange(byte_rows, dtype=jnp.int32)
    shown = jnp.where(here[:, None] < true_lengths[None, :], byte_ids, -1)
    shown = shown.reshape(tok_rows, 2, seq_count).transpose(2, 1, 0)
    shown = lax.all_to_all(shown, "seq", split_axis=0, concat_axis=0, tiled=True)
    length = lax.dynamic_index_in_dim(true_lengths, place, 0, keepdims=False)
    wo_other, wg_other, wu_other, wd_other = swapped((w_output, w_gate, w_up, w_down))
    grad_rows = lax.dynamic_slice_in_dim(out_grad, core * half, half, 0)
    grad_own = lax.all_to_all(grad_rows, "seq", split_axis=1, concat_axis=0, tiled=True)
    grad_own = grad_own.reshape(own_rows, width)

    tiles = own_rows // TT
    pairs = jnp.pad(shown.transpose(1, 0, 2).reshape(2, total), ((0, 0), (1, 1)), constant_values=-1)
    rows = jnp.concatenate([pairs[:, j : j + total] for j in range(3)], axis=0).reshape(6, seq_count, 2, half)
    rows = jnp.where(first, rows[:, :, 0], rows[:, :, 1]).reshape(6, tiles, TT).transpose(1, 0, 2)
    cid = jnp.pad(rows, ((0, 0), (0, 2), (0, 0)), constant_values=-1)

    vocab = byte_table.shape[0]
    raw = jnp.pad(byte_table, ((0, CJ - vocab), (0, 0)))
    scorer, gain_one, gain_two = block_scorer[None], attn_gain[None], ffn_gain[None]
    tokens, normed, pool_w, mix, table_cat = gbst_fwd(cid, raw, conv_taps, scorer, gain_one)
    normed_all = whole(normed, swapped(normed))
    w_qkv = jnp.concatenate([w_query, w_key, w_value], axis=1)
    qkv = matmul(normed_all, w_qkv).astype(B16)
    limit = ((length + 1) // 2).reshape(1)
    weights, att, att_t, inv = attn_fwd(limit, qkv, bias_curve(rel_table, proj // DH))
    att_own, att_send = halves(att)
    att_recv = swapped(att_send)
    (layer, hidden_back, d_own, d_send, out_own, out_other, gate_own, up_own, down_own,
     gate_other, up_other, down_other, g_gain_two) = middle(
        tokens, att_own, att_recv, w_output, wo_other, w_gate, wg_other, w_up, wu_other, w_down, wd_other,
        grad_own, gain_two
    )
    d_att = whole(d_own, swapped(d_send))

    ffn_width = w_gate.shape[1]
    add = lambda a, b: (a.astype(F32) + b.astype(F32)).astype(B16)
    own_cols = (gate_own, up_own, down_own, out_own)
    other_cols = swapped((gate_other, up_other, down_other, out_other))
    large = jnp.concatenate([add(a, b) for a, b in zip(own_cols, other_cols)], axis=1)
    large = lax.psum_scatter(large, "dp", scatter_dimension=0, tiled=True)

    pairs = proj // 128
    early = pairs - 1
    dk_a, dv_a, dq_a, near_a, far_a = attn_bwd(weights, qkv, d_att, att_t, inv, 0, early)
    sent = layer.reshape(seq_count, half, width)
    layer_out = lax.all_to_all(sent[:, :, None], "seq", split_axis=0, concat_axis=2, tiled=True)
    late, dk_a, dv_a, dq_a, large, layer_out = lax.optimization_barrier((d_att, dk_a, dv_a, dq_a, large, layer_out))
    large = lax.psum_scatter(large, "seq", scatter_dimension=0, tiled=True)
    dk_b, dv_b, dq_b, near_b, far_b = attn_bwd(weights, qkv, late, att_t, inv, early, 1)
    near, far = jnp.concatenate([near_a, near_b]), jnp.concatenate([far_a, far_b])
    dk_b, large = lax.optimization_barrier((dk_b, large))
    pieces = (dq_a, dq_b, dk_a, dk_b, dv_a, dv_b)
    part_own, part_send, g_qkv = post(core.reshape(1).astype(jnp.int32), pieces, w_qkv, normed_all, seq_count)
    part_own = part_own.reshape(own_rows, width)
    part_recv = swapped(part_send).reshape(own_rows, width)
    large = lax.all_gather(large, "seq", axis=0, tiled=True)
    part_own, large = lax.optimization_barrier((part_own, large))
    large = lax.all_gather(large, "dp", axis=0, tiled=True)
    g_rel = rel_grad(near, far, near.shape[2])
    rel_row = jnp.pad(g_rel.reshape(1, -1), ((0, 0), (0, width - g_rel.size)))
    blank = jnp.zeros_like(rel_row)
    rel_rows = [jnp.where(first, rel_row, blank), jnp.where(first, blank, rel_row)]
    extra = jnp.concatenate([g_gain_two] + rel_rows + [jnp.zeros((5, width), F32)], axis=0)
    tail = gbst_bwd(
        cid, pool_w, mix, tokens, hidden_back, part_own, part_recv, gain_one, table_cat, raw, conv_taps, scorer, extra
    )
    left, right = two_ways(g_qkv, give, (X_SWAP + (tail,), Y_SWAP + (tail,)))
    tail = give(tail, "mp", 0)
    left = give(left, *Y_SWAP)
    right = give(right, *X_SWAP)
    tail = give(tail, *X_SWAP)
    both = give(jnp.concatenate([left, right], axis=1), *Z_NEAR)
    tail = give(tail, *Y_SWAP)
    both = give(both, *Z_FAR).astype(B16)
    tail = tail + hop(tail.astype(B16), *Z_NEAR).astype(F32)
    both = take(both, *Z_FAR)
    tail = (tail + hop(tail.astype(B16), *Z_FAR).astype(F32)).astype(B16)
    both = take(both, *Z_NEAR)
    cut = both.shape[1] // 2
    left, right = take(both[:, :cut], *Y_SWAP), take(both[:, cut:], *X_SWAP)
    tail = take(tail, *Y_SWAP)
    left, right = take(left, *X_SWAP), take(right, *Y_SWAP)
    tail = take(tail, *X_SWAP)
    tail = take(tail, "mp", 0).astype(F32)
    g_gate, g_up, g_down, g_out = unpack(large, ffn_width)
    g_qkv = jnp.concatenate([left, right], axis=1)
    g_query, g_key, g_value = (g_qkv[:, i * proj : (i + 1) * proj].astype(F32) for i in range(3))
    g_table, small, g_gain_two = tail[:CJ], tail[CJ : CJ + 7], tail[CJ + 8]
    g_rel = jnp.where(first, tail[CJ + 9], tail[CJ + 10])[: g_rel.size].reshape(g_rel.shape)

    layer_out = after(layer_out, tail).reshape(half, seq_count, width).astype(F32)
    return (
        layer_out, g_table[:vocab], small[:5], small[5], small[6], g_query, g_key, g_value, g_out, g_rel,
        g_gain_two, g_gate, g_up, g_down,
    )


def chosen(*args):
    ids, lengths, w_query, out_grad = args[0], args[1], args[6], args[15]
    seq_count = lax.axis_size("seq")
    total = out_grad.shape[0] * seq_count
    fits = (
        lengths.shape[0] == seq_count
        and lax.axis_size("mp") == 2
        and lax.axis_size("dp") == 4
        and seq_count == 4
        and total % (2 * TT) == 0
        and total % CK == 0
        and total % (CK * SUB) == 0
        and w_query.shape[1] % 128 == 0
        and w_query.shape[1] >= 256
        and args[12].shape[1] % FC == 0
        and args[2].shape[1] % 128 == 0
        and (total // (2 * seq_count)) % 32 == 0
        and (total // 2) % RT == 0
        and (ids.shape[0] // 2) % 12 == 0
    )
    return local_item(*args) if fits else local_general(*args)


def solution(mesh):
    return jax.shard_map(
        chosen,
        mesh=mesh,
        in_specs=(
            P("seq", "dp"),
            P("dp"),
            P(),
            P(),
            P(),
            P(),
            P(None, "mp"),
            P(None, "mp"),
            P(None, "mp"),
            P("mp", None),
            P(None, "mp"),
            P(),
            P(None, "mp"),
            P(None, "mp"),
            P("mp", None),
            P("seq", "dp", None),
        ),
        out_specs=(
            P(("seq", "mp"), "dp", None),
            P(),
            P(),
            P(),
            P(),
            P(None, "mp"),
            P(None, "mp"),
            P(None, "mp"),
            P("mp", None),
            P(None, "mp"),
            P(),
            P(None, "mp"),
            P(None, "mp"),
            P("mp", None),
        ),
        check_vma=False,
    )
```

```python
import functools

import jax
import jax.numpy as jnp
from jax import lax
from jax.experimental import pallas as pl
from jax.experimental.pallas import tpu as pltpu
from jax.sharding import PartitionSpec as P

DH = 64
BUCKETS = 32
MICRO = 4


EPS = 1e-06
NEG = -1000000000.0
EDGES = (12, 16, 23, 32, 46, 64, 91)
HIGH = lax.Precision.HIGHEST
F32 = jnp.float32
B16 = jnp.bfloat16


def extended(cells, sides, width):
    for axis, dim in sides:
        count = lax.axis_size(axis)
        ends = count - 1
        head = lax.slice_in_dim(cells, 0, width, axis=dim)
        tail = lax.slice_in_dim(cells, cells.shape[dim] - width, cells.shape[dim], axis=dim)
        cells = jnp.concatenate(
            [
                lax.ppermute(tail, axis, [(i, (i + 1) % count) for i in range(ends)]),
                cells,
                lax.ppermute(head, axis, [((i + 1) % count, i) for i in range(ends)]),
            ],
            axis=dim,
        )
    return cells


def for_sending(array):
    return jax.tree.map(lambda a: a.astype(jnp.bfloat16) if a.dtype == jnp.float32 else a, array)


def bucket_of(offset):
    distance = jnp.abs(offset)
    far = jnp.full(offset.shape, 8, jnp.int32)
    for edge in EDGES:
        far = far + (distance >= edge).astype(jnp.int32)
    near = jnp.where(distance < 8, distance, far)
    return near + 16 * (offset > 0).astype(jnp.int32)


def bias_onehot(query_places, key_places):
    offset = key_places[None, :] - query_places[:, None]
    return (bucket_of(offset)[:, :, None] == jnp.arange(BUCKETS, dtype=jnp.int32)).astype(F32)


def rms_norm(hidden, gain):
    return hidden * lax.rsqrt(jnp.mean(hidden * hidden, axis=-1, keepdims=True) + EPS) * gain


def activation(gate, up):
    return jax.nn.gelu(gate, approximate=True) * up


def gbst_tail(conv_out, scorer):
    byte_count, item_count, model_width = conv_out.shape
    weighted = jnp.einsum("pid,d->pi", conv_out, scorer, precision=HIGH)
    pooled_all = []
    scores_all = []
    for block_size in (1, 2, 3, 4):
        block_means = conv_out.reshape(
            byte_count // block_size, block_size, item_count, model_width
        ).mean(axis=1)
        pooled_all.append(jnp.repeat(block_means, block_size, axis=0))
        score_means = weighted.reshape(byte_count // block_size, block_size, item_count).mean(
            axis=1
        )
        scores_all.append(jnp.repeat(score_means, block_size, axis=0))
    mixing = jax.nn.softmax(jnp.stack(scores_all), axis=0)
    mixture = mixing[0][:, :, None] * pooled_all[0]
    for block_index in range(1, 4):
        mixture = mixture + mixing[block_index][:, :, None] * pooled_all[block_index]
    return mixture.reshape(byte_count // 2, 2, item_count, model_width).mean(axis=1)


def local_general(
    byte_ids,
    true_lengths,
    byte_table,
    conv_taps,
    block_scorer,
    attn_gain,
    w_query,
    w_key,
    w_value,
    w_output,
    rel_table,
    ffn_gain,
    w_gate,
    w_up,
    w_down,
    out_grad,
):
    seq_count = lax.axis_size("seq")
    seq_place = lax.axis_index("seq")
    core_place = lax.axis_index("mp")
    byte_rows = byte_ids.shape[0]
    tok_rows = byte_rows // 2
    half_rows = tok_rows // lax.axis_size("mp")
    total_tokens = tok_rows * seq_count
    item_count = byte_ids.shape[1] // MICRO
    proj_width = w_query.shape[1]
    head_count = proj_width // DH
    ffn_width = w_gate.shape[1]
    taps = conv_taps.astype(F32)
    scorer = block_scorer.astype(F32)
    gain_one = attn_gain.astype(F32)
    gain_two = ffn_gain.astype(F32)
    rel_local = rel_table.astype(F32)
    gate_up = jnp.concatenate([w_gate, w_up], axis=1)
    query_places = seq_place * tok_rows + jnp.arange(tok_rows, dtype=jnp.int32)
    key_places = jnp.arange(total_tokens, dtype=jnp.int32)
    onehot_bias = bias_onehot(query_places, key_places)
    bias = jnp.einsum("qkb,bh->hqk", onehot_bias, rel_local, precision=HIGH)
    byte_places = seq_place * byte_rows + jnp.arange(byte_rows, dtype=jnp.int32)
    vocab_range = jnp.arange(byte_table.shape[0], dtype=jnp.int32)
    sum_table = jnp.zeros(byte_table.shape, F32)
    sum_taps = jnp.zeros(conv_taps.shape, F32)
    sum_scorer = jnp.zeros(block_scorer.shape, F32)
    sum_gain_one = jnp.zeros(attn_gain.shape, F32)
    sum_query = jnp.zeros(w_query.shape, F32)
    sum_key = jnp.zeros(w_key.shape, F32)
    sum_value = jnp.zeros(w_value.shape, F32)
    sum_output = jnp.zeros(w_output.shape, F32)
    sum_rel = jnp.zeros(rel_table.shape, F32)
    sum_gain_two = jnp.zeros(ffn_gain.shape, F32)
    sum_gate = jnp.zeros(w_gate.shape, F32)
    sum_up = jnp.zeros(w_up.shape, F32)
    sum_down = jnp.zeros(w_down.shape, F32)
    outputs = []
    for micro in range(MICRO):
        first = micro * item_count
        ids_now = byte_ids[:, first : first + item_count]
        lengths = true_lengths[first : first + item_count]
        keep = (byte_places[:, None] < lengths[None, :]).astype(F32)
        onehot = (ids_now[:, :, None] == vocab_range).astype(F32) * keep[:, :, None]
        embedded = jnp.einsum(
            "piv,vd->pid", onehot.astype(B16), byte_table, preferred_element_type=F32
        ).astype(B16)
        framed = extended(embedded, (("seq", 0),), 2)
        conv_out = taps[0] * framed[0:byte_rows]
        for tap_index in range(1, 5):
            conv_out = conv_out + taps[tap_index] * framed[tap_index : tap_index + byte_rows]
        tokens, gbst_pull = jax.vjp(gbst_tail, conv_out, scorer)
        normed, norm_pull = jax.vjp(rms_norm, tokens, gain_one)
        normed_low = normed.astype(B16)
        query = jnp.einsum("qid,dh->qih", normed_low, w_query, preferred_element_type=F32).astype(
            B16
        )
        keys_here = jnp.einsum("qid,dh->qih", normed_low, w_key, preferred_element_type=F32).astype(
            B16
        )
        values_here = jnp.einsum(
            "qid,dh->qih", normed_low, w_value, preferred_element_type=F32
        ).astype(B16)
        keys_all, values_all = (
            lax.all_gather(keys_here, "seq", axis=0, tiled=True),
            lax.all_gather(values_here, "seq", axis=0, tiled=True),
        )
        query4 = query.reshape(tok_rows, item_count, head_count, DH)
        keys4 = keys_all.reshape(total_tokens, item_count, head_count, DH)
        values4 = values_all.reshape(total_tokens, item_count, head_count, DH)
        key_ok = 2 * key_places[None, :] < lengths[:, None]

        def scores_of():
            raw = jnp.einsum("qihe,kihe->ihqk", query4, keys4, preferred_element_type=F32)
            return jnp.where(key_ok[:, None, None, :], raw + bias[None], NEG)

        scores = scores_of()
        top = jnp.max(scores, axis=-1, keepdims=True)
        log_total = top + jnp.log(jnp.sum(jnp.exp(scores - top), axis=-1, keepdims=True))
        probs_low = jnp.exp(scores - log_total).astype(B16)
        attended = (
            jnp.einsum("ihqk,kihe->qihe", probs_low, values4, preferred_element_type=F32)
            .reshape(tok_rows, item_count, proj_width)
            .astype(B16)
        )
        attn_half = lax.psum_scatter(
            jnp.einsum("qih,hd->qid", attended, w_output, preferred_element_type=F32),
            "mp",
            scatter_dimension=0,
            tiled=True,
        )
        tokens_half = lax.dynamic_slice_in_dim(tokens, core_place * half_rows, half_rows, 0)
        hidden_half = tokens_half + attn_half
        normed_two, norm_two_pull = jax.vjp(rms_norm, hidden_half, gain_two)
        normed_full = lax.all_gather(normed_two.astype(B16), "mp", axis=0, tiled=True)
        projected = jnp.einsum("qid,df->qif", normed_full, gate_up, preferred_element_type=F32)
        inner, inner_pull = jax.vjp(
            activation, projected[..., :ffn_width], projected[..., ffn_width:]
        )
        inner_low = inner.astype(B16)
        ffn_half = lax.psum_scatter(
            jnp.einsum("qif,fd->qid", inner_low, w_down, preferred_element_type=F32).astype(
                jnp.bfloat16
            ),
            "mp",
            scatter_dimension=0,
            tiled=True,
        ).astype(jnp.float32)
        outputs.append(hidden_half + ffn_half)
        grad_low = out_grad[:, first : first + item_count]
        grad_half = lax.dynamic_slice_in_dim(grad_low, core_place * half_rows, half_rows, 0).astype(
            F32
        )
        sum_down = sum_down + jnp.einsum(
            "qif,qid->fd", inner_low, grad_low, preferred_element_type=F32
        )
        grad_inner = jnp.einsum("qid,fd->qif", grad_low, w_down, preferred_element_type=F32)
        gate_grad, up_grad = inner_pull(grad_inner)
        gate_low = gate_grad.astype(B16)
        up_low = up_grad.astype(B16)
        sum_gate = sum_gate + jnp.einsum(
            "qid,qif->df", normed_full, gate_low, preferred_element_type=F32
        )
        sum_up = sum_up + jnp.einsum("qid,qif->df", normed_full, up_low, preferred_element_type=F32)
        normed_two_grad = lax.psum_scatter(
            jnp.einsum("qif,df->qid", gate_low, w_gate, preferred_element_type=F32)
            + jnp.einsum("qif,df->qid", up_low, w_up, preferred_element_type=F32),
            "mp",
            scatter_dimension=0,
            tiled=True,
        )
        hidden_norm_grad, gain_two_grad = norm_two_pull(normed_two_grad)
        hidden_grad = grad_half + hidden_norm_grad
        hidden_full = lax.all_gather(for_sending(hidden_grad), "mp", axis=0, tiled=True).astype(
            hidden_grad.dtype
        )
        hidden_low = hidden_full.astype(B16)
        sum_output = sum_output + jnp.einsum(
            "qih,qid->hd", attended, hidden_low, preferred_element_type=F32
        )
        attended_grad = jnp.einsum(
            "qid,hd->qih", hidden_low, w_output, preferred_element_type=F32
        ).astype(B16)
        attended_grad4 = attended_grad.reshape(tok_rows, item_count, head_count, DH)
        scores = scores_of()
        probs = jnp.exp(scores - log_total)
        probs_low = probs.astype(B16)
        probs_grad = jnp.einsum(
            "qihe,kihe->ihqk", attended_grad4, values4, preferred_element_type=F32
        )
        inner_sum = jnp.sum(probs * probs_grad, axis=-1, keepdims=True)
        scores_grad = probs * (probs_grad - inner_sum)
        sum_rel = sum_rel + jnp.einsum(
            "qkb,hqk->bh", onehot_bias, jnp.sum(scores_grad, axis=0), precision=HIGH
        )
        scores_low = scores_grad.astype(B16)
        query_grad = (
            jnp.einsum("ihqk,kihe->qihe", scores_low, keys4, preferred_element_type=F32)
            .reshape(tok_rows, item_count, proj_width)
            .astype(B16)
        )
        key_part = jnp.einsum("ihqk,qihe->kihe", scores_low, query4, preferred_element_type=F32)
        value_part = jnp.einsum(
            "ihqk,qihe->kihe", probs_low, attended_grad4, preferred_element_type=F32
        )
        key_sums = lax.psum_scatter(
            jnp.concatenate(
                [
                    key_part.reshape(tok_rows * lax.axis_size("seq"), item_count, proj_width),
                    value_part.reshape(tok_rows * lax.axis_size("seq"), item_count, proj_width),
                ],
                axis=2,
            ).astype(jnp.bfloat16),
            "seq",
            scatter_dimension=0,
            tiled=True,
        ).astype(jnp.float32)
        keys_grad = key_sums[..., :proj_width].astype(B16)
        values_grad = key_sums[..., proj_width:].astype(B16)
        sum_query = sum_query + jnp.einsum(
            "qid,qih->dh", normed_low, query_grad, preferred_element_type=F32
        )
        sum_key = sum_key + jnp.einsum(
            "qid,qih->dh", normed_low, keys_grad, preferred_element_type=F32
        )
        sum_value = sum_value + jnp.einsum(
            "qid,qih->dh", normed_low, values_grad, preferred_element_type=F32
        )
        partial_grad = (
            jnp.einsum("qih,dh->qid", query_grad, w_query, preferred_element_type=F32)
            + jnp.einsum("qih,dh->qid", keys_grad, w_key, preferred_element_type=F32)
            + jnp.einsum("qih,dh->qid", values_grad, w_value, preferred_element_type=F32)
        )
        normed_grad, gain_two_total = (
            lax.psum(partial_grad.astype(jnp.bfloat16), "mp").astype(jnp.float32),
            lax.psum(gain_two_grad.astype(jnp.bfloat16), "mp").astype(jnp.float32),
        )
        sum_gain_two = sum_gain_two + gain_two_total
        tokens_norm_grad, gain_one_grad = norm_pull(normed_grad)
        sum_gain_one = sum_gain_one + gain_one_grad
        tokens_grad = hidden_full + tokens_norm_grad
        conv_grad, scorer_grad = gbst_pull(tokens_grad)
        sum_scorer = sum_scorer + scorer_grad
        framed_grad = extended(conv_grad.astype(jnp.bfloat16), (("seq", 0),), 2).astype(
            conv_grad.dtype
        )
        embedded_grad = taps[0] * framed_grad[4 : 4 + byte_rows]
        for tap_index in range(1, 5):
            embedded_grad = (
                embedded_grad
                + taps[tap_index] * framed_grad[4 - tap_index : 4 - tap_index + byte_rows]
            )
        tap_sums = [
            jnp.sum(conv_grad * framed[tap_index : tap_index + byte_rows], axis=(0, 1))
            for tap_index in range(5)
        ]
        sum_taps = sum_taps + jnp.stack(tap_sums)
        sum_table = sum_table + jnp.einsum("piv,pid->vd", onehot, embedded_grad, precision=HIGH)
    totals = lax.psum(
        (
            sum_table,
            sum_taps,
            sum_scorer,
            sum_gain_one,
            sum_query,
            sum_key,
            sum_value,
            sum_output,
            sum_rel,
            sum_gain_two,
            sum_gate,
            sum_up,
            sum_down,
        ),
        ("dp", "seq"),
    )
    layer_out = jnp.concatenate(outputs, axis=1)
    return (
        layer_out,
        totals[0],
        totals[1],
        totals[2],
        totals[3],
        totals[4],
        totals[5],
        totals[6],
        totals[7],
        totals[8],
        totals[9],
        totals[10],
        totals[11],
        totals[12],
    )


LOG2E = 1.4426950408889634
LN2 = 0.6931471805599453
NT = (((1,), (1,)), ((), ()))
NN = (((1,), (0,)), ((), ()))
CK = 256
SUB = 3

def dot(a, b, dims):
    return lax.dot_general(a, b, dims, preferred_element_type=F32)

def split3(x):
    hi = x.astype(B16)
    rest = x - hi.astype(F32)
    mid = rest.astype(B16)
    lo = (rest - mid.astype(F32)).astype(B16)
    return hi, mid, lo

def split3_xla(x):
    cut = lambda a: lax.reduce_precision(a, exponent_bits=8, mantissa_bits=7)
    hi = cut(x)
    mid = cut(x - hi)
    return hi.astype(B16), mid.astype(B16), (x - hi - mid).astype(B16)


def attn_fwd_body(limit_ref, q_ref, k_ref, v_ref, curve_ref, e_ref, o_ref, ot_ref, inv_ref,
                  kext, vext, table, qext, norms):
    total = k_ref.shape[0]
    tq = CK
    chunks = total // CK
    step = pl.program_id(1)

    @pl.when(step == 0)
    def _():
        lane = lax.broadcasted_iota(jnp.int32, (total, 128), 1)
        place = lax.broadcasted_iota(jnp.int32, (total, 128), 0)
        masked = jnp.where(place < limit_ref[0], 0.0, -1e9).astype(F32)
        k = k_ref[...].astype(F32)
        q = q_ref[...].astype(F32)
        pick = lax.broadcasted_iota(jnp.int32, (128, 128), 0) // 64 == lax.broadcasted_iota(jnp.int32, (128, 128), 1)
        pick = jnp.where(pick, 1.0, 0.0).astype(B16)
        size_q = jnp.max(dot((q * q).astype(B16), pick, NN), axis=0, keepdims=True)
        size_k = jnp.max(dot((k * k).astype(B16), pick, NN), axis=0, keepdims=True)
        both = size_q * size_k
        vt = v_ref[...].T
        for h in range(2):
            norms[h] = jnp.max(both[:, h : h + 1])
            own = (lane < 64) if h == 0 else (lane >= 64)
            base = 64 if h == 0 else 0
            extra = jnp.where(lane == base, masked, jnp.where((lane > base) & (lane < base + 4), 1.0, 0.0))
            kext[h] = jnp.where(own, k, extra).astype(B16)
            vext[h, 0:64, :] = vt[64 * h : 64 * h + 64, :]
            vext[h, 64:80, :] = jnp.ones((16, total), B16)
            curve = curve_ref[h : h + 1, :]
            for g in range(5):
                lo = 1024 + 2 * CK - g * CK - 256
                if g in (0, 4):
                    table[h, g * CK : (g + 1) * CK, :] = jnp.broadcast_to(curve[:, lo : lo + 1], (CK, CK))
                else:
                    window = jnp.broadcast_to(curve[:, lo : lo + 512], (CK, 512))
                    rolled = pltpu.roll(window, 0, 1, stride=1, stride_axis=0)
                    table[h, g * CK : (g + 1) * CK, :] = rolled[:, 256:512]

    lane_q = lax.broadcasted_iota(jnp.int32, (tq, 128), 1)

    def scores(h, u, c):
        d = jnp.clip(c - (step * SUB + u), -2, 2) + 2
        k_now = kext[h, pl.ds(c * CK if isinstance(c, int) else pl.multiple_of(c * CK, CK), CK), :]
        return dot(k_now, qext[u, h], NT) * LOG2E + table[h, pl.ds(pl.multiple_of(d * CK, CK), CK), :]

    for u in range(SUB):
        q = q_ref[pl.ds(pl.multiple_of((step * SUB + u) * tq, tq), tq), :]
        for h in range(2):
            own = (lane_q < 64) if h == 0 else (lane_q >= 64)
            base = 64 if h == 0 else 0
            qext[u, h] = jnp.where(own, q, jnp.where(lane_q == base, 1.0, 0.0).astype(B16))

    for h in range(2):
        @pl.when(norms[h] > 48.0 * 48.0)
        def _(h=h):
            own = (lane_q < 64) if h == 0 else (lane_q >= 64)
            base = 64 if h == 0 else 0

            def settle(u, carry):
                def grow(c, top):
                    return jnp.maximum(top, jnp.max(scores(h, u, c), axis=0, keepdims=True))
                top = lax.fori_loop(0, chunks, grow, jnp.full((1, tq), -3e38, F32))
                hi, mid, lo = split3(-jnp.broadcast_to(top * LN2, (128, tq)).T)
                extra = jnp.where(lane_q == base, jnp.ones_like(hi), jnp.zeros_like(hi))
                for at, part in ((1, hi), (2, mid), (3, lo)):
                    extra = jnp.where(lane_q == base + at, part, extra)
                qext[u, h] = jnp.where(own, qext[u, h], extra)
                return carry
            lax.fori_loop(0, SUB, settle, 0)

    for u in range(SUB):
        cols = slice(u * tq, (u + 1) * tq)
        for h in range(2):
            for c in range(chunks):
                e_ref[h, c * CK : (c + 1) * CK, cols] = jnp.exp2(scores(h, u, c)).astype(B16)
        outs = []
        for h in range(2):
            sums = dot(vext[h], e_ref[h, :, cols], NN)
            inv = 1.0 / sums[64:65, :]
            inv_ref[h : h + 1, cols] = inv
            outs.append(sums[0:64, :] * inv)
        out = jnp.concatenate(outs, axis=0)
        ot_ref[:, cols] = out
        o_ref[cols, :] = out.astype(B16).T

def attn_fwd(limit, qkv, curve):
    total = qkv.shape[0]
    pairs = qkv.shape[1] // 3 // 128
    tq = CK
    full = lambda off: pl.BlockSpec((total, 128), lambda p, i, s: (0, off + p))
    spec = pltpu.PrefetchScalarGridSpec(
        num_scalar_prefetch=1, grid=(pairs, total // (tq * SUB)),
        in_specs=[full(0), full(pairs), full(2 * pairs), pl.BlockSpec((None, 2, 2048), lambda p, i, s: (p, 0, 0))],
        out_specs=[
            pl.BlockSpec((2, total, SUB * tq), lambda p, i, s: (p, 0, i)),
            pl.BlockSpec((SUB * tq, 128), lambda p, i, s: (i, p)),
            pl.BlockSpec((128, SUB * tq), lambda p, i, s: (p, i)),
            pl.BlockSpec((None, 2, SUB * tq), lambda p, i, s: (p, 0, i)),
        ],
        scratch_shapes=[
            pltpu.VMEM((2, total, 128), B16), pltpu.VMEM((2, 80, total), B16),
            pltpu.VMEM((2, 5 * CK, tq), F32), pltpu.VMEM((SUB, 2, tq, 128), B16),
            pltpu.SMEM((2,), F32),
        ])
    n = 2 * pairs * total * total
    return pl.pallas_call(
        attn_fwd_body, grid_spec=spec, name="attn_fwd",
        out_shape=[jax.ShapeDtypeStruct((2 * pairs, total, total), B16),
                   jax.ShapeDtypeStruct((total, 128 * pairs), B16),
                   jax.ShapeDtypeStruct((128 * pairs, total), F32),
                   jax.ShapeDtypeStruct((pairs, 2, total), F32)],
        compiler_params=pltpu.CompilerParams(vmem_limit_bytes=56 << 20, dimension_semantics=("arbitrary", "arbitrary")),
        cost_estimate=pl.CostEstimate(flops=4 * 64 * n, transcendentals=n, bytes_accessed=2 * n),
    )(limit, qkv, qkv, qkv, curve)

def attn_bwd_body(e_ref, k_ref, v_ref, q_ref, do_ref, ot_ref, inv_ref,
                  dk_ref, dv_ref, dqo_ref, near_ref, far_ref,
                  doe, dop, qind, ds, band, dq_ref):
    total = q_ref.shape[0]
    ck = k_ref.shape[0]
    blocks = total // CK
    chunks = pl.num_programs(1)
    step = pl.program_id(1)

    @pl.when(step == 0)
    def _():
        parts = []
        dt = do_ref[...].T
        row = lax.broadcasted_iota(jnp.int32, (64, total), 0)
        for h in range(2):
            at = slice(64 * h, 64 * h + 64)
            part = (dt[at].astype(F32) * inv_ref[h : h + 1, :]).astype(B16)
            parts.append(part)
            inner = -jnp.sum(part.astype(F32) * ot_ref[at, :], axis=0, keepdims=True)
            hi, mid, lo = split3(jnp.broadcast_to(inner, (64, total)))
            extra = jnp.where(row == 0, hi, jnp.where(row == 1, mid, jnp.where(row == 2, lo, jnp.zeros_like(hi))))
            doe[h, 64 * h : 64 * h + 64, :] = part
            doe[h, 64 - 64 * h : 128 - 64 * h, :] = extra
            lane = lax.broadcasted_iota(jnp.int32, (total, 128), 1)
            own = (lane < 64) if h == 0 else (lane >= 64)
            base = 64 if h == 0 else 0
            at128 = lax.broadcasted_iota(jnp.int32, (total, 128), 0) >> 7
            qind[h] = jnp.where(own, q_ref[...], jnp.where(lane - base == at128, 1.0, 0.0).astype(B16))
        dop[...] = jnp.concatenate(parts, axis=0).T
        dq_ref[...] = jnp.zeros_like(dq_ref)
        band[...] = jnp.zeros_like(band)
        far_ref[...] = jnp.zeros_like(far_ref)

    lane = lax.broadcasted_iota(jnp.int32, (ck, 128), 1)
    v = v_ref[...]
    kt = k_ref[...].T
    for h in range(2):
        own = (lane < 64) if h == 0 else (lane >= 64)
        base = 64 if h == 0 else 0
        ones = jnp.where((lane >= base) & (lane < base + 3), 1.0, 0.0).astype(B16)
        vx = jnp.where(own, v, ones)
        for c in range(blocks):
            cols = slice(c * CK, (c + 1) * CK)
            pg = dot(vx, doe[h, :, cols], NN)
            ds[h, :, cols] = e_ref[h, :, cols] * pg.astype(B16)
    block = lax.broadcasted_iota(jnp.int32, (1, 128), 1)
    dvs, dks = [], []
    for h in range(2):
        at = slice(64 * h, 64 * h + 64)
        base = 64 if h == 0 else 0
        dvs.append(dot(e_ref[h], dop[...], NN))
        dk = dot(ds[h], qind[h], NN)
        dks.append(dk)
        dq_ref[at, :] += dot(kt[at], ds[h], NN)
        for u in range(SUB):
            kb = step * SUB + u
            rows = slice(u * CK, (u + 1) * CK)
            sums_u = jnp.sum(dk[rows], axis=0, keepdims=True)
            spot = block - base
            inside = (spot >= 0) & (spot < total // 128)
            far_ref[h, 0:1, :] += jnp.where(inside & (spot < 2 * kb - 1), sums_u, 0.0)
            far_ref[h, 1:2, :] += jnp.where(inside & (spot >= 2 * kb + 3), sums_u, 0.0)
            band[h, :, 128 : 128 + CK] += ds[h, rows, pl.ds(pl.multiple_of(kb * CK, CK), CK)].astype(F32)

            @pl.when(kb > 0)
            def _(h=h, kb=kb, rows=rows):
                band[h, :, 0:128] += ds[h, rows, pl.ds(pl.multiple_of(kb * CK - 128, 128), 128)].astype(F32)

            @pl.when(kb < blocks - 1)
            def _(h=h, kb=kb, rows=rows):
                band[h, :, 128 + CK : 256 + CK] += ds[h, rows, pl.ds(pl.multiple_of(kb * CK + CK, 128), 128)].astype(F32)

    dk_ref[...] = jnp.where(lane < 64, dks[0], dks[1]).astype(B16).T
    dv_ref[...] = jnp.where(lane < 64, dvs[0], dvs[1]).astype(B16).T

    @pl.when(step == chunks - 1)
    def _():
        dqo_ref[...] = dq_ref[...].astype(B16)
        width = CK + 256
        row = lax.broadcasted_iota(jnp.int32, (CK, width), 0)
        col = lax.broadcasted_iota(jnp.int32, (CK, width), 1)
        offset = row - col + 128
        for h in range(2):
            all_now = band[h]
            near = jnp.where(jnp.abs(offset) < 128, all_now, 0.0)
            folded = near[0:8, :]
            for g in range(1, CK // 8):
                folded = folded + pltpu.roll(near[8 * g : 8 * g + 8, :], width - 8 * g, 1)
            line = folded[0:1, :]
            for g in range(1, 8):
                line = line + pltpu.roll(folded[g : g + 1, :], width - g, 1)
            near_ref[h, 0:1, :] = line
            near_ref[h, 1:2, :] = jnp.sum(jnp.where(offset >= 128, all_now, 0.0), axis=0, keepdims=True)
            near_ref[h, 2:3, :] = jnp.sum(jnp.where(offset <= -128, all_now, 0.0), axis=0, keepdims=True)
            near_ref[h, 3:8, :] = jnp.zeros((5, width), F32)

def attn_bwd(e, qkv, d_att, att_t, inv, start, count):
    total = qkv.shape[0]
    pairs = qkv.shape[1] // 3 // 128
    ck = CK * SUB
    full = pl.BlockSpec((total, 128), lambda p, i: (0, start + p))
    part = lambda off: pl.BlockSpec((ck, 128), lambda p, i: (i, off + start + p))
    flat = pl.BlockSpec((128, ck), lambda p, i: (p, i))
    tall = pl.BlockSpec((128, total), lambda p, i: (p, 0))
    n = 2 * count * total * total
    return pl.pallas_call(
        attn_bwd_body, grid=(count, total // ck), name="attn_bwd",
        in_specs=[pl.BlockSpec((2, ck, total), lambda p, i: (start + p, i, 0)), part(pairs), part(2 * pairs),
                  full, full, pl.BlockSpec((128, total), lambda p, i: (start + p, 0)),
                  pl.BlockSpec((None, 2, total), lambda p, i: (start + p, 0, 0))],
        out_specs=[flat, flat, tall,
                   pl.BlockSpec((2, 8, CK + 256), lambda p, i: (p, 0, 0)),
                   pl.BlockSpec((2, 8, 128), lambda p, i: (p, 0, 0))],
        out_shape=[jax.ShapeDtypeStruct((128 * count, total), B16)] * 3
        + [jax.ShapeDtypeStruct((2 * count, 8, CK + 256), F32), jax.ShapeDtypeStruct((2 * count, 8, 128), F32)],
        scratch_shapes=[
            pltpu.VMEM((2, 128, total), B16), pltpu.VMEM((total, 128), B16), pltpu.VMEM((2, total, 128), B16),
            pltpu.VMEM((2, ck, total), B16), pltpu.VMEM((2, CK, CK + 256), F32), pltpu.VMEM((128, total), F32),
        ],
        compiler_params=pltpu.CompilerParams(vmem_limit_bytes=60 << 20, dimension_semantics=("arbitrary", "arbitrary")),
        cost_estimate=pl.CostEstimate(flops=8 * 64 * n, transcendentals=0, bytes_accessed=2 * n),
    )(e, qkv, qkv, qkv, d_att, att_t, inv)

def bias_curve(rel, heads):
    offset = 1024 - jnp.arange(2048, dtype=jnp.int32)
    onehot = (bucket_of(offset)[:, None] == jnp.arange(32, dtype=jnp.int32)).astype(F32)
    curve = jnp.einsum("xb,bh->hx", onehot, rel.astype(F32) * LOG2E, precision=lax.Precision.HIGHEST)
    return curve.reshape(heads // 2, 2, 2048)

def rel_grad(near, far, width):
    x = jnp.arange(width, dtype=jnp.int32)
    onehot = (bucket_of(128 - x)[:, None] == jnp.arange(32, dtype=jnp.int32)).astype(F32)
    onehot = onehot * (x[:, None] < 256)
    g = jnp.einsum("hx,xb->bh", near[:, 0, :], onehot, precision=lax.Precision.HIGHEST)
    up = jnp.sum(near[:, 1, :], axis=1) + jnp.sum(far[:, 0], axis=1)
    down = jnp.sum(near[:, 2, :], axis=1) + jnp.sum(far[:, 1], axis=1)
    slot = jnp.arange(32)[:, None]
    return g + jnp.where(slot == 31, up[None], 0.0) + jnp.where(slot == 15, down[None], 0.0)

CJ = 272
CC = 1408
TT = 384

def means_of(even, odd):
    t = lax.broadcasted_iota(jnp.int32, even.shape, 1)
    width = even.shape[1]
    prev = lambda x: pltpu.roll(x, 1, 1)
    succ = lambda x: pltpu.roll(x, width - 1, 1)
    two = even + odd
    four = two + jnp.where(t % 2 == 0, succ(two), prev(two))
    place = t - 3 * ((t * 21846) >> 16)
    first = two + succ(even)
    middle_e = prev(two) + even
    middle_o = odd + succ(two)
    last = prev(odd) + two
    three_e = jnp.where(place == 0, first, jnp.where(place == 1, middle_e, last))
    three_o = jnp.where(place == 0, first, jnp.where(place == 1, middle_o, last))
    third = 1.0 / 3.0
    return [(even, odd), (two * 0.5, two * 0.5), (three_e * third, three_o * third), (four * 0.25, four * 0.25)]

def masks():
    t = lax.broadcasted_iota(jnp.int32, (TT, 1), 0)
    p = lax.broadcasted_iota(jnp.int32, (1, 2 * TT), 1)
    par = p >= TT
    tp = jnp.where(par, p - TT, p)
    third = lambda x: (x * 21846) >> 16
    blk = third(2 * tp + jnp.where(par, 1, 0))
    even = t == jnp.where(par, -1, tp)
    odd = t == jnp.where(par, tp, -1)
    return even, odd, (t >> 1) == (tp >> 1), third(2 * t) == blk, third(2 * t + 1) == blk


def fill_onehot(ids_ref, oht):
    row = lax.broadcasted_iota(jnp.int32, (CJ, TT), 0)
    for j in range(5):
        for side in range(2):
            hit = row == ids_ref[j + side : j + side + 1, :]
            oht[CJ * j : CJ * (j + 1), TT * side : TT * (side + 1)] = jnp.where(hit, 1.0, 0.0).astype(B16)
    oht[5 * CJ :, :] = jnp.zeros((CC - 5 * CJ, 2 * TT), B16)

def gbst_fwd_body(cid_ref, raw_ref, taps_ref, scorer_ref, gain_ref, tok_ref, norm_ref, w_ref, mix_ref, table_ref,
                  oht, rest, tvec, both, wide):
    @pl.when(pl.program_id(0) == 0)
    def _():
        raw = raw_ref[...].astype(F32)
        for j in range(5):
            at = slice(CJ * j, CJ * (j + 1))
            tap = taps_ref[j : j + 1, :].astype(F32)
            cat = raw * tap
            hi = cat.astype(B16)
            table_ref[at, :] = hi
            rest[at, :] = (cat - hi.astype(F32)).astype(B16)
            parts = split3(jnp.broadcast_to(tap * scorer_ref[...].astype(F32), (16, cat.shape[1])))
            which = lax.broadcasted_iota(jnp.int32, (16, cat.shape[1]), 0)
            zero = jnp.zeros_like(parts[0])
            rows = jnp.where(which == 0, parts[0], jnp.where(which == 1, parts[1], jnp.where(which == 2, parts[2], zero)))
            scores = dot(rows, raw_ref[...], NT)
            line = split3(jnp.broadcast_to(scores[0:1] + scores[1:2] + scores[2:3], (16, CJ)))
            which = lax.broadcasted_iota(jnp.int32, (16, CJ), 0)
            zero = jnp.zeros_like(line[0])
            tvec[j] = jnp.where(which == 0, line[0], jnp.where(which == 1, line[1], jnp.where(which == 2, line[2], zero)))
        table_ref[5 * CJ :, :] = jnp.zeros((CC - 5 * CJ, table_ref.shape[1]), B16)
        rest[5 * CJ :, :] = jnp.zeros((CC - 5 * CJ, table_ref.shape[1]), B16)
    fill_onehot(cid_ref, oht)
    parts = dot(tvec[0], oht[0:CJ, :], NN)
    for j in range(1, 5):
        parts = parts + dot(tvec[j], oht[CJ * j : CJ * (j + 1), :], NN)
    weighted = parts[0:1] + parts[1:2] + parts[2:3]
    scores = means_of(weighted[:, :TT], weighted[:, TT:])
    rows = []
    for side in range(2):
        mine = [s[side] for s in scores]
        top = jnp.maximum(jnp.maximum(mine[0], mine[1]), jnp.maximum(mine[2], mine[3]))
        e = [jnp.exp(s - top) for s in mine]
        inv = 1.0 / (e[0] + e[1] + e[2] + e[3])
        rows.append([x * inv for x in e])
    mix = jnp.concatenate([rows[side][b] for b in range(4) for side in range(2)], axis=0)
    mix_ref[...] = mix
    col = mix.T
    c = lambda i: col[:, i : i + 1]
    even, odd, pair, tri_e, tri_o = masks()
    two = 0.25 * (c(2) + c(3))
    w = jnp.where(even, 0.5 * c(0) + two, jnp.where(odd, 0.5 * c(1) + two, 0.0))
    w = w + jnp.where(pair, 0.125 * (c(6) + c(7)), 0.0)
    w = w + jnp.where(tri_e, c(4) * (1.0 / 6.0), 0.0) + jnp.where(tri_o, c(5) * (1.0 / 6.0), 0.0)
    w_hi = w.astype(B16)
    w_lo = (w - w_hi.astype(F32)).astype(B16)
    w_ref[...] = w_hi
    both[0:TT, :] = w_hi
    both[TT:, :] = w_lo
    a = dot(both[...], oht[...], NT)
    a = a[0:TT] + a[TT:]
    a_hi = a.astype(B16)
    wide[0:TT, :] = a_hi
    wide[TT:, :] = (a - a_hi.astype(F32)).astype(B16)
    tokens = dot(wide[...], table_ref[...], NN)
    tokens = tokens[0:TT] + tokens[TT:] + dot(a_hi, rest[...], NN)
    tok_ref[...] = tokens
    r = lax.rsqrt(jnp.mean(tokens * tokens, axis=1, keepdims=True) + EPS)
    norm_ref[...] = (tokens * r * gain_ref[...].astype(F32)).astype(B16)

def gbst_fwd(cid, raw, taps, scorer, gain):
    tiles = cid.shape[0]
    d = raw.shape[1]
    rows = tiles * TT
    const = lambda shape: pl.BlockSpec(shape, lambda i: (0,) * len(shape))
    return pl.pallas_call(
        gbst_fwd_body, grid=(tiles,), name="gbst_fwd",
        in_specs=[pl.BlockSpec((None, 8, TT), lambda i: (i, 0, 0)), const((CJ, d)), const((5, d)), const((1, d)), const((1, d))],
        out_specs=[pl.BlockSpec((TT, d), lambda i: (i, 0)), pl.BlockSpec((TT, d), lambda i: (i, 0)),
                   pl.BlockSpec((TT, 2 * TT), lambda i: (i, 0)), pl.BlockSpec((None, 8, TT), lambda i: (i, 0, 0)),
                   const((CC, d))],
        out_shape=[jax.ShapeDtypeStruct((rows, d), F32), jax.ShapeDtypeStruct((rows, d), B16),
                   jax.ShapeDtypeStruct((rows, 2 * TT), B16), jax.ShapeDtypeStruct((tiles, 8, TT), F32),
                   jax.ShapeDtypeStruct((CC, d), B16)],
        scratch_shapes=[pltpu.VMEM((CC, 2 * TT), B16), pltpu.VMEM((CC, d), B16), pltpu.VMEM((5, 16, CJ), B16),
                        pltpu.VMEM((2 * TT, 2 * TT), B16), pltpu.VMEM((2 * TT, CC), B16)],
        compiler_params=pltpu.CompilerParams(vmem_limit_bytes=56 << 20),
        cost_estimate=pl.CostEstimate(flops=rows * CC * d * 8, transcendentals=0, bytes_accessed=rows * d * 8),
    )(cid, raw, taps, scorer, gain)

def gbst_bwd_body(cid_ref, w_ref, mix_ref, tok_ref, hid_ref, nb_ref, nr_ref, gain_ref, table_ref, raw_ref, taps_ref, scorer_ref,
                  extra_ref, gt_ref, small_ref, oht, big, usum):
    i = pl.program_id(0)
    fill_onehot(cid_ref, oht)

    @pl.when(i == 0)
    def _():
        big[...] = jnp.zeros_like(big)
        usum[...] = jnp.zeros_like(usum)
        small_ref[...] = jnp.zeros_like(small_ref)
    x = tok_ref[...]
    n = nb_ref[...].astype(F32) + nr_ref[...].astype(F32)
    r = lax.rsqrt(jnp.mean(x * x, axis=1, keepdims=True) + EPS)
    u = n * gain_ref[...].astype(F32)
    xr = x * r
    g = hid_ref[...].astype(F32) + r * (u - xr * jnp.mean(u * xr, axis=1, keepdims=True))
    small_ref[6:7, :] += jnp.sum(n * xr, axis=0, keepdims=True)
    gb = g.astype(B16)
    hh = dot(gb, table_ref[...], NT).astype(B16)
    gram = dot(hh, oht[...], NN)
    even, odd, pair, tri_e, tri_o = masks()
    lanesum = lambda m: jnp.sum(jnp.where(m, gram, 0.0), axis=1, keepdims=True)
    me = 0.5 * lanesum(even)
    mo = 0.5 * lanesum(odd)
    m2 = 0.5 * (me + mo)
    m4 = 0.125 * lanesum(pair)
    m3e = lanesum(tri_e) * (1.0 / 6.0)
    m3o = lanesum(tri_o) * (1.0 / 6.0)
    lane8 = lax.broadcasted_iota(jnp.int32, (TT, 128), 1)
    cols = jnp.zeros((TT, 128), F32)
    for k, v in enumerate((me, mo, m2, m2, m3e, m3o, m4, m4)):
        cols = jnp.where(lane8 == k, v, cols)
    dmix = cols.T[0:8, :]
    mix = mix_ref[...]
    row = lambda a, k: a[k : k + 1, :]
    sides = []
    for side in range(2):
        inner = sum(row(mix, 2 * b + side) * row(dmix, 2 * b + side) for b in range(4))
        sides.append([row(mix, 2 * b + side) * (row(dmix, 2 * b + side) - inner) for b in range(4)])
    dwe = jnp.zeros((1, TT), F32)
    dwo = jnp.zeros((1, TT), F32)
    for b in range(4):
        e, o = means_of(sides[0][b], sides[1][b])[b]
        dwe = dwe + e
        dwo = dwo + o
    dw = jnp.concatenate([dwe, dwo], axis=1)
    hi, mid, lo = split3(jnp.broadcast_to(dw, (16, 2 * TT)))
    which = lax.broadcasted_iota(jnp.int32, (16, 2 * TT), 0)
    dw3 = jnp.where(which == 0, hi, jnp.where(which == 1, mid, jnp.where(which == 2, lo, jnp.zeros_like(hi))))
    usum[...] += dot(dw3, oht[...], NT)
    at = dot(oht[...], w_ref[...], NT).astype(B16)
    big[...] += dot(at, gb, NN)

    @pl.when(i == pl.num_programs(0) - 1)
    def _():
        us = usum[...]
        urow = us[0:1] + us[1:2] + us[2:3]
        hi, mid, lo = split3(jnp.broadcast_to(urow, (16, CC)))
        which = lax.broadcasted_iota(jnp.int32, (16, CC), 0)
        u3 = jnp.where(which == 0, hi, jnp.where(which == 1, mid, jnp.where(which == 2, lo, jnp.zeros_like(hi))))
        gs = dot(u3, table_ref[...], NN)
        small_ref[5:6, :] = gs[0:1] + gs[1:2] + gs[2:3]
        ucol = jnp.broadcast_to(urow, (128, CC)).T[:, 0:1]
        total = jnp.zeros((CJ, gt_ref.shape[1]), F32)
        for j in range(5):
            m = big[CJ * j : CJ * (j + 1), :] + ucol[CJ * j : CJ * (j + 1)] * scorer_ref[...].astype(F32)
            total = total + m * taps_ref[j : j + 1, :].astype(F32)
            small_ref[j : j + 1, :] = jnp.sum(m * raw_ref[...].astype(F32), axis=0, keepdims=True)
        gt_ref[0:CJ, :] = total
        gt_ref[CJ : CJ + 8, :] = small_ref[...]
        gt_ref[CJ + 8 :, :] = extra_ref[...]

def gbst_bwd(cid, w, mix, tok, hid, nb, nr, gain, table, raw, taps, scorer, extra):
    tiles = cid.shape[0]
    d = table.shape[1]
    rows = tiles * TT
    const = lambda shape: pl.BlockSpec(shape, lambda i: (0,) * len(shape))
    tile = lambda width: pl.BlockSpec((TT, width), lambda i: (i, 0))
    return pl.pallas_call(
        gbst_bwd_body, grid=(tiles,), name="gbst_bwd",
        in_specs=[pl.BlockSpec((None, 8, TT), lambda i: (i, 0, 0)), tile(2 * TT), pl.BlockSpec((None, 8, TT), lambda i: (i, 0, 0)),
                  tile(d), tile(d), tile(d), tile(d), const((1, d)), const((CC, d)), const((CJ, d)), const((5, d)), const((1, d)), const((8, d))],
        out_specs=const((CJ + 16, d)),
        out_shape=jax.ShapeDtypeStruct((CJ + 16, d), F32),
        scratch_shapes=[pltpu.VMEM((8, d), F32), pltpu.VMEM((CC, 2 * TT), B16), pltpu.VMEM((CC, d), F32), pltpu.VMEM((16, CC), F32)],
        compiler_params=pltpu.CompilerParams(vmem_limit_bytes=56 << 20),
        cost_estimate=pl.CostEstimate(flops=rows * CC * d * 8, transcendentals=0, bytes_accessed=rows * d * 12),
    )(cid, w, mix, tok, hid, nb, nr, gain, table, raw, taps, scorer, extra)


FC = 512
RT = 288


def middle_body(tok_ref, ao_ref, ar_ref, woo_ref, wor_ref, wgo_ref, wgr_ref, wuo_ref, wur_ref, wdo_ref, wdr_ref,
                og_ref, gain_ref,
                layer_ref, back_ref, down_ref, dsend_ref, goo_ref, gor_ref, ggo_ref, guo_ref, gdo_ref, ggr_ref, gur_ref, gdr_ref,
                gain_out,
                hid, n2, n2t, ogt, outs, n2b, wg, wu, wd, inner_s, gb_s, ub_s):
    i = pl.program_id(0)
    steps = pl.num_programs(0)
    rows = tok_ref.shape[0]
    tiles = [slice(r, r + RT) for r in range(0, rows, RT)]
    gain = gain_ref[...].astype(F32)

    @pl.when(i == 0)
    def _():
        for at in tiles:
            h = tok_ref[at, :] + dot(ao_ref[at, :], woo_ref[...], NN) + dot(ar_ref[at, :], wor_ref[...], NN)
            hid[at, :] = h
            r = lax.rsqrt(jnp.mean(h * h, axis=1, keepdims=True) + EPS)
            n2[at, :] = (h * r * gain).astype(B16)
            outs[at, :] = h
            n2b[at, :] = jnp.zeros((RT, h.shape[1]), F32)
        n2t[...] = n2[...].T
        ogt[...] = og_ref[...].T

    @pl.when(i < steps // 2)
    def _():
        wg[...] = wgo_ref[...]
        wu[...] = wuo_ref[...]
        wd[...] = wdo_ref[...]

    @pl.when(i >= steps // 2)
    def _():
        wg[...] = wgr_ref[...]
        wu[...] = wur_ref[...]
        wd[...] = wdr_ref[...]

    for at in tiles:
        x = n2[at, :]
        gate = dot(x, wg[...], NN)
        up = dot(x, wu[...], NN)
        gi = dot(og_ref[at, :], wd[...], NT)
        act, slope = gelu_parts(gate)
        inner = (act * up).astype(B16)
        gb = (gi * up * slope).astype(B16)
        ub = (gi * act).astype(B16)
        inner_s[at, :] = inner
        gb_s[at, :] = gb
        ub_s[at, :] = ub
        outs[at, :] += dot(inner, wd[...], NN)
        n2b[at, :] += dot(gb, wg[...], NT) + dot(ub, wu[...], NT)
    pieces = [dot(n2t[...], gb_s[...], NN), dot(n2t[...], ub_s[...], NN), dot(ogt[...], inner_s[...], NN)]
    pieces = [x.astype(B16) for x in pieces]

    @pl.when(i < steps // 2)
    def _():
        for ref, x in zip((ggo_ref, guo_ref, gdo_ref), pieces):
            ref[...] = x

    @pl.when(i >= steps // 2)
    def _():
        for ref, x in zip((ggr_ref, gur_ref, gdr_ref), pieces):
            ref[...] = x

    @pl.when(i == steps - 1)
    def _():
        total = jnp.zeros(gain.shape, F32)
        for at in tiles:
            h = hid[at, :]
            layer_ref[at, :] = outs[at, :].astype(B16)
            r = lax.rsqrt(jnp.mean(h * h, axis=1, keepdims=True) + EPS)
            back = n2b[at, :]
            u = back * gain
            hr = h * r
            total = total + jnp.sum(back * hr, axis=0, keepdims=True)
            hb = og_ref[at, :].astype(F32) + r * (u - hr * jnp.mean(u * hr, axis=1, keepdims=True))
            back_ref[at, :] = hb
            low = hb.astype(B16)
            n2[at, :] = low
            down_ref[at, :] = dot(low, woo_ref[...], NT).astype(B16)
            dsend_ref[at, :] = dot(low, wor_ref[...], NT).astype(B16)
        gain_out[...] = total
        n2t[...] = n2[...].T
        goo_ref[...] = dot(n2t[...], ao_ref[...], NN).astype(B16)
        gor_ref[...] = dot(n2t[...], ar_ref[...], NN).astype(B16)


def middle(tok, att_own, att_recv, wo, wo_other, wg, wg_other, wu, wu_other, wd, wd_other, og, gain):
    rows, d = tok.shape
    proj = att_own.shape[1]
    ffn = wg.shape[1]
    half = ffn // FC
    const = lambda *shape: pl.BlockSpec(shape, lambda i: (0,) * len(shape))
    once = lambda *shape: pl.BlockSpec(shape, lambda i: (0,) * len(shape), pipeline_mode=pl.Buffered(1))
    low = lambda i: jnp.minimum(i, half - 1)
    high = lambda i: jnp.maximum(i - half, 0)
    wide = lambda f: pl.BlockSpec((d, FC), lambda i: (0, f(i)))
    tall = lambda f: pl.BlockSpec((FC, d), lambda i: (f(i), 0))
    sds = jax.ShapeDtypeStruct
    flops = 2 * rows * d * (8 * 2 * ffn + 6 * proj) * 9 // 8
    return pl.pallas_call(
        middle_body, grid=(2 * half,), name="middle",
        in_specs=[once(rows, d), once(rows, proj), once(rows, proj), once(proj, d), once(proj, d),
                  wide(low), wide(high), wide(low), wide(high), tall(low), tall(high), once(rows, d), const(1, d)],
        out_specs=[once(rows, d), once(rows, d), once(rows, proj), once(rows, proj), once(d, proj), once(d, proj),
                   wide(low), wide(low), wide(low), wide(high), wide(high), wide(high), const(1, d)],
        out_shape=[sds((rows, d), B16), sds((rows, d), F32), sds((rows, proj), B16), sds((rows, proj), B16),
                   sds((d, proj), B16), sds((d, proj), B16)] + [sds((d, ffn), B16)] * 6 + [sds((1, d), F32)],
        scratch_shapes=[
            pltpu.VMEM((rows, d), F32), pltpu.VMEM((rows, d), B16), pltpu.VMEM((d, rows), B16), pltpu.VMEM((d, rows), B16),
            pltpu.VMEM((rows, d), F32), pltpu.VMEM((rows, d), F32),
            pltpu.VMEM((d, FC), B16), pltpu.VMEM((d, FC), B16), pltpu.VMEM((FC, d), B16),
            pltpu.VMEM((rows, FC), B16), pltpu.VMEM((rows, FC), B16), pltpu.VMEM((rows, FC), B16),
        ],
        compiler_params=pltpu.CompilerParams(vmem_limit_bytes=61 << 20, dimension_semantics=("arbitrary",)),
        cost_estimate=pl.CostEstimate(flops=flops, transcendentals=rows * 2 * ffn, bytes_accessed=rows * d * 20 + 24 * d * ffn),
    )(tok, att_own, att_recv, wo, wo_other, wg, wg_other, wu, wu_other, wd, wd_other, og, gain)


def post_body(core_ref, qa, qb, ka, kb, va, vb, w_ref, n_ref, own_ref, send_ref, g_ref, rows):
    i = pl.program_id(0)
    span = n_ref.shape[0]
    d = jnp.concatenate([qa[...], qb[...], ka[...], kb[...], va[...], vb[...]], axis=0)
    back = dot(w_ref[...], d, NN).astype(B16).T
    rows[pl.ds(pl.multiple_of(i * span, span), span), :] = back
    part = dot(n_ref[...].T, d, NT)

    @pl.when(i == 0)
    def _():
        g_ref[...] = part

    @pl.when(i > 0)
    def _():
        g_ref[...] += part

    @pl.when(i == pl.num_programs(0) - 1)
    def _():
        core = core_ref[0]
        half = own_ref.shape[1]
        for s in range(own_ref.shape[0]):
            own_ref[s] = rows[pl.ds(pl.multiple_of((2 * s + core) * half, 32), half), :]
            send_ref[s] = rows[pl.ds(pl.multiple_of((2 * s + 1 - core) * half, 32), half), :]


def post(core, pieces, w, normed, blocks):
    total, d = normed.shape
    span = CK * SUB
    half = total // blocks // 2
    lanes = lambda x: pl.BlockSpec((x.shape[0], span), lambda i, s: (0, i))
    const = lambda *shape: pl.BlockSpec(shape, lambda i, s: (0,) * len(shape))
    spec = pltpu.PrefetchScalarGridSpec(
        num_scalar_prefetch=1, grid=(total // span,),
        in_specs=[lanes(x) for x in pieces] + [const(*w.shape), pl.BlockSpec((span, d), lambda i, s: (i, 0))],
        out_specs=[const(blocks, half, d), const(blocks, half, d), const(*w.shape)],
        scratch_shapes=[pltpu.VMEM((total, d), B16)])
    return pl.pallas_call(
        post_body, grid_spec=spec, name="post",
        out_shape=[jax.ShapeDtypeStruct((blocks, half, d), B16), jax.ShapeDtypeStruct((blocks, half, d), B16),
                   jax.ShapeDtypeStruct(w.shape, F32)],
        compiler_params=pltpu.CompilerParams(vmem_limit_bytes=56 << 20, dimension_semantics=("arbitrary",)),
        cost_estimate=pl.CostEstimate(flops=4 * total * d * w.shape[1], transcendentals=0, bytes_accessed=30 * total * d // 4),
    )(core, *pieces, w, normed)


def unpack_body(x_ref, gate_ref, up_ref, down_ref, out_ref):
    f = gate_ref.shape[1]
    gate_ref[...] = x_ref[:, 0:f].astype(F32)
    up_ref[...] = x_ref[:, f : 2 * f].astype(F32)
    down_ref[...] = x_ref[:, 2 * f : 3 * f].astype(F32).T
    out_ref[...] = x_ref[:, 3 * f :].astype(F32).T


def unpack(x, f):
    d, columns = x.shape
    p = columns - 3 * f
    row = lambda width: pl.BlockSpec((128, width), lambda i: (i, 0))
    col = lambda width: pl.BlockSpec((width, 128), lambda i: (0, i))
    return pl.pallas_call(
        unpack_body, grid=(d // 128,), name="unpack",
        in_specs=[row(columns)], out_specs=[row(f), row(f), col(f), col(p)],
        out_shape=[jax.ShapeDtypeStruct((d, f), F32), jax.ShapeDtypeStruct((d, f), F32),
                   jax.ShapeDtypeStruct((f, d), F32), jax.ShapeDtypeStruct((p, d), F32)],
        compiler_params=pltpu.CompilerParams(vmem_limit_bytes=40 << 20, dimension_semantics=("arbitrary",)),
        cost_estimate=pl.CostEstimate(flops=0, transcendentals=0, bytes_accessed=6 * d * columns),
    )(x)


def swapped(tree):
    return jax.tree.map(lambda a: lax.ppermute(a, "mp", [(0, 1), (1, 0)]), tree)


def matmul(a, b):
    return dot(a, b, NN)


def grad_of(a, b):
    return lax.dot_general(a, b, (((0,), (0,)), ((), ())), preferred_element_type=F32)


X_SWAP = ("dp", 0)
Y_SWAP = ("dp", 1)
Z_NEAR = ("seq", 0)
Z_FAR = ("seq", 1)


def hop(x, axis, bit):
    count = lax.axis_size(axis)
    return lax.ppermute(x, axis, [(i, i ^ (1 << bit)) for i in range(count)])


def side_of(axis, bit):
    return (lax.axis_index(axis) >> bit) & 1


def give(x, axis, bit, behind=None):
    side = side_of(axis, bit)
    rows = x.shape[0] // 2
    keep = lax.dynamic_slice_in_dim(x, side * rows, rows, 0)
    send = lax.dynamic_slice_in_dim(x, (1 - side) * rows, rows, 0)
    recv = hop(send.astype(B16), axis, bit)
    if behind is not None:
        recv, keep = after(recv, behind), after(keep, behind)
    return keep.astype(F32) + recv.astype(F32)


def take(x, axis, bit):
    first = side_of(axis, bit) == 0
    other = hop(x, axis, bit)
    return jnp.concatenate([jnp.where(first, x, other), jnp.where(first, other, x)], axis=0)


def two_ways(x, step, ways):
    cut = x.shape[1] // 2
    return [step(x[:, :cut], *ways[0]), step(x[:, cut:], *ways[1])]


def after(value, *others):
    return lax.optimization_barrier((value,) + others)[0]


def gelu_parts(gate):
    c = 0.7978845608028654
    inside = c * (gate + 0.044715 * gate * gate * gate)
    th = jnp.tanh(inside)
    value = 0.5 * gate * (1.0 + th)
    slope = 0.5 * (1.0 + th) + 0.5 * gate * (1.0 - th * th) * (c * (1.0 + 3.0 * 0.044715 * gate * gate))
    return value, slope


def local_item(
    byte_ids, true_lengths, byte_table, conv_taps, block_scorer, attn_gain, w_query, w_key, w_value,
    w_output, rel_table, ffn_gain, w_gate, w_up, w_down, out_grad,
):
    seq_count = lax.axis_size("seq")
    place = lax.axis_index("seq")
    core = lax.axis_index("mp")
    tok_rows = out_grad.shape[0]
    half = tok_rows // 2
    width = out_grad.shape[2]
    own_rows = seq_count * half
    total = 2 * own_rows
    proj = w_query.shape[1]
    first = core == 0

    def halves(full):
        parts = full.reshape(seq_count, 2, half, full.shape[1])
        own = jnp.where(first, parts[:, 0], parts[:, 1]).reshape(own_rows, -1)
        other = jnp.where(first, parts[:, 1], parts[:, 0]).reshape(own_rows, -1)
        return own, other

    def whole(own, other):
        shape = (seq_count, half, own.shape[1])
        low, high = jnp.where(first, own, other), jnp.where(first, other, own)
        return jnp.stack([low.reshape(shape), high.reshape(shape)], axis=1).reshape(total, -1)

    byte_rows = byte_ids.shape[0]
    here = place * byte_rows + jnp.arange(byte_rows, dtype=jnp.int32)
    shown = jnp.where(here[:, None] < true_lengths[None, :], byte_ids, -1)
    shown = shown.reshape(tok_rows, 2, seq_count).transpose(2, 1, 0)
    shown = lax.all_to_all(shown, "seq", split_axis=0, concat_axis=0, tiled=True)
    length = lax.dynamic_index_in_dim(true_lengths, place, 0, keepdims=False)
    wo_other, wg_other, wu_other, wd_other = swapped((w_output, w_gate, w_up, w_down))
    grad_rows = lax.dynamic_slice_in_dim(out_grad, core * half, half, 0)
    grad_own = lax.all_to_all(grad_rows, "seq", split_axis=1, concat_axis=0, tiled=True)
    grad_own = grad_own.reshape(own_rows, width)

    tiles = own_rows // TT
    pairs = jnp.pad(shown.transpose(1, 0, 2).reshape(2, total), ((0, 0), (1, 1)), constant_values=-1)
    rows = jnp.concatenate([pairs[:, j : j + total] for j in range(3)], axis=0).reshape(6, seq_count, 2, half)
    rows = jnp.where(first, rows[:, :, 0], rows[:, :, 1]).reshape(6, tiles, TT).transpose(1, 0, 2)
    cid = jnp.pad(rows, ((0, 0), (0, 2), (0, 0)), constant_values=-1)

    vocab = byte_table.shape[0]
    raw = jnp.pad(byte_table, ((0, CJ - vocab), (0, 0)))
    scorer, gain_one, gain_two = block_scorer[None], attn_gain[None], ffn_gain[None]
    tokens, normed, pool_w, mix, table_cat = gbst_fwd(cid, raw, conv_taps, scorer, gain_one)
    normed_all = whole(normed, swapped(normed))
    w_qkv = jnp.concatenate([w_query, w_key, w_value], axis=1)
    qkv = matmul(normed_all, w_qkv).astype(B16)
    limit = ((length + 1) // 2).reshape(1)
    weights, att, att_t, inv = attn_fwd(limit, qkv, bias_curve(rel_table, proj // DH))
    att_own, att_send = halves(att)
    att_recv = swapped(att_send)
    (layer, hidden_back, d_own, d_send, out_own, out_other, gate_own, up_own, down_own,
     gate_other, up_other, down_other, g_gain_two) = middle(
        tokens, att_own, att_recv, w_output, wo_other, w_gate, wg_other, w_up, wu_other, w_down, wd_other,
        grad_own, gain_two
    )
    d_att = whole(d_own, swapped(d_send))

    ffn_width = w_gate.shape[1]
    add = lambda a, b: (a.astype(F32) + b.astype(F32)).astype(B16)
    own_cols = (gate_own, up_own, down_own, out_own)
    other_cols = swapped((gate_other, up_other, down_other, out_other))
    large = jnp.concatenate([add(a, b) for a, b in zip(own_cols, other_cols)], axis=1)
    large = lax.psum_scatter(large, "dp", scatter_dimension=0, tiled=True)

    pairs = proj // 128
    early = pairs - 1
    dk_a, dv_a, dq_a, near_a, far_a = attn_bwd(weights, qkv, d_att, att_t, inv, 0, early)
    sent = layer.reshape(seq_count, half, width)
    layer_out = lax.all_to_all(sent[:, :, None], "seq", split_axis=0, concat_axis=2, tiled=True)
    late, dk_a, dv_a, dq_a, large, layer_out = lax.optimization_barrier((d_att, dk_a, dv_a, dq_a, large, layer_out))
    large = lax.psum_scatter(large, "seq", scatter_dimension=0, tiled=True)
    dk_b, dv_b, dq_b, near_b, far_b = attn_bwd(weights, qkv, late, att_t, inv, early, 1)
    near, far = jnp.concatenate([near_a, near_b]), jnp.concatenate([far_a, far_b])
    dk_b, large = lax.optimization_barrier((dk_b, large))
    pieces = (dq_a, dq_b, dk_a, dk_b, dv_a, dv_b)
    part_own, part_send, g_qkv = post(core.reshape(1).astype(jnp.int32), pieces, w_qkv, normed_all, seq_count)
    part_own = part_own.reshape(own_rows, width)
    part_recv = swapped(part_send).reshape(own_rows, width)
    large = lax.all_gather(large, "seq", axis=0, tiled=True)
    layer_out = layer_out.reshape(half, seq_count, width).astype(F32)
    part_own, large, layer_out = lax.optimization_barrier((part_own, large, layer_out))
    large = lax.all_gather(large, "dp", axis=0, tiled=True)
    g_rel = rel_grad(near, far, near.shape[2])
    rel_row = jnp.pad(g_rel.reshape(1, -1), ((0, 0), (0, width - g_rel.size)))
    blank = jnp.zeros_like(rel_row)
    rel_rows = [jnp.where(first, rel_row, blank), jnp.where(first, blank, rel_row)]
    extra = jnp.concatenate([g_gain_two] + rel_rows + [jnp.zeros((5, width), F32)], axis=0)
    tail = gbst_bwd(
        cid, pool_w, mix, tokens, hidden_back, part_own, part_recv, gain_one, table_cat, raw, conv_taps, scorer, extra
    )
    left, right = two_ways(g_qkv, give, (X_SWAP + (tail,), Y_SWAP + (tail,)))
    tail = give(tail, "mp", 0)
    left = give(left, *Y_SWAP)
    right = give(right, *X_SWAP)
    tail = give(tail, *X_SWAP)
    both = give(jnp.concatenate([left, right], axis=1), *Z_NEAR)
    tail = give(tail, *Y_SWAP)
    both = give(both, *Z_FAR).astype(B16)
    tail = tail + hop(tail.astype(B16), *Z_NEAR).astype(F32)
    both = take(both, *Z_FAR)
    tail = (tail + hop(tail.astype(B16), *Z_FAR).astype(F32)).astype(B16)
    both = take(both, *Z_NEAR)
    both, large = lax.optimization_barrier((both, large))
    cut = both.shape[1] // 2
    left, right = take(both[:, :cut], *Y_SWAP), take(both[:, cut:], *X_SWAP)
    tail = take(tail, *Y_SWAP)
    left, right = take(left, *X_SWAP), take(right, *Y_SWAP)
    tail = take(tail, *X_SWAP)
    tail = take(tail, "mp", 0).astype(F32)
    g_gate, g_up, g_down, g_out = unpack(large, ffn_width)
    g_qkv = jnp.concatenate([left, right], axis=1)
    g_query, g_key, g_value = (g_qkv[:, i * proj : (i + 1) * proj].astype(F32) for i in range(3))
    g_table, small, g_gain_two = tail[:CJ], tail[CJ : CJ + 7], tail[CJ + 8]
    g_rel = jnp.where(first, tail[CJ + 9], tail[CJ + 10])[: g_rel.size].reshape(g_rel.shape)

    return (
        layer_out, g_table[:vocab], small[:5], small[5], small[6], g_query, g_key, g_value, g_out, g_rel,
        g_gain_two, g_gate, g_up, g_down,
    )


def chosen(*args):
    ids, lengths, w_query, out_grad = args[0], args[1], args[6], args[15]
    seq_count = lax.axis_size("seq")
    total = out_grad.shape[0] * seq_count
    fits = (
        lengths.shape[0] == seq_count
        and lax.axis_size("mp") == 2
        and lax.axis_size("dp") == 4
        and seq_count == 4
        and total % (2 * TT) == 0
        and total % CK == 0
        and total % (CK * SUB) == 0
        and w_query.shape[1] % 128 == 0
        and w_query.shape[1] >= 256
        and args[12].shape[1] % FC == 0
        and args[2].shape[1] % 128 == 0
        and (total // (2 * seq_count)) % 32 == 0
        and (total // 2) % RT == 0
        and (ids.shape[0] // 2) % 12 == 0
    )
    return local_item(*args) if fits else local_general(*args)


def solution(mesh):
    return jax.shard_map(
        chosen,
        mesh=mesh,
        in_specs=(
            P("seq", "dp"),
            P("dp"),
            P(),
            P(),
            P(),
            P(),
            P(None, "mp"),
            P(None, "mp"),
            P(None, "mp"),
            P("mp", None),
            P(None, "mp"),
            P(),
            P(None, "mp"),
            P(None, "mp"),
            P("mp", None),
            P("seq", "dp", None),
        ),
        out_specs=(
            P(("seq", "mp"), "dp", None),
            P(),
            P(),
            P(),
            P(),
            P(None, "mp"),
            P(None, "mp"),
            P(None, "mp"),
            P("mp", None),
            P(None, "mp"),
            P(),
            P(None, "mp"),
            P(None, "mp"),
            P("mp", None),
        ),
        check_vma=False,
    )
```

```python
import functools

import jax
import jax.numpy as jnp
from jax import lax
from jax.experimental import pallas as pl
from jax.experimental.pallas import tpu as pltpu
from jax.sharding import PartitionSpec as P

DH = 64
BUCKETS = 32
MICRO = 4


EPS = 1e-06
NEG = -1000000000.0
EDGES = (12, 16, 23, 32, 46, 64, 91)
HIGH = lax.Precision.HIGHEST
F32 = jnp.float32
B16 = jnp.bfloat16


def extended(cells, sides, width):
    for axis, dim in sides:
        count = lax.axis_size(axis)
        ends = count - 1
        head = lax.slice_in_dim(cells, 0, width, axis=dim)
        tail = lax.slice_in_dim(cells, cells.shape[dim] - width, cells.shape[dim], axis=dim)
        cells = jnp.concatenate(
            [
                lax.ppermute(tail, axis, [(i, (i + 1) % count) for i in range(ends)]),
                cells,
                lax.ppermute(head, axis, [((i + 1) % count, i) for i in range(ends)]),
            ],
            axis=dim,
        )
    return cells


def for_sending(array):
    return jax.tree.map(lambda a: a.astype(jnp.bfloat16) if a.dtype == jnp.float32 else a, array)


def bucket_of(offset):
    distance = jnp.abs(offset)
    far = jnp.full(offset.shape, 8, jnp.int32)
    for edge in EDGES:
        far = far + (distance >= edge).astype(jnp.int32)
    near = jnp.where(distance < 8, distance, far)
    return near + 16 * (offset > 0).astype(jnp.int32)


def bias_onehot(query_places, key_places):
    offset = key_places[None, :] - query_places[:, None]
    return (bucket_of(offset)[:, :, None] == jnp.arange(BUCKETS, dtype=jnp.int32)).astype(F32)


def rms_norm(hidden, gain):
    return hidden * lax.rsqrt(jnp.mean(hidden * hidden, axis=-1, keepdims=True) + EPS) * gain


def activation(gate, up):
    return jax.nn.gelu(gate, approximate=True) * up


def gbst_tail(conv_out, scorer):
    byte_count, item_count, model_width = conv_out.shape
    weighted = jnp.einsum("pid,d->pi", conv_out, scorer, precision=HIGH)
    pooled_all = []
    scores_all = []
    for block_size in (1, 2, 3, 4):
        block_means = conv_out.reshape(
            byte_count // block_size, block_size, item_count, model_width
        ).mean(axis=1)
        pooled_all.append(jnp.repeat(block_means, block_size, axis=0))
        score_means = weighted.reshape(byte_count // block_size, block_size, item_count).mean(
            axis=1
        )
        scores_all.append(jnp.repeat(score_means, block_size, axis=0))
    mixing = jax.nn.softmax(jnp.stack(scores_all), axis=0)
    mixture = mixing[0][:, :, None] * pooled_all[0]
    for block_index in range(1, 4):
        mixture = mixture + mixing[block_index][:, :, None] * pooled_all[block_index]
    return mixture.reshape(byte_count // 2, 2, item_count, model_width).mean(axis=1)


def local_general(
    byte_ids,
    true_lengths,
    byte_table,
    conv_taps,
    block_scorer,
    attn_gain,
    w_query,
    w_key,
    w_value,
    w_output,
    rel_table,
    ffn_gain,
    w_gate,
    w_up,
    w_down,
    out_grad,
):
    seq_count = lax.axis_size("seq")
    seq_place = lax.axis_index("seq")
    core_place = lax.axis_index("mp")
    byte_rows = byte_ids.shape[0]
    tok_rows = byte_rows // 2
    half_rows = tok_rows // lax.axis_size("mp")
    total_tokens = tok_rows * seq_count
    item_count = byte_ids.shape[1] // MICRO
    proj_width = w_query.shape[1]
    head_count = proj_width // DH
    ffn_width = w_gate.shape[1]
    taps = conv_taps.astype(F32)
    scorer = block_scorer.astype(F32)
    gain_one = attn_gain.astype(F32)
    gain_two = ffn_gain.astype(F32)
    rel_local = rel_table.astype(F32)
    gate_up = jnp.concatenate([w_gate, w_up], axis=1)
    query_places = seq_place * tok_rows + jnp.arange(tok_rows, dtype=jnp.int32)
    key_places = jnp.arange(total_tokens, dtype=jnp.int32)
    onehot_bias = bias_onehot(query_places, key_places)
    bias = jnp.einsum("qkb,bh->hqk", onehot_bias, rel_local, precision=HIGH)
    byte_places = seq_place * byte_rows + jnp.arange(byte_rows, dtype=jnp.int32)
    vocab_range = jnp.arange(byte_table.shape[0], dtype=jnp.int32)
    sum_table = jnp.zeros(byte_table.shape, F32)
    sum_taps = jnp.zeros(conv_taps.shape, F32)
    sum_scorer = jnp.zeros(block_scorer.shape, F32)
    sum_gain_one = jnp.zeros(attn_gain.shape, F32)
    sum_query = jnp.zeros(w_query.shape, F32)
    sum_key = jnp.zeros(w_key.shape, F32)
    sum_value = jnp.zeros(w_value.shape, F32)
    sum_output = jnp.zeros(w_output.shape, F32)
    sum_rel = jnp.zeros(rel_table.shape, F32)
    sum_gain_two = jnp.zeros(ffn_gain.shape, F32)
    sum_gate = jnp.zeros(w_gate.shape, F32)
    sum_up = jnp.zeros(w_up.shape, F32)
    sum_down = jnp.zeros(w_down.shape, F32)
    outputs = []
    for micro in range(MICRO):
        first = micro * item_count
        ids_now = byte_ids[:, first : first + item_count]
        lengths = true_lengths[first : first + item_count]
        keep = (byte_places[:, None] < lengths[None, :]).astype(F32)
        onehot = (ids_now[:, :, None] == vocab_range).astype(F32) * keep[:, :, None]
        embedded = jnp.einsum(
            "piv,vd->pid", onehot.astype(B16), byte_table, preferred_element_type=F32
        ).astype(B16)
        framed = extended(embedded, (("seq", 0),), 2)
        conv_out = taps[0] * framed[0:byte_rows]
        for tap_index in range(1, 5):
            conv_out = conv_out + taps[tap_index] * framed[tap_index : tap_index + byte_rows]
        tokens, gbst_pull = jax.vjp(gbst_tail, conv_out, scorer)
        normed, norm_pull = jax.vjp(rms_norm, tokens, gain_one)
        normed_low = normed.astype(B16)
        query = jnp.einsum("qid,dh->qih", normed_low, w_query, preferred_element_type=F32).astype(
            B16
        )
        keys_here = jnp.einsum("qid,dh->qih", normed_low, w_key, preferred_element_type=F32).astype(
            B16
        )
        values_here = jnp.einsum(
            "qid,dh->qih", normed_low, w_value, preferred_element_type=F32
        ).astype(B16)
        keys_all, values_all = (
            lax.all_gather(keys_here, "seq", axis=0, tiled=True),
            lax.all_gather(values_here, "seq", axis=0, tiled=True),
        )
        query4 = query.reshape(tok_rows, item_count, head_count, DH)
        keys4 = keys_all.reshape(total_tokens, item_count, head_count, DH)
        values4 = values_all.reshape(total_tokens, item_count, head_count, DH)
        key_ok = 2 * key_places[None, :] < lengths[:, None]

        def scores_of():
            raw = jnp.einsum("qihe,kihe->ihqk", query4, keys4, preferred_element_type=F32)
            return jnp.where(key_ok[:, None, None, :], raw + bias[None], NEG)

        scores = scores_of()
        top = jnp.max(scores, axis=-1, keepdims=True)
        log_total = top + jnp.log(jnp.sum(jnp.exp(scores - top), axis=-1, keepdims=True))
        probs_low = jnp.exp(scores - log_total).astype(B16)
        attended = (
            jnp.einsum("ihqk,kihe->qihe", probs_low, values4, preferred_element_type=F32)
            .reshape(tok_rows, item_count, proj_width)
            .astype(B16)
        )
        attn_half = lax.psum_scatter(
            jnp.einsum("qih,hd->qid", attended, w_output, preferred_element_type=F32),
            "mp",
            scatter_dimension=0,
            tiled=True,
        )
        tokens_half = lax.dynamic_slice_in_dim(tokens, core_place * half_rows, half_rows, 0)
        hidden_half = tokens_half + attn_half
        normed_two, norm_two_pull = jax.vjp(rms_norm, hidden_half, gain_two)
        normed_full = lax.all_gather(normed_two.astype(B16), "mp", axis=0, tiled=True)
        projected = jnp.einsum("qid,df->qif", normed_full, gate_up, preferred_element_type=F32)
        inner, inner_pull = jax.vjp(
            activation, projected[..., :ffn_width], projected[..., ffn_width:]
        )
        inner_low = inner.astype(B16)
        ffn_half = lax.psum_scatter(
            jnp.einsum("qif,fd->qid", inner_low, w_down, preferred_element_type=F32).astype(
                jnp.bfloat16
            ),
            "mp",
            scatter_dimension=0,
            tiled=True,
        ).astype(jnp.float32)
        outputs.append(hidden_half + ffn_half)
        grad_low = out_grad[:, first : first + item_count]
        grad_half = lax.dynamic_slice_in_dim(grad_low, core_place * half_rows, half_rows, 0).astype(
            F32
        )
        sum_down = sum_down + jnp.einsum(
            "qif,qid->fd", inner_low, grad_low, preferred_element_type=F32
        )
        grad_inner = jnp.einsum("qid,fd->qif", grad_low, w_down, preferred_element_type=F32)
        gate_grad, up_grad = inner_pull(grad_inner)
        gate_low = gate_grad.astype(B16)
        up_low = up_grad.astype(B16)
        sum_gate = sum_gate + jnp.einsum(
            "qid,qif->df", normed_full, gate_low, preferred_element_type=F32
        )
        sum_up = sum_up + jnp.einsum("qid,qif->df", normed_full, up_low, preferred_element_type=F32)
        normed_two_grad = lax.psum_scatter(
            jnp.einsum("qif,df->qid", gate_low, w_gate, preferred_element_type=F32)
            + jnp.einsum("qif,df->qid", up_low, w_up, preferred_element_type=F32),
            "mp",
            scatter_dimension=0,
            tiled=True,
        )
        hidden_norm_grad, gain_two_grad = norm_two_pull(normed_two_grad)
        hidden_grad = grad_half + hidden_norm_grad
        hidden_full = lax.all_gather(for_sending(hidden_grad), "mp", axis=0, tiled=True).astype(
            hidden_grad.dtype
        )
        hidden_low = hidden_full.astype(B16)
        sum_output = sum_output + jnp.einsum(
            "qih,qid->hd", attended, hidden_low, preferred_element_type=F32
        )
        attended_grad = jnp.einsum(
            "qid,hd->qih", hidden_low, w_output, preferred_element_type=F32
        ).astype(B16)
        attended_grad4 = attended_grad.reshape(tok_rows, item_count, head_count, DH)
        scores = scores_of()
        probs = jnp.exp(scores - log_total)
        probs_low = probs.astype(B16)
        probs_grad = jnp.einsum(
            "qihe,kihe->ihqk", attended_grad4, values4, preferred_element_type=F32
        )
        inner_sum = jnp.sum(probs * probs_grad, axis=-1, keepdims=True)
        scores_grad = probs * (probs_grad - inner_sum)
        sum_rel = sum_rel + jnp.einsum(
            "qkb,hqk->bh", onehot_bias, jnp.sum(scores_grad, axis=0), precision=HIGH
        )
        scores_low = scores_grad.astype(B16)
        query_grad = (
            jnp.einsum("ihqk,kihe->qihe", scores_low, keys4, preferred_element_type=F32)
            .reshape(tok_rows, item_count, proj_width)
            .astype(B16)
        )
        key_part = jnp.einsum("ihqk,qihe->kihe", scores_low, query4, preferred_element_type=F32)
        value_part = jnp.einsum(
            "ihqk,qihe->kihe", probs_low, attended_grad4, preferred_element_type=F32
        )
        key_sums = lax.psum_scatter(
            jnp.concatenate(
                [
                    key_part.reshape(tok_rows * lax.axis_size("seq"), item_count, proj_width),
                    value_part.reshape(tok_rows * lax.axis_size("seq"), item_count, proj_width),
                ],
                axis=2,
            ).astype(jnp.bfloat16),
            "seq",
            scatter_dimension=0,
            tiled=True,
        ).astype(jnp.float32)
        keys_grad = key_sums[..., :proj_width].astype(B16)
        values_grad = key_sums[..., proj_width:].astype(B16)
        sum_query = sum_query + jnp.einsum(
            "qid,qih->dh", normed_low, query_grad, preferred_element_type=F32
        )
        sum_key = sum_key + jnp.einsum(
            "qid,qih->dh", normed_low, keys_grad, preferred_element_type=F32
        )
        sum_value = sum_value + jnp.einsum(
            "qid,qih->dh", normed_low, values_grad, preferred_element_type=F32
        )
        partial_grad = (
            jnp.einsum("qih,dh->qid", query_grad, w_query, preferred_element_type=F32)
            + jnp.einsum("qih,dh->qid", keys_grad, w_key, preferred_element_type=F32)
            + jnp.einsum("qih,dh->qid", values_grad, w_value, preferred_element_type=F32)
        )
        normed_grad, gain_two_total = (
            lax.psum(partial_grad.astype(jnp.bfloat16), "mp").astype(jnp.float32),
            lax.psum(gain_two_grad.astype(jnp.bfloat16), "mp").astype(jnp.float32),
        )
        sum_gain_two = sum_gain_two + gain_two_total
        tokens_norm_grad, gain_one_grad = norm_pull(normed_grad)
        sum_gain_one = sum_gain_one + gain_one_grad
        tokens_grad = hidden_full + tokens_norm_grad
        conv_grad, scorer_grad = gbst_pull(tokens_grad)
        sum_scorer = sum_scorer + scorer_grad
        framed_grad = extended(conv_grad.astype(jnp.bfloat16), (("seq", 0),), 2).astype(
            conv_grad.dtype
        )
        embedded_grad = taps[0] * framed_grad[4 : 4 + byte_rows]
        for tap_index in range(1, 5):
            embedded_grad = (
                embedded_grad
                + taps[tap_index] * framed_grad[4 - tap_index : 4 - tap_index + byte_rows]
            )
        tap_sums = [
            jnp.sum(conv_grad * framed[tap_index : tap_index + byte_rows], axis=(0, 1))
            for tap_index in range(5)
        ]
        sum_taps = sum_taps + jnp.stack(tap_sums)
        sum_table = sum_table + jnp.einsum("piv,pid->vd", onehot, embedded_grad, precision=HIGH)
    totals = lax.psum(
        (
            sum_table,
            sum_taps,
            sum_scorer,
            sum_gain_one,
            sum_query,
            sum_key,
            sum_value,
            sum_output,
            sum_rel,
            sum_gain_two,
            sum_gate,
            sum_up,
            sum_down,
        ),
        ("dp", "seq"),
    )
    layer_out = jnp.concatenate(outputs, axis=1)
    return (
        layer_out,
        totals[0],
        totals[1],
        totals[2],
        totals[3],
        totals[4],
        totals[5],
        totals[6],
        totals[7],
        totals[8],
        totals[9],
        totals[10],
        totals[11],
        totals[12],
    )


LOG2E = 1.4426950408889634
LN2 = 0.6931471805599453
NT = (((1,), (1,)), ((), ()))
NN = (((1,), (0,)), ((), ()))
CK = 256
SUB = 3

def dot(a, b, dims):
    return lax.dot_general(a, b, dims, preferred_element_type=F32)

def split3(x):
    hi = x.astype(B16)
    rest = x - hi.astype(F32)
    mid = rest.astype(B16)
    lo = (rest - mid.astype(F32)).astype(B16)
    return hi, mid, lo

def split3_xla(x):
    cut = lambda a: lax.reduce_precision(a, exponent_bits=8, mantissa_bits=7)
    hi = cut(x)
    mid = cut(x - hi)
    return hi.astype(B16), mid.astype(B16), (x - hi - mid).astype(B16)


def attn_fwd_body(limit_ref, q_ref, k_ref, v_ref, curve_ref, e_ref, o_ref, ot_ref, inv_ref,
                  kext, vext, table, qext, norms):
    total = k_ref.shape[0]
    tq = CK
    chunks = total // CK
    step = pl.program_id(1)

    @pl.when(step == 0)
    def _():
        lane = lax.broadcasted_iota(jnp.int32, (total, 128), 1)
        place = lax.broadcasted_iota(jnp.int32, (total, 128), 0)
        masked = jnp.where(place < limit_ref[0], 0.0, -1e9).astype(F32)
        k = k_ref[...].astype(F32)
        q = q_ref[...].astype(F32)
        pick = lax.broadcasted_iota(jnp.int32, (128, 128), 0) // 64 == lax.broadcasted_iota(jnp.int32, (128, 128), 1)
        pick = jnp.where(pick, 1.0, 0.0).astype(B16)
        size_q = jnp.max(dot((q * q).astype(B16), pick, NN), axis=0, keepdims=True)
        size_k = jnp.max(dot((k * k).astype(B16), pick, NN), axis=0, keepdims=True)
        both = size_q * size_k
        vt = v_ref[...].T
        for h in range(2):
            norms[h] = jnp.max(both[:, h : h + 1])
            own = (lane < 64) if h == 0 else (lane >= 64)
            base = 64 if h == 0 else 0
            extra = jnp.where(lane == base, masked, jnp.where((lane > base) & (lane < base + 4), 1.0, 0.0))
            kext[h] = jnp.where(own, k, extra).astype(B16)
            vext[h, 0:64, :] = vt[64 * h : 64 * h + 64, :]
            vext[h, 64:80, :] = jnp.ones((16, total), B16)
            curve = curve_ref[h : h + 1, :]
            for g in range(5):
                lo = 1024 + 2 * CK - g * CK - 256
                if g in (0, 4):
                    table[h, g * CK : (g + 1) * CK, :] = jnp.broadcast_to(curve[:, lo : lo + 1], (CK, CK))
                else:
                    window = jnp.broadcast_to(curve[:, lo : lo + 512], (CK, 512))
                    rolled = pltpu.roll(window, 0, 1, stride=1, stride_axis=0)
                    table[h, g * CK : (g + 1) * CK, :] = rolled[:, 256:512]

    lane_q = lax.broadcasted_iota(jnp.int32, (tq, 128), 1)

    def scores(h, u, c):
        d = jnp.clip(c - (step * SUB + u), -2, 2) + 2
        k_now = kext[h, pl.ds(c * CK if isinstance(c, int) else pl.multiple_of(c * CK, CK), CK), :]
        return dot(k_now, qext[u, h], NT) * LOG2E + table[h, pl.ds(pl.multiple_of(d * CK, CK), CK), :]

    for u in range(SUB):
        q = q_ref[pl.ds(pl.multiple_of((step * SUB + u) * tq, tq), tq), :]
        for h in range(2):
            own = (lane_q < 64) if h == 0 else (lane_q >= 64)
            base = 64 if h == 0 else 0
            qext[u, h] = jnp.where(own, q, jnp.where(lane_q == base, 1.0, 0.0).astype(B16))

    for h in range(2):
        @pl.when(norms[h] > 48.0 * 48.0)
        def _(h=h):
            own = (lane_q < 64) if h == 0 else (lane_q >= 64)
            base = 64 if h == 0 else 0

            def settle(u, carry):
                def grow(c, top):
                    return jnp.maximum(top, jnp.max(scores(h, u, c), axis=0, keepdims=True))
                top = lax.fori_loop(0, chunks, grow, jnp.full((1, tq), -3e38, F32))
                hi, mid, lo = split3(-jnp.broadcast_to(top * LN2, (128, tq)).T)
                extra = jnp.where(lane_q == base, jnp.ones_like(hi), jnp.zeros_like(hi))
                for at, part in ((1, hi), (2, mid), (3, lo)):
                    extra = jnp.where(lane_q == base + at, part, extra)
                qext[u, h] = jnp.where(own, qext[u, h], extra)
                return carry
            lax.fori_loop(0, SUB, settle, 0)

    for u in range(SUB):
        cols = slice(u * tq, (u + 1) * tq)
        for h in range(2):
            for c in range(chunks):
                e_ref[h, c * CK : (c + 1) * CK, cols] = jnp.exp2(scores(h, u, c)).astype(B16)
        outs = []
        for h in range(2):
            sums = dot(vext[h], e_ref[h, :, cols], NN)
            inv = 1.0 / sums[64:65, :]
            inv_ref[h : h + 1, cols] = inv
            outs.append(sums[0:64, :] * inv)
        out = jnp.concatenate(outs, axis=0)
        ot_ref[:, cols] = out
        o_ref[cols, :] = out.astype(B16).T

def attn_fwd(limit, qkv, curve):
    total = qkv.shape[0]
    pairs = qkv.shape[1] // 3 // 128
    tq = CK
    full = lambda off: pl.BlockSpec((total, 128), lambda p, i, s: (0, off + p))
    spec = pltpu.PrefetchScalarGridSpec(
        num_scalar_prefetch=1, grid=(pairs, total // (tq * SUB)),
        in_specs=[full(0), full(pairs), full(2 * pairs), pl.BlockSpec((None, 2, 2048), lambda p, i, s: (p, 0, 0))],
        out_specs=[
            pl.BlockSpec((2, total, SUB * tq), lambda p, i, s: (p, 0, i)),
            pl.BlockSpec((SUB * tq, 128), lambda p, i, s: (i, p)),
            pl.BlockSpec((128, SUB * tq), lambda p, i, s: (p, i)),
            pl.BlockSpec((None, 2, SUB * tq), lambda p, i, s: (p, 0, i)),
        ],
        scratch_shapes=[
            pltpu.VMEM((2, total, 128), B16), pltpu.VMEM((2, 80, total), B16),
            pltpu.VMEM((2, 5 * CK, tq), F32), pltpu.VMEM((SUB, 2, tq, 128), B16),
            pltpu.SMEM((2,), F32),
        ])
    n = 2 * pairs * total * total
    return pl.pallas_call(
        attn_fwd_body, grid_spec=spec, name="attn_fwd",
        out_shape=[jax.ShapeDtypeStruct((2 * pairs, total, total), B16),
                   jax.ShapeDtypeStruct((total, 128 * pairs), B16),
                   jax.ShapeDtypeStruct((128 * pairs, total), F32),
                   jax.ShapeDtypeStruct((pairs, 2, total), F32)],
        compiler_params=pltpu.CompilerParams(vmem_limit_bytes=56 << 20, dimension_semantics=("arbitrary", "arbitrary")),
        cost_estimate=pl.CostEstimate(flops=4 * 64 * n, transcendentals=n, bytes_accessed=2 * n),
    )(limit, qkv, qkv, qkv, curve)

def attn_bwd_body(e_ref, k_ref, v_ref, q_ref, do_ref, ot_ref, inv_ref,
                  dk_ref, dv_ref, dqo_ref, near_ref, far_ref,
                  doe, dop, qind, ds, band, dq_ref):
    total = q_ref.shape[0]
    ck = k_ref.shape[0]
    blocks = total // CK
    chunks = pl.num_programs(1)
    step = pl.program_id(1)

    @pl.when(step == 0)
    def _():
        parts = []
        dt = do_ref[...].T
        row = lax.broadcasted_iota(jnp.int32, (64, total), 0)
        for h in range(2):
            at = slice(64 * h, 64 * h + 64)
            part = (dt[at].astype(F32) * inv_ref[h : h + 1, :]).astype(B16)
            parts.append(part)
            inner = -jnp.sum(part.astype(F32) * ot_ref[at, :], axis=0, keepdims=True)
            hi, mid, lo = split3(jnp.broadcast_to(inner, (64, total)))
            extra = jnp.where(row == 0, hi, jnp.where(row == 1, mid, jnp.where(row == 2, lo, jnp.zeros_like(hi))))
            doe[h, 64 * h : 64 * h + 64, :] = part
            doe[h, 64 - 64 * h : 128 - 64 * h, :] = extra
            lane = lax.broadcasted_iota(jnp.int32, (total, 128), 1)
            own = (lane < 64) if h == 0 else (lane >= 64)
            base = 64 if h == 0 else 0
            at128 = lax.broadcasted_iota(jnp.int32, (total, 128), 0) >> 7
            qind[h] = jnp.where(own, q_ref[...], jnp.where(lane - base == at128, 1.0, 0.0).astype(B16))
        dop[...] = jnp.concatenate(parts, axis=0).T
        dq_ref[...] = jnp.zeros_like(dq_ref)
        band[...] = jnp.zeros_like(band)
        far_ref[...] = jnp.zeros_like(far_ref)

    lane = lax.broadcasted_iota(jnp.int32, (ck, 128), 1)
    v = v_ref[...]
    kt = k_ref[...].T
    for h in range(2):
        own = (lane < 64) if h == 0 else (lane >= 64)
        base = 64 if h == 0 else 0
        ones = jnp.where((lane >= base) & (lane < base + 3), 1.0, 0.0).astype(B16)
        vx = jnp.where(own, v, ones)
        for c in range(blocks):
            cols = slice(c * CK, (c + 1) * CK)
            pg = dot(vx, doe[h, :, cols], NN)
            ds[h, :, cols] = e_ref[h, :, cols] * pg.astype(B16)
    block = lax.broadcasted_iota(jnp.int32, (1, 128), 1)
    dvs, dks = [], []
    for h in range(2):
        at = slice(64 * h, 64 * h + 64)
        base = 64 if h == 0 else 0
        dvs.append(dot(e_ref[h], dop[...], NN))
        dk = dot(ds[h], qind[h], NN)
        dks.append(dk)
        dq_ref[at, :] += dot(kt[at], ds[h], NN)
        for u in range(SUB):
            kb = step * SUB + u
            rows = slice(u * CK, (u + 1) * CK)
            sums_u = jnp.sum(dk[rows], axis=0, keepdims=True)
            spot = block - base
            inside = (spot >= 0) & (spot < total // 128)
            far_ref[h, 0:1, :] += jnp.where(inside & (spot < 2 * kb - 1), sums_u, 0.0)
            far_ref[h, 1:2, :] += jnp.where(inside & (spot >= 2 * kb + 3), sums_u, 0.0)
            band[h, :, 128 : 128 + CK] += ds[h, rows, pl.ds(pl.multiple_of(kb * CK, CK), CK)].astype(F32)

            @pl.when(kb > 0)
            def _(h=h, kb=kb, rows=rows):
                band[h, :, 0:128] += ds[h, rows, pl.ds(pl.multiple_of(kb * CK - 128, 128), 128)].astype(F32)

            @pl.when(kb < blocks - 1)
            def _(h=h, kb=kb, rows=rows):
                band[h, :, 128 + CK : 256 + CK] += ds[h, rows, pl.ds(pl.multiple_of(kb * CK + CK, 128), 128)].astype(F32)

    dk_ref[...] = jnp.where(lane < 64, dks[0], dks[1]).astype(B16).T
    dv_ref[...] = jnp.where(lane < 64, dvs[0], dvs[1]).astype(B16).T

    @pl.when(step == chunks - 1)
    def _():
        dqo_ref[...] = dq_ref[...].astype(B16)
        width = CK + 256
        row = lax.broadcasted_iota(jnp.int32, (CK, width), 0)
        col = lax.broadcasted_iota(jnp.int32, (CK, width), 1)
        offset = row - col + 128
        for h in range(2):
            all_now = band[h]
            near = jnp.where(jnp.abs(offset) < 128, all_now, 0.0)
            folded = near[0:8, :]
            for g in range(1, CK // 8):
                folded = folded + pltpu.roll(near[8 * g : 8 * g + 8, :], width - 8 * g, 1)
            line = folded[0:1, :]
            for g in range(1, 8):
                line = line + pltpu.roll(folded[g : g + 1, :], width - g, 1)
            near_ref[h, 0:1, :] = line
            near_ref[h, 1:2, :] = jnp.sum(jnp.where(offset >= 128, all_now, 0.0), axis=0, keepdims=True)
            near_ref[h, 2:3, :] = jnp.sum(jnp.where(offset <= -128, all_now, 0.0), axis=0, keepdims=True)
            near_ref[h, 3:8, :] = jnp.zeros((5, width), F32)

def attn_bwd(e, qkv, d_att, att_t, inv, start, count):
    total = qkv.shape[0]
    pairs = qkv.shape[1] // 3 // 128
    ck = CK * SUB
    full = pl.BlockSpec((total, 128), lambda p, i: (0, start + p))
    part = lambda off: pl.BlockSpec((ck, 128), lambda p, i: (i, off + start + p))
    flat = pl.BlockSpec((128, ck), lambda p, i: (p, i))
    tall = pl.BlockSpec((128, total), lambda p, i: (p, 0))
    n = 2 * count * total * total
    return pl.pallas_call(
        attn_bwd_body, grid=(count, total // ck), name="attn_bwd",
        in_specs=[pl.BlockSpec((2, ck, total), lambda p, i: (start + p, i, 0)), part(pairs), part(2 * pairs),
                  full, full, pl.BlockSpec((128, total), lambda p, i: (start + p, 0)),
                  pl.BlockSpec((None, 2, total), lambda p, i: (start + p, 0, 0))],
        out_specs=[flat, flat, tall,
                   pl.BlockSpec((2, 8, CK + 256), lambda p, i: (p, 0, 0)),
                   pl.BlockSpec((2, 8, 128), lambda p, i: (p, 0, 0))],
        out_shape=[jax.ShapeDtypeStruct((128 * count, total), B16)] * 3
        + [jax.ShapeDtypeStruct((2 * count, 8, CK + 256), F32), jax.ShapeDtypeStruct((2 * count, 8, 128), F32)],
        scratch_shapes=[
            pltpu.VMEM((2, 128, total), B16), pltpu.VMEM((total, 128), B16), pltpu.VMEM((2, total, 128), B16),
            pltpu.VMEM((2, ck, total), B16), pltpu.VMEM((2, CK, CK + 256), F32), pltpu.VMEM((128, total), F32),
        ],
        compiler_params=pltpu.CompilerParams(vmem_limit_bytes=60 << 20, dimension_semantics=("arbitrary", "arbitrary")),
        cost_estimate=pl.CostEstimate(flops=8 * 64 * n, transcendentals=0, bytes_accessed=2 * n),
    )(e, qkv, qkv, qkv, d_att, att_t, inv)

def bias_curve(rel, heads):
    offset = 1024 - jnp.arange(2048, dtype=jnp.int32)
    onehot = (bucket_of(offset)[:, None] == jnp.arange(32, dtype=jnp.int32)).astype(F32)
    curve = jnp.einsum("xb,bh->hx", onehot, rel.astype(F32) * LOG2E, precision=lax.Precision.HIGHEST)
    return curve.reshape(heads // 2, 2, 2048)

def rel_grad(near, far, width):
    x = jnp.arange(width, dtype=jnp.int32)
    onehot = (bucket_of(128 - x)[:, None] == jnp.arange(32, dtype=jnp.int32)).astype(F32)
    onehot = onehot * (x[:, None] < 256)
    g = jnp.einsum("hx,xb->bh", near[:, 0, :], onehot, precision=lax.Precision.HIGHEST)
    up = jnp.sum(near[:, 1, :], axis=1) + jnp.sum(far[:, 0], axis=1)
    down = jnp.sum(near[:, 2, :], axis=1) + jnp.sum(far[:, 1], axis=1)
    slot = jnp.arange(32)[:, None]
    return g + jnp.where(slot == 31, up[None], 0.0) + jnp.where(slot == 15, down[None], 0.0)

CJ = 272
CC = 1408
TT = 384

def means_of(even, odd):
    t = lax.broadcasted_iota(jnp.int32, even.shape, 1)
    width = even.shape[1]
    prev = lambda x: pltpu.roll(x, 1, 1)
    succ = lambda x: pltpu.roll(x, width - 1, 1)
    two = even + odd
    four = two + jnp.where(t % 2 == 0, succ(two), prev(two))
    place = t - 3 * ((t * 21846) >> 16)
    first = two + succ(even)
    middle_e = prev(two) + even
    middle_o = odd + succ(two)
    last = prev(odd) + two
    three_e = jnp.where(place == 0, first, jnp.where(place == 1, middle_e, last))
    three_o = jnp.where(place == 0, first, jnp.where(place == 1, middle_o, last))
    third = 1.0 / 3.0
    return [(even, odd), (two * 0.5, two * 0.5), (three_e * third, three_o * third), (four * 0.25, four * 0.25)]

def masks():
    t = lax.broadcasted_iota(jnp.int32, (TT, 1), 0)
    p = lax.broadcasted_iota(jnp.int32, (1, 2 * TT), 1)
    par = p >= TT
    tp = jnp.where(par, p - TT, p)
    third = lambda x: (x * 21846) >> 16
    blk = third(2 * tp + jnp.where(par, 1, 0))
    even = t == jnp.where(par, -1, tp)
    odd = t == jnp.where(par, tp, -1)
    return even, odd, (t >> 1) == (tp >> 1), third(2 * t) == blk, third(2 * t + 1) == blk


def fill_onehot(ids_ref, oht):
    row = lax.broadcasted_iota(jnp.int32, (CJ, TT), 0)
    for j in range(5):
        for side in range(2):
            hit = row == ids_ref[j + side : j + side + 1, :]
            oht[CJ * j : CJ * (j + 1), TT * side : TT * (side + 1)] = jnp.where(hit, 1.0, 0.0).astype(B16)
    oht[5 * CJ :, :] = jnp.zeros((CC - 5 * CJ, 2 * TT), B16)

def gbst_fwd_body(cid_ref, raw_ref, taps_ref, scorer_ref, gain_ref, tok_ref, norm_ref, w_ref, mix_ref, table_ref,
                  oht, rest, tvec, both, wide):
    @pl.when(pl.program_id(0) == 0)
    def _():
        raw = raw_ref[...].astype(F32)
        for j in range(5):
            at = slice(CJ * j, CJ * (j + 1))
            tap = taps_ref[j : j + 1, :].astype(F32)
            cat = raw * tap
            hi = cat.astype(B16)
            table_ref[at, :] = hi
            rest[at, :] = (cat - hi.astype(F32)).astype(B16)
            parts = split3(jnp.broadcast_to(tap * scorer_ref[...].astype(F32), (16, cat.shape[1])))
            which = lax.broadcasted_iota(jnp.int32, (16, cat.shape[1]), 0)
            zero = jnp.zeros_like(parts[0])
            rows = jnp.where(which == 0, parts[0], jnp.where(which == 1, parts[1], jnp.where(which == 2, parts[2], zero)))
            scores = dot(rows, raw_ref[...], NT)
            line = split3(jnp.broadcast_to(scores[0:1] + scores[1:2] + scores[2:3], (16, CJ)))
            which = lax.broadcasted_iota(jnp.int32, (16, CJ), 0)
            zero = jnp.zeros_like(line[0])
            tvec[j] = jnp.where(which == 0, line[0], jnp.where(which == 1, line[1], jnp.where(which == 2, line[2], zero)))
        table_ref[5 * CJ :, :] = jnp.zeros((CC - 5 * CJ, table_ref.shape[1]), B16)
        rest[5 * CJ :, :] = jnp.zeros((CC - 5 * CJ, table_ref.shape[1]), B16)
    fill_onehot(cid_ref, oht)
    parts = dot(tvec[0], oht[0:CJ, :], NN)
    for j in range(1, 5):
        parts = parts + dot(tvec[j], oht[CJ * j : CJ * (j + 1), :], NN)
    weighted = parts[0:1] + parts[1:2] + parts[2:3]
    scores = means_of(weighted[:, :TT], weighted[:, TT:])
    rows = []
    for side in range(2):
        mine = [s[side] for s in scores]
        top = jnp.maximum(jnp.maximum(mine[0], mine[1]), jnp.maximum(mine[2], mine[3]))
        e = [jnp.exp(s - top) for s in mine]
        inv = 1.0 / (e[0] + e[1] + e[2] + e[3])
        rows.append([x * inv for x in e])
    mix = jnp.concatenate([rows[side][b] for b in range(4) for side in range(2)], axis=0)
    mix_ref[...] = mix
    col = mix.T
    c = lambda i: col[:, i : i + 1]
    even, odd, pair, tri_e, tri_o = masks()
    two = 0.25 * (c(2) + c(3))
    w = jnp.where(even, 0.5 * c(0) + two, jnp.where(odd, 0.5 * c(1) + two, 0.0))
    w = w + jnp.where(pair, 0.125 * (c(6) + c(7)), 0.0)
    w = w + jnp.where(tri_e, c(4) * (1.0 / 6.0), 0.0) + jnp.where(tri_o, c(5) * (1.0 / 6.0), 0.0)
    w_hi = w.astype(B16)
    w_lo = (w - w_hi.astype(F32)).astype(B16)
    w_ref[...] = w_hi
    both[0:TT, :] = w_hi
    both[TT:, :] = w_lo
    a = dot(both[...], oht[...], NT)
    a = a[0:TT] + a[TT:]
    a_hi = a.astype(B16)
    wide[0:TT, :] = a_hi
    wide[TT:, :] = (a - a_hi.astype(F32)).astype(B16)
    tokens = dot(wide[...], table_ref[...], NN)
    tokens = tokens[0:TT] + tokens[TT:] + dot(a_hi, rest[...], NN)
    tok_ref[...] = tokens
    r = lax.rsqrt(jnp.mean(tokens * tokens, axis=1, keepdims=True) + EPS)
    norm_ref[...] = (tokens * r * gain_ref[...].astype(F32)).astype(B16)

def gbst_fwd(cid, raw, taps, scorer, gain):
    tiles = cid.shape[0]
    d = raw.shape[1]
    rows = tiles * TT
    const = lambda shape: pl.BlockSpec(shape, lambda i: (0,) * len(shape))
    return pl.pallas_call(
        gbst_fwd_body, grid=(tiles,), name="gbst_fwd",
        in_specs=[pl.BlockSpec((None, 8, TT), lambda i: (i, 0, 0)), const((CJ, d)), const((5, d)), const((1, d)), const((1, d))],
        out_specs=[pl.BlockSpec((TT, d), lambda i: (i, 0)), pl.BlockSpec((TT, d), lambda i: (i, 0)),
                   pl.BlockSpec((TT, 2 * TT), lambda i: (i, 0)), pl.BlockSpec((None, 8, TT), lambda i: (i, 0, 0)),
                   const((CC, d))],
        out_shape=[jax.ShapeDtypeStruct((rows, d), F32), jax.ShapeDtypeStruct((rows, d), B16),
                   jax.ShapeDtypeStruct((rows, 2 * TT), B16), jax.ShapeDtypeStruct((tiles, 8, TT), F32),
                   jax.ShapeDtypeStruct((CC, d), B16)],
        scratch_shapes=[pltpu.VMEM((CC, 2 * TT), B16), pltpu.VMEM((CC, d), B16), pltpu.VMEM((5, 16, CJ), B16),
                        pltpu.VMEM((2 * TT, 2 * TT), B16), pltpu.VMEM((2 * TT, CC), B16)],
        compiler_params=pltpu.CompilerParams(vmem_limit_bytes=56 << 20),
        cost_estimate=pl.CostEstimate(flops=rows * CC * d * 8, transcendentals=0, bytes_accessed=rows * d * 8),
    )(cid, raw, taps, scorer, gain)

def gbst_bwd_body(cid_ref, w_ref, mix_ref, tok_ref, hid_ref, nb_ref, nr_ref, gain_ref, table_ref, raw_ref, taps_ref, scorer_ref,
                  extra_ref, gt_ref, small_ref, oht, big, usum):
    i = pl.program_id(0)
    fill_onehot(cid_ref, oht)

    @pl.when(i == 0)
    def _():
        big[...] = jnp.zeros_like(big)
        usum[...] = jnp.zeros_like(usum)
        small_ref[...] = jnp.zeros_like(small_ref)
    x = tok_ref[...]
    n = nb_ref[...].astype(F32) + nr_ref[...].astype(F32)
    r = lax.rsqrt(jnp.mean(x * x, axis=1, keepdims=True) + EPS)
    u = n * gain_ref[...].astype(F32)
    xr = x * r
    g = hid_ref[...].astype(F32) + r * (u - xr * jnp.mean(u * xr, axis=1, keepdims=True))
    small_ref[6:7, :] += jnp.sum(n * xr, axis=0, keepdims=True)
    gb = g.astype(B16)
    hh = dot(gb, table_ref[...], NT).astype(B16)
    gram = dot(hh, oht[...], NN)
    even, odd, pair, tri_e, tri_o = masks()
    lanesum = lambda m: jnp.sum(jnp.where(m, gram, 0.0), axis=1, keepdims=True)
    me = 0.5 * lanesum(even)
    mo = 0.5 * lanesum(odd)
    m2 = 0.5 * (me + mo)
    m4 = 0.125 * lanesum(pair)
    m3e = lanesum(tri_e) * (1.0 / 6.0)
    m3o = lanesum(tri_o) * (1.0 / 6.0)
    lane8 = lax.broadcasted_iota(jnp.int32, (TT, 128), 1)
    cols = jnp.zeros((TT, 128), F32)
    for k, v in enumerate((me, mo, m2, m2, m3e, m3o, m4, m4)):
        cols = jnp.where(lane8 == k, v, cols)
    dmix = cols.T[0:8, :]
    mix = mix_ref[...]
    row = lambda a, k: a[k : k + 1, :]
    sides = []
    for side in range(2):
        inner = sum(row(mix, 2 * b + side) * row(dmix, 2 * b + side) for b in range(4))
        sides.append([row(mix, 2 * b + side) * (row(dmix, 2 * b + side) - inner) for b in range(4)])
    dwe = jnp.zeros((1, TT), F32)
    dwo = jnp.zeros((1, TT), F32)
    for b in range(4):
        e, o = means_of(sides[0][b], sides[1][b])[b]
        dwe = dwe + e
        dwo = dwo + o
    dw = jnp.concatenate([dwe, dwo], axis=1)
    hi, mid, lo = split3(jnp.broadcast_to(dw, (16, 2 * TT)))
    which = lax.broadcasted_iota(jnp.int32, (16, 2 * TT), 0)
    dw3 = jnp.where(which == 0, hi, jnp.where(which == 1, mid, jnp.where(which == 2, lo, jnp.zeros_like(hi))))
    usum[...] += dot(dw3, oht[...], NT)
    at = dot(oht[...], w_ref[...], NT).astype(B16)
    big[...] += dot(at, gb, NN)

    @pl.when(i == pl.num_programs(0) - 1)
    def _():
        us = usum[...]
        urow = us[0:1] + us[1:2] + us[2:3]
        hi, mid, lo = split3(jnp.broadcast_to(urow, (16, CC)))
        which = lax.broadcasted_iota(jnp.int32, (16, CC), 0)
        u3 = jnp.where(which == 0, hi, jnp.where(which == 1, mid, jnp.where(which == 2, lo, jnp.zeros_like(hi))))
        gs = dot(u3, table_ref[...], NN)
        small_ref[5:6, :] = gs[0:1] + gs[1:2] + gs[2:3]
        ucol = jnp.broadcast_to(urow, (128, CC)).T[:, 0:1]
        total = jnp.zeros((CJ, gt_ref.shape[1]), F32)
        for j in range(5):
            m = big[CJ * j : CJ * (j + 1), :] + ucol[CJ * j : CJ * (j + 1)] * scorer_ref[...].astype(F32)
            total = total + m * taps_ref[j : j + 1, :].astype(F32)
            small_ref[j : j + 1, :] = jnp.sum(m * raw_ref[...].astype(F32), axis=0, keepdims=True)
        gt_ref[0:CJ, :] = total
        gt_ref[CJ : CJ + 8, :] = small_ref[...]
        gt_ref[CJ + 8 :, :] = extra_ref[...]

def gbst_bwd(cid, w, mix, tok, hid, nb, nr, gain, table, raw, taps, scorer, extra):
    tiles = cid.shape[0]
    d = table.shape[1]
    rows = tiles * TT
    const = lambda shape: pl.BlockSpec(shape, lambda i: (0,) * len(shape))
    tile = lambda width: pl.BlockSpec((TT, width), lambda i: (i, 0))
    return pl.pallas_call(
        gbst_bwd_body, grid=(tiles,), name="gbst_bwd",
        in_specs=[pl.BlockSpec((None, 8, TT), lambda i: (i, 0, 0)), tile(2 * TT), pl.BlockSpec((None, 8, TT), lambda i: (i, 0, 0)),
                  tile(d), tile(d), tile(d), tile(d), const((1, d)), const((CC, d)), const((CJ, d)), const((5, d)), const((1, d)), const((8, d))],
        out_specs=const((CJ + 16, d)),
        out_shape=jax.ShapeDtypeStruct((CJ + 16, d), F32),
        scratch_shapes=[pltpu.VMEM((8, d), F32), pltpu.VMEM((CC, 2 * TT), B16), pltpu.VMEM((CC, d), F32), pltpu.VMEM((16, CC), F32)],
        compiler_params=pltpu.CompilerParams(vmem_limit_bytes=56 << 20),
        cost_estimate=pl.CostEstimate(flops=rows * CC * d * 8, transcendentals=0, bytes_accessed=rows * d * 12),
    )(cid, w, mix, tok, hid, nb, nr, gain, table, raw, taps, scorer, extra)


FC = 512
RT = 288


def middle_body(tok_ref, ao_ref, ar_ref, woo_ref, wor_ref, wgo_ref, wgr_ref, wuo_ref, wur_ref, wdo_ref, wdr_ref,
                og_ref, gain_ref,
                layer_ref, back_ref, down_ref, dsend_ref, goo_ref, gor_ref, ggo_ref, guo_ref, gdo_ref, ggr_ref, gur_ref, gdr_ref,
                gain_out,
                hid, n2, n2t, ogt, outs, n2b, wg, wu, wd, inner_s, gb_s, ub_s):
    i = pl.program_id(0)
    steps = pl.num_programs(0)
    rows = tok_ref.shape[0]
    tiles = [slice(r, r + RT) for r in range(0, rows, RT)]
    gain = gain_ref[...].astype(F32)

    @pl.when(i == 0)
    def _():
        for at in tiles:
            h = tok_ref[at, :] + dot(ao_ref[at, :], woo_ref[...], NN) + dot(ar_ref[at, :], wor_ref[...], NN)
            hid[at, :] = h
            r = lax.rsqrt(jnp.mean(h * h, axis=1, keepdims=True) + EPS)
            n2[at, :] = (h * r * gain).astype(B16)
            outs[at, :] = h
            n2b[at, :] = jnp.zeros((RT, h.shape[1]), F32)
        n2t[...] = n2[...].T
        ogt[...] = og_ref[...].T

    @pl.when(i < steps // 2)
    def _():
        wg[...] = wgo_ref[...]
        wu[...] = wuo_ref[...]
        wd[...] = wdo_ref[...]

    @pl.when(i >= steps // 2)
    def _():
        wg[...] = wgr_ref[...]
        wu[...] = wur_ref[...]
        wd[...] = wdr_ref[...]

    for at in tiles:
        x = n2[at, :]
        gate = dot(x, wg[...], NN)
        up = dot(x, wu[...], NN)
        gi = dot(og_ref[at, :], wd[...], NT)
        act, slope = gelu_parts(gate)
        inner = (act * up).astype(B16)
        gb = (gi * up * slope).astype(B16)
        ub = (gi * act).astype(B16)
        inner_s[at, :] = inner
        gb_s[at, :] = gb
        ub_s[at, :] = ub
        outs[at, :] += dot(inner, wd[...], NN)
        n2b[at, :] += dot(gb, wg[...], NT) + dot(ub, wu[...], NT)
    pieces = [dot(n2t[...], gb_s[...], NN), dot(n2t[...], ub_s[...], NN), dot(ogt[...], inner_s[...], NN)]
    pieces = [x.astype(B16) for x in pieces]

    @pl.when(i < steps // 2)
    def _():
        for ref, x in zip((ggo_ref, guo_ref, gdo_ref), pieces):
            ref[...] = x

    @pl.when(i >= steps // 2)
    def _():
        for ref, x in zip((ggr_ref, gur_ref, gdr_ref), pieces):
            ref[...] = x

    @pl.when(i == steps - 1)
    def _():
        total = jnp.zeros(gain.shape, F32)
        for at in tiles:
            h = hid[at, :]
            layer_ref[at, :] = outs[at, :].astype(B16)
            r = lax.rsqrt(jnp.mean(h * h, axis=1, keepdims=True) + EPS)
            back = n2b[at, :]
            u = back * gain
            hr = h * r
            total = total + jnp.sum(back * hr, axis=0, keepdims=True)
            hb = og_ref[at, :].astype(F32) + r * (u - hr * jnp.mean(u * hr, axis=1, keepdims=True))
            back_ref[at, :] = hb
            low = hb.astype(B16)
            n2[at, :] = low
            down_ref[at, :] = dot(low, woo_ref[...], NT).astype(B16)
            dsend_ref[at, :] = dot(low, wor_ref[...], NT).astype(B16)
        gain_out[...] = total
        n2t[...] = n2[...].T
        goo_ref[...] = dot(n2t[...], ao_ref[...], NN).astype(B16)
        gor_ref[...] = dot(n2t[...], ar_ref[...], NN).astype(B16)


def middle(tok, att_own, att_recv, wo, wo_other, wg, wg_other, wu, wu_other, wd, wd_other, og, gain):
    rows, d = tok.shape
    proj = att_own.shape[1]
    ffn = wg.shape[1]
    half = ffn // FC
    const = lambda *shape: pl.BlockSpec(shape, lambda i: (0,) * len(shape))
    once = lambda *shape: pl.BlockSpec(shape, lambda i: (0,) * len(shape), pipeline_mode=pl.Buffered(1))
    low = lambda i: jnp.minimum(i, half - 1)
    high = lambda i: jnp.maximum(i - half, 0)
    wide = lambda f: pl.BlockSpec((d, FC), lambda i: (0, f(i)))
    tall = lambda f: pl.BlockSpec((FC, d), lambda i: (f(i), 0))
    sds = jax.ShapeDtypeStruct
    flops = 2 * rows * d * (8 * 2 * ffn + 6 * proj) * 9 // 8
    return pl.pallas_call(
        middle_body, grid=(2 * half,), name="middle",
        in_specs=[once(rows, d), once(rows, proj), once(rows, proj), once(proj, d), once(proj, d),
                  wide(low), wide(high), wide(low), wide(high), tall(low), tall(high), once(rows, d), const(1, d)],
        out_specs=[once(rows, d), once(rows, d), once(rows, proj), once(rows, proj), once(d, proj), once(d, proj),
                   wide(low), wide(low), wide(low), wide(high), wide(high), wide(high), const(1, d)],
        out_shape=[sds((rows, d), B16), sds((rows, d), F32), sds((rows, proj), B16), sds((rows, proj), B16),
                   sds((d, proj), B16), sds((d, proj), B16)] + [sds((d, ffn), B16)] * 6 + [sds((1, d), F32)],
        scratch_shapes=[
            pltpu.VMEM((rows, d), F32), pltpu.VMEM((rows, d), B16), pltpu.VMEM((d, rows), B16), pltpu.VMEM((d, rows), B16),
            pltpu.VMEM((rows, d), F32), pltpu.VMEM((rows, d), F32),
            pltpu.VMEM((d, FC), B16), pltpu.VMEM((d, FC), B16), pltpu.VMEM((FC, d), B16),
            pltpu.VMEM((rows, FC), B16), pltpu.VMEM((rows, FC), B16), pltpu.VMEM((rows, FC), B16),
        ],
        compiler_params=pltpu.CompilerParams(vmem_limit_bytes=61 << 20, dimension_semantics=("arbitrary",)),
        cost_estimate=pl.CostEstimate(flops=flops, transcendentals=rows * 2 * ffn, bytes_accessed=rows * d * 20 + 24 * d * ffn),
    )(tok, att_own, att_recv, wo, wo_other, wg, wg_other, wu, wu_other, wd, wd_other, og, gain)


def post_body(core_ref, qa, qb, ka, kb, va, vb, w_ref, n_ref, own_ref, send_ref, g_ref, rows):
    i = pl.program_id(0)
    span = n_ref.shape[0]
    d = jnp.concatenate([qa[...], qb[...], ka[...], kb[...], va[...], vb[...]], axis=0)
    back = dot(w_ref[...], d, NN).astype(B16).T
    rows[pl.ds(pl.multiple_of(i * span, span), span), :] = back
    part = dot(n_ref[...].T, d, NT)

    @pl.when(i == 0)
    def _():
        g_ref[...] = part

    @pl.when(i > 0)
    def _():
        g_ref[...] += part

    @pl.when(i == pl.num_programs(0) - 1)
    def _():
        core = core_ref[0]
        half = own_ref.shape[1]
        for s in range(own_ref.shape[0]):
            own_ref[s] = rows[pl.ds(pl.multiple_of((2 * s + core) * half, 32), half), :]
            send_ref[s] = rows[pl.ds(pl.multiple_of((2 * s + 1 - core) * half, 32), half), :]


def post(core, pieces, w, normed, blocks):
    total, d = normed.shape
    span = CK * SUB
    half = total // blocks // 2
    lanes = lambda x: pl.BlockSpec((x.shape[0], span), lambda i, s: (0, i))
    const = lambda *shape: pl.BlockSpec(shape, lambda i, s: (0,) * len(shape))
    spec = pltpu.PrefetchScalarGridSpec(
        num_scalar_prefetch=1, grid=(total // span,),
        in_specs=[lanes(x) for x in pieces] + [const(*w.shape), pl.BlockSpec((span, d), lambda i, s: (i, 0))],
        out_specs=[const(blocks, half, d), const(blocks, half, d), const(*w.shape)],
        scratch_shapes=[pltpu.VMEM((total, d), B16)])
    return pl.pallas_call(
        post_body, grid_spec=spec, name="post",
        out_shape=[jax.ShapeDtypeStruct((blocks, half, d), B16), jax.ShapeDtypeStruct((blocks, half, d), B16),
                   jax.ShapeDtypeStruct(w.shape, F32)],
        compiler_params=pltpu.CompilerParams(vmem_limit_bytes=56 << 20, dimension_semantics=("arbitrary",)),
        cost_estimate=pl.CostEstimate(flops=4 * total * d * w.shape[1], transcendentals=0, bytes_accessed=30 * total * d // 4),
    )(core, *pieces, w, normed)


def unpack_body(x_ref, gate_ref, up_ref, down_ref, out_ref):
    f = gate_ref.shape[1]
    gate_ref[...] = x_ref[:, 0:f].astype(F32)
    up_ref[...] = x_ref[:, f : 2 * f].astype(F32)
    down_ref[...] = x_ref[:, 2 * f : 3 * f].astype(F32).T
    out_ref[...] = x_ref[:, 3 * f :].astype(F32).T


def unpack(x, f):
    d, columns = x.shape
    p = columns - 3 * f
    row = lambda width: pl.BlockSpec((128, width), lambda i: (i, 0))
    col = lambda width: pl.BlockSpec((width, 128), lambda i: (0, i))
    return pl.pallas_call(
        unpack_body, grid=(d // 128,), name="unpack",
        in_specs=[row(columns)], out_specs=[row(f), row(f), col(f), col(p)],
        out_shape=[jax.ShapeDtypeStruct((d, f), F32), jax.ShapeDtypeStruct((d, f), F32),
                   jax.ShapeDtypeStruct((f, d), F32), jax.ShapeDtypeStruct((p, d), F32)],
        compiler_params=pltpu.CompilerParams(vmem_limit_bytes=40 << 20, dimension_semantics=("arbitrary",)),
        cost_estimate=pl.CostEstimate(flops=0, transcendentals=0, bytes_accessed=6 * d * columns),
    )(x)


def swapped(tree):
    return jax.tree.map(lambda a: lax.ppermute(a, "mp", [(0, 1), (1, 0)]), tree)


def matmul(a, b):
    return dot(a, b, NN)


def grad_of(a, b):
    return lax.dot_general(a, b, (((0,), (0,)), ((), ())), preferred_element_type=F32)


X_SWAP = ("dp", 0)
Y_SWAP = ("dp", 1)
Z_NEAR = ("seq", 0)
Z_FAR = ("seq", 1)


def hop(x, axis, bit):
    count = lax.axis_size(axis)
    return lax.ppermute(x, axis, [(i, i ^ (1 << bit)) for i in range(count)])


def side_of(axis, bit):
    return (lax.axis_index(axis) >> bit) & 1


def give(x, axis, bit, behind=None):
    side = side_of(axis, bit)
    rows = x.shape[0] // 2
    keep = lax.dynamic_slice_in_dim(x, side * rows, rows, 0)
    send = lax.dynamic_slice_in_dim(x, (1 - side) * rows, rows, 0)
    recv = hop(send.astype(B16), axis, bit)
    if behind is not None:
        recv, keep = after(recv, behind), after(keep, behind)
    return keep.astype(F32) + recv.astype(F32)


def halves_of(x, axis, bit):
    side = side_of(axis, bit)
    rows = x.shape[0] // 2
    keep = lax.dynamic_slice_in_dim(x, side * rows, rows, 0)
    send = lax.dynamic_slice_in_dim(x, (1 - side) * rows, rows, 0)
    return keep, hop(send.astype(B16), axis, bit)


def take(x, axis, bit):
    first = side_of(axis, bit) == 0
    other = hop(x, axis, bit)
    return jnp.concatenate([jnp.where(first, x, other), jnp.where(first, other, x)], axis=0)


def two_ways(x, step, ways):
    cut = x.shape[1] // 2
    return [step(x[:, :cut], *ways[0]), step(x[:, cut:], *ways[1])]


def after(value, *others):
    return lax.optimization_barrier((value,) + others)[0]


def gelu_parts(gate):
    c = 0.7978845608028654
    inside = c * (gate + 0.044715 * gate * gate * gate)
    th = jnp.tanh(inside)
    value = 0.5 * gate * (1.0 + th)
    slope = 0.5 * (1.0 + th) + 0.5 * gate * (1.0 - th * th) * (c * (1.0 + 3.0 * 0.044715 * gate * gate))
    return value, slope


def local_item(
    byte_ids, true_lengths, byte_table, conv_taps, block_scorer, attn_gain, w_query, w_key, w_value,
    w_output, rel_table, ffn_gain, w_gate, w_up, w_down, out_grad,
):
    seq_count = lax.axis_size("seq")
    place = lax.axis_index("seq")
    core = lax.axis_index("mp")
    tok_rows = out_grad.shape[0]
    half = tok_rows // 2
    width = out_grad.shape[2]
    own_rows = seq_count * half
    total = 2 * own_rows
    proj = w_query.shape[1]
    first = core == 0

    def halves(full):
        parts = full.reshape(seq_count, 2, half, full.shape[1])
        own = jnp.where(first, parts[:, 0], parts[:, 1]).reshape(own_rows, -1)
        other = jnp.where(first, parts[:, 1], parts[:, 0]).reshape(own_rows, -1)
        return own, other

    def whole(own, other):
        shape = (seq_count, half, own.shape[1])
        low, high = jnp.where(first, own, other), jnp.where(first, other, own)
        return jnp.stack([low.reshape(shape), high.reshape(shape)], axis=1).reshape(total, -1)

    byte_rows = byte_ids.shape[0]
    here = place * byte_rows + jnp.arange(byte_rows, dtype=jnp.int32)
    shown = jnp.where(here[:, None] < true_lengths[None, :], byte_ids, -1)
    shown = shown.reshape(tok_rows, 2, seq_count).transpose(2, 1, 0)
    shown = lax.all_to_all(shown, "seq", split_axis=0, concat_axis=0, tiled=True)
    length = lax.dynamic_index_in_dim(true_lengths, place, 0, keepdims=False)
    wo_other, wg_other, wu_other, wd_other = swapped((w_output, w_gate, w_up, w_down))
    grad_rows = lax.dynamic_slice_in_dim(out_grad, core * half, half, 0)
    grad_own = lax.all_to_all(grad_rows, "seq", split_axis=1, concat_axis=0, tiled=True)
    grad_own = grad_own.reshape(own_rows, width)

    tiles = own_rows // TT
    pairs = jnp.pad(shown.transpose(1, 0, 2).reshape(2, total), ((0, 0), (1, 1)), constant_values=-1)
    rows = jnp.concatenate([pairs[:, j : j + total] for j in range(3)], axis=0).reshape(6, seq_count, 2, half)
    rows = jnp.where(first, rows[:, :, 0], rows[:, :, 1]).reshape(6, tiles, TT).transpose(1, 0, 2)
    cid = jnp.pad(rows, ((0, 0), (0, 2), (0, 0)), constant_values=-1)

    vocab = byte_table.shape[0]
    raw = jnp.pad(byte_table, ((0, CJ - vocab), (0, 0)))
    scorer, gain_one, gain_two = block_scorer[None], attn_gain[None], ffn_gain[None]
    tokens, normed, pool_w, mix, table_cat = gbst_fwd(cid, raw, conv_taps, scorer, gain_one)
    normed_all = whole(normed, swapped(normed))
    w_qkv = jnp.concatenate([w_query, w_key, w_value], axis=1)
    qkv = matmul(normed_all, w_qkv).astype(B16)
    limit = ((length + 1) // 2).reshape(1)
    weights, att, att_t, inv = attn_fwd(limit, qkv, bias_curve(rel_table, proj // DH))
    att_own, att_send = halves(att)
    att_recv = swapped(att_send)
    (layer, hidden_back, d_own, d_send, out_own, out_other, gate_own, up_own, down_own,
     gate_other, up_other, down_other, g_gain_two) = middle(
        tokens, att_own, att_recv, w_output, wo_other, w_gate, wg_other, w_up, wu_other, w_down, wd_other,
        grad_own, gain_two
    )
    d_att = whole(d_own, swapped(d_send))

    ffn_width = w_gate.shape[1]
    add = lambda a, b: (a.astype(F32) + b.astype(F32)).astype(B16)
    own_cols = (gate_own, up_own, down_own, out_own)
    other_cols = swapped((gate_other, up_other, down_other, out_other))
    large = jnp.concatenate([add(a, b) for a, b in zip(own_cols, other_cols)], axis=1)
    large = lax.psum_scatter(large, "dp", scatter_dimension=0, tiled=True)

    pairs = proj // 128
    early = pairs - 1
    dk_a, dv_a, dq_a, near_a, far_a = attn_bwd(weights, qkv, d_att, att_t, inv, 0, early)
    sent = layer.reshape(seq_count, half, width)
    layer_out = lax.all_to_all(sent[:, :, None], "seq", split_axis=0, concat_axis=2, tiled=True)
    late, dk_a, dv_a, dq_a, large, layer_out = lax.optimization_barrier((d_att, dk_a, dv_a, dq_a, large, layer_out))
    large = lax.psum_scatter(large, "seq", scatter_dimension=0, tiled=True)
    dk_b, dv_b, dq_b, near_b, far_b = attn_bwd(weights, qkv, late, att_t, inv, early, 1)
    near, far = jnp.concatenate([near_a, near_b]), jnp.concatenate([far_a, far_b])
    dk_b, large = lax.optimization_barrier((dk_b, large))
    pieces = (dq_a, dq_b, dk_a, dk_b, dv_a, dv_b)
    part_own, part_send, g_qkv = post(core.reshape(1).astype(jnp.int32), pieces, w_qkv, normed_all, seq_count)
    part_own = part_own.reshape(own_rows, width)
    part_recv = swapped(part_send).reshape(own_rows, width)
    large = lax.all_gather(large, "seq", axis=0, tiled=True)
    layer_out = layer_out.reshape(half, seq_count, width).astype(F32)
    (keep_left, left), (keep_right, right) = two_ways(g_qkv, halves_of, (X_SWAP, Y_SWAP))
    part_own, large, layer_out, left, right = lax.optimization_barrier((part_own, large, layer_out, left, right))
    large = lax.all_gather(large, "dp", axis=0, tiled=True)
    g_rel = rel_grad(near, far, near.shape[2])
    rel_row = jnp.pad(g_rel.reshape(1, -1), ((0, 0), (0, width - g_rel.size)))
    blank = jnp.zeros_like(rel_row)
    rel_rows = [jnp.where(first, rel_row, blank), jnp.where(first, blank, rel_row)]
    extra = jnp.concatenate([g_gain_two] + rel_rows + [jnp.zeros((5, width), F32)], axis=0)
    tail = gbst_bwd(
        cid, pool_w, mix, tokens, hidden_back, part_own, part_recv, gain_one, table_cat, raw, conv_taps, scorer, extra
    )
    left = after(keep_left, tail) + after(left, tail).astype(F32)
    right = after(keep_right, tail) + after(right, tail).astype(F32)
    tail = give(tail, "mp", 0)
    left = give(left, *Y_SWAP)
    right = give(right, *X_SWAP)
    tail = give(tail, *X_SWAP)
    both = give(jnp.concatenate([left, right], axis=1), *Z_NEAR)
    tail = give(tail, *Y_SWAP)
    both = give(both, *Z_FAR).astype(B16)
    tail = tail + hop(tail.astype(B16), *Z_NEAR).astype(F32)
    both = take(both, *Z_FAR)
    tail = (tail + hop(tail.astype(B16), *Z_FAR).astype(F32)).astype(B16)
    both = take(both, *Z_NEAR)
    both, large = lax.optimization_barrier((both, large))
    cut = both.shape[1] // 2
    left, right = take(both[:, :cut], *Y_SWAP), take(both[:, cut:], *X_SWAP)
    tail = take(tail, *Y_SWAP)
    left, right = take(left, *X_SWAP), take(right, *Y_SWAP)
    tail = take(tail, *X_SWAP)
    tail = take(tail, "mp", 0).astype(F32)
    g_gate, g_up, g_down, g_out = unpack(large, ffn_width)
    g_qkv = jnp.concatenate([left, right], axis=1)
    g_query, g_key, g_value = (g_qkv[:, i * proj : (i + 1) * proj].astype(F32) for i in range(3))
    g_table, small, g_gain_two = tail[:CJ], tail[CJ : CJ + 7], tail[CJ + 8]
    g_rel = jnp.where(first, tail[CJ + 9], tail[CJ + 10])[: g_rel.size].reshape(g_rel.shape)

    return (
        layer_out, g_table[:vocab], small[:5], small[5], small[6], g_query, g_key, g_value, g_out, g_rel,
        g_gain_two, g_gate, g_up, g_down,
    )


def chosen(*args):
    ids, lengths, w_query, out_grad = args[0], args[1], args[6], args[15]
    seq_count = lax.axis_size("seq")
    total = out_grad.shape[0] * seq_count
    fits = (
        lengths.shape[0] == seq_count
        and lax.axis_size("mp") == 2
        and lax.axis_size("dp") == 4
        and seq_count == 4
        and total % (2 * TT) == 0
        and total % CK == 0
        and total % (CK * SUB) == 0
        and w_query.shape[1] % 128 == 0
        and w_query.shape[1] >= 256
        and args[12].shape[1] % FC == 0
        and args[2].shape[1] % 128 == 0
        and (total // (2 * seq_count)) % 32 == 0
        and (total // 2) % RT == 0
        and (ids.shape[0] // 2) % 12 == 0
    )
    return local_item(*args) if fits else local_general(*args)


def solution(mesh):
    return jax.shard_map(
        chosen,
        mesh=mesh,
        in_specs=(
            P("seq", "dp"),
            P("dp"),
            P(),
            P(),
            P(),
            P(),
            P(None, "mp"),
            P(None, "mp"),
            P(None, "mp"),
            P("mp", None),
            P(None, "mp"),
            P(),
            P(None, "mp"),
            P(None, "mp"),
            P("mp", None),
            P("seq", "dp", None),
        ),
        out_specs=(
            P(("seq", "mp"), "dp", None),
            P(),
            P(),
            P(),
            P(),
            P(None, "mp"),
            P(None, "mp"),
            P(None, "mp"),
            P("mp", None),
            P(None, "mp"),
            P(),
            P(None, "mp"),
            P(None, "mp"),
            P("mp", None),
        ),
        check_vma=False,
    )
```
